32 devices in a mesh: chan: 4 (over x, core), rad: 8 (over z, y).
Axes of the slice: x: 2, y: 2, z: 4, core: 2. Of those that a mesh axis runs over, the one named last changes fastest.
Arguments:
- psi: float32 [2, 768, 128, 128], P(None, 'chan', 'rad'), may hold values from -6 to 6
- k_prev: float32 [2, 768, 128, 128], P(None, 'chan', 'rad'), may hold values from -6 to 6
- gaunt: bfloat16 [4, 768, 768], replicated, may hold values from -0.875 to 0.875
- dipole: bfloat16 [768, 768], replicated, may hold values from -0.875 to 0.875
- kinetic: float32 [128, 128], replicated, as said below
- chan_l: int32 [768, 2], P('chan'), may hold values from 0 to 23
- field_amp: float32 [1], replicated, may hold values from 0.02 to 0.1
Outputs:
- deriv: float32 [2, 768, 128, 128], P(None, 'chan', 'rad')
The draws below stay inside these ranges and needn't reach their ends.
Inputs may be any that keep to these rules, and one draw needn't show every extreme that they name: `kinetic`: symmetric; zero where the row's and the column's blocks of 16 indices are more than one block apart.
All inputs are finite; a program needn't handle non-finite values.
Results may differ from the reference program's by a relative error of at most 0.00037.
Values may be sent and summed in bfloat16 or wider, within the bound.
A program may use at most 64 MiB of HBM per device.

```python
import jax
import jax.numpy as jnp
from jax import lax

C = 768
R_DEV = 16
LAM = 4
NR = 128


def draw_kinetic(key, part):
    spread = 1.0 / (3.0 * R_DEV) ** 0.5
    raw = jax.random.normal(key, (NR, NR), jnp.float32) * spread
    blocks = jnp.arange(NR, dtype=jnp.int32) // R_DEV
    band = (jnp.abs(blocks[:, None] - blocks[None, :]) <= 1).astype(jnp.float32)
    return (raw + raw.T) * 0.5 * band + 2.0 * jnp.eye(NR, dtype=jnp.float32)


def touch_ends(drawn, stream_key, low, largest):
    place = [jax.random.randint(jax.random.fold_in(stream_key, axis), (), 0, length) for axis, length in enumerate(drawn.shape)]
    widest = drawn.shape.index(max(drawn.shape))
    next_to = place[:widest] + [(place[widest] + 1) % drawn.shape[widest]] + place[widest + 1:]
    return drawn.at[tuple(place)].set(low).at[tuple(next_to)].set(largest)


def levels(stream_key, extent, split, smallest, high):
    def one(position, blocks):
        draws = jax.random.uniform(jax.random.fold_in(jax.random.fold_in(stream_key, 6), position), (blocks,), jnp.float32, smallest / len(split), high / len(split))
        return jnp.repeat(jnp.exp(draws), extent[position] // blocks).reshape((-1,) + (1,) * (len(extent) - position - 1))

    gain = one(*split[0])
    for cut in split[1:]:
        gain = gain * one(*cut)
    return gain


def gaussian(own_key, shape, deviation, bound, shards=(), kind=jnp.bfloat16):
    array = jax.random.normal(own_key, shape, jnp.float32) * deviation
    if len(shards) > 0:
        array = levels(own_key, shape, shards, -0.22, 0.18) * array
    return jnp.clip(array, min=-bound, max=bound).astype(kind)


def setup_inputs(seed: int = 0) -> dict:
    splits = jax.random.split(jax.random.key(seed), 8)
    return {
        "psi": gaussian(splits[0], (2, C, NR, NR), 1.0, 6.0, ((1, 4), (2, 8)), jnp.float32),
        "k_prev": gaussian(splits[1], (2, C, NR, NR), 1.0, 6.0, ((1, 4), (2, 8)), jnp.float32),
        "gaunt": gaussian(splits[2], (LAM, C, C), (C // 16) ** -0.5, 0.875),
        "dipole": gaussian(splits[3], (C, C), (C // 16) ** -0.5, 0.875),
        "kinetic": draw_kinetic(jax.random.fold_in(splits[7], 71), 0),
        "chan_l": touch_ends(jax.random.randint(splits[5], (C, 2), 0, 24), jax.random.fold_in(splits[5], 1), 0, 23).astype(jnp.int32),
        "field_amp": jnp.clip(jax.random.uniform(splits[6], (1,), jnp.float32, 0.02, 0.1), 0.02, 0.1),
    }


def radial_grid(count):
    return 1.0 + 8.0 * jnp.arange(count, dtype=jnp.float32) / count


def reference(psi, k_prev, gaunt, dipole, kinetic, chan_l, field_amp):
    highest = lax.Precision.HIGHEST
    section = psi + 0.5 * k_prev
    sent = section.astype(jnp.bfloat16)
    radius = radial_grid(NR)
    along_r1 = jnp.einsum('ij,acjk->acik', kinetic, section, precision=highest)
    along_r2 = jnp.einsum('acij,kj->acik', section, kinetic, precision=highest)
    lvals = chan_l.astype(jnp.float32)
    first_l = lvals[:, 0] * (lvals[:, 0] + 1.0)
    second_l = lvals[:, 1] * (lvals[:, 1] + 1.0)
    potential = (first_l[:, None, None] / (2.0 * radius * radius)[None, :, None]
                 + second_l[:, None, None] / (2.0 * radius * radius)[None, None, :]
                 - 2.0 / radius[None, :, None] - 2.0 / radius[None, None, :])
    first_r = jnp.broadcast_to(radius[:, None], (NR, NR)).reshape(-1)
    second_r = jnp.broadcast_to(radius[None, :], (NR, NR)).reshape(-1)
    far = jnp.maximum(first_r, second_r)
    near = jnp.minimum(first_r, second_r)
    inverse = 1.0 / far
    ratio = near * inverse
    flat = sent.reshape(2, C, NR * NR).astype(jnp.float32)
    power = inverse
    total = jnp.zeros((2, C, NR * NR), jnp.float32)
    for order in range(LAM):
        mixed = jnp.einsum('cd,adq->acq', gaunt[order].astype(jnp.float32), flat, precision=highest)
        total = total + power[None, None, :] * mixed
        power = power * ratio
    mixed = jnp.einsum('cd,adq->acq', dipole.astype(jnp.float32), flat, precision=highest)
    total = total + (field_amp[0] * (first_r + second_r))[None, None, :] * mixed
    coupled = total.astype(jnp.bfloat16).reshape(2, C, NR, NR)
    ham = along_r1 + along_r2 + potential[None] * section + coupled.astype(jnp.float32)
    return jnp.stack([ham[1], -ham[0]])
```

```python
import functools

import jax
import jax.numpy as jnp
from jax import lax
from jax.experimental import pallas as pl
from jax.experimental.pallas import tpu as pltpu
from jax.sharding import PartitionSpec as P


def extended(array, sides, width):
    for axis, dim in sides:
        peers, length = (lax.axis_size(axis), array.shape[dim])
        up = [(i, (i + 1) % peers) for i in range(peers - 1)]
        down = [(j, i) for i, j in up]
        last = lax.slice_in_dim(array, length - width, length, axis=dim)
        initial = lax.slice_in_dim(array, 0, width, axis=dim)
        before = lax.ppermute(last, axis, up)
        after = lax.ppermute(initial, axis, down)
        array = jnp.concatenate([before, array, after], axis=dim)
    return array


def on_device(psi, k_prev, gaunt, dipole, kinetic, chan_l, field_amp):
    highest = lax.Precision.HIGHEST
    section = psi + 0.5 * k_prev
    local_chan = section.shape[1]
    rows = section.shape[2]
    width = section.shape[3]
    rad_at = lax.axis_index("rad")
    first_r = (
        1.0 + 8.0 * (rad_at * rows + jnp.arange(rows, dtype=jnp.int32)).astype(jnp.float32) / width
    )
    second_r = 1.0 + 8.0 * jnp.arange(width, dtype=jnp.float32) / width
    along_r2 = jnp.einsum("acij,kj->acik", section, kinetic, precision=highest)
    padded = extended(section.astype(jnp.bfloat16), (("rad", 2),), rows).astype(section.dtype)
    band = lax.dynamic_slice_in_dim(kinetic, rad_at * rows, rows, 0)
    widened = jnp.pad(band, ((0, 0), (rows, rows)))
    local_band = lax.dynamic_slice_in_dim(widened, rad_at * rows, 3 * rows, 1)
    along_r1 = jnp.einsum("ij,acjk->acik", local_band, padded, precision=highest)
    lvals = chan_l.astype(jnp.float32)
    first_l = lvals[:, 0] * (lvals[:, 0] + 1.0)
    second_l = lvals[:, 1] * (lvals[:, 1] + 1.0)
    potential = (
        first_l[:, None, None] / (2.0 * first_r * first_r)[None, :, None]
        + second_l[:, None, None] / (2.0 * second_r * second_r)[None, None, :]
        - 2.0 / first_r[None, :, None]
        - 2.0 / second_r[None, None, :]
    )
    sent = section.astype(jnp.bfloat16).reshape(2, local_chan, rows * width)
    chan_at = lax.axis_index("chan")
    block = lax.all_to_all(sent, "chan", split_axis=2, concat_axis=1, tiled=True)
    count = block.shape[2]
    place = chan_at * count + jnp.arange(count, dtype=jnp.int32)
    row_r = 1.0 + 8.0 * (rad_at * rows + place // width).astype(jnp.float32) / width
    col_r = 1.0 + 8.0 * (place % width).astype(jnp.float32) / width
    far = jnp.maximum(row_r, col_r)
    near = jnp.minimum(row_r, col_r)
    inverse = 1.0 / far
    ratio = near * inverse
    power = inverse
    total = jnp.zeros(block.shape, jnp.float32)
    for order in range(gaunt.shape[0]):
        mixed = jnp.einsum("cd,adq->acq", gaunt[order], block, preferred_element_type=jnp.float32)
        total = total + power[None, None, :] * mixed
        power = power * ratio
    mixed = jnp.einsum("cd,adq->acq", dipole, block, preferred_element_type=jnp.float32)
    total = total + (field_amp[0] * (row_r + col_r))[None, None, :] * mixed
    coupled = lax.all_to_all(
        total.astype(jnp.bfloat16), "chan", split_axis=1, concat_axis=2, tiled=True
    )
    coupled = coupled.reshape(coupled.shape[0], local_chan, rows, width)
    ham = along_r1 + along_r2 + potential[None] * section + coupled.astype(jnp.float32)
    return jnp.stack([ham[1], -ham[0]])


MESH = pl.DeviceIdType.MESH
GROUP = 16
LOADS = ((0, 1), (1, 2), (2, 4), (4, 8), (8, 12))


def split_bf16(value):
    high = value.astype(jnp.bfloat16)
    return high, (value - high.astype(jnp.float32)).astype(jnp.bfloat16)


def fused_kernel(
    peers,
    rads,
    psi,
    k_prev,
    gaunt,
    dipole,
    kin_main,
    chan_main,
    field,
    out,
    kin,
    chan_l,
    pbuf,
    kbuf,
    sec,
    xg,
    halo,
    acc,
    acc1,
    weights,
    wr1,
    kk,
    lmul,
    langle,
    load_sem,
    small_sem,
    hs,
    hr,
    xs,
    xr,
    cs,
    cr,
    fs,
    fl,
    fr,
    ys,
    yr,
    zs,
    zr,
):
    rows, chans, lanes = sec.shape
    width = lanes // 2
    orders = weights.shape[0]
    chips = peers // 2
    groups = chans // GROUP
    lead = rows // 4
    chan_at = lax.axis_index("chan")
    rad_at = lax.axis_index("rad")
    core = chan_at % 2
    chip = chan_at // 2
    partner = chan_at + 1 - 2 * core
    minor = rad_at % 2
    other = rad_at + 1 - 2 * minor
    ahead = rad_at + 2 - 4 * minor
    behind = rad_at - 2 + 4 * minor
    has_ahead = jnp.logical_and(ahead >= 0, ahead < rads)
    has_behind = jnp.logical_and(behind >= 0, behind < rads)
    near_slot = 1 - minor
    far_slot = minor

    def block(owner):
        return pl.ds(pl.multiple_of(owner * chans, GROUP), chans)

    def cut_of(group):
        return pl.ds(pl.multiple_of(group * GROUP, GROUP), GROUP)

    def block_cut(owner, group):
        return pl.ds(pl.multiple_of(owner * chans + group * GROUP, GROUP), GROUP)

    def chip_peer(step):
        return lax.rem(chip + step, chips) * 2 + core

    def chip_source(step):
        return lax.rem(chip - step + chips, chips) * 2 + core

    def load(which, part):
        source, target = ((psi, pbuf), (k_prev, kbuf))[which]
        first, last = LOADS[part]
        cut = slice(first * GROUP, last * GROUP)
        return pltpu.make_async_copy(
            source.at[:, cut, :, :], target.at[:, cut, :, :], load_sem.at[which, part]
        )

    def load_weight(order):
        source = gaunt.at[order] if order < orders - 1 else dipole
        return pltpu.make_async_copy(
            source.at[block(chan_at), :], weights.at[order], small_sem.at[2]
        )

    def remote(source, target, send, recv, device):
        return pltpu.make_async_remote_copy(
            src_ref=source,
            dst_ref=target,
            send_sem=send,
            recv_sem=recv,
            device_id=device,
            device_id_type=MESH,
        )

    def lead_copy(step, some, owner):
        view = xg.at[0:lead, some, :]
        device = {"chan": chip_peer(step)}
        return remote(view, view, hs.at[step - 1], hr.at[step - 1], device)

    def chip_copy(step, some_rows, owner, place):
        view = xg.at[some_rows, block(owner), :]
        device = {"chan": chip_peer(step)}
        return remote(view, view, xs.at[step - 1], xr.at[step - 1, place], device)

    def core_copy(some_rows, owner):
        view = xg.at[some_rows, block(owner), :]
        return remote(view, view, cs, cr, {"chan": partner})

    def relay_lead(step, owner):
        view = xg.at[0:lead, block(owner), :]
        return remote(view, view, fs.at[step - 1], fl.at[step - 1], {"chan": partner})

    def relay_copy(step, some_rows, owner, place):
        view = xg.at[some_rows, block(owner), :]
        return remote(view, view, fs.at[step - 1], fr.at[step - 1, place], {"chan": partner})

    def half_of(half):
        return slice(half * (rows // 2), (half + 1) * (rows // 2))

    def side_copy(group, half):
        source = xg.at[half_of(half), block_cut(chan_at, group), :]
        target = halo.at[minor, half_of(half), cut_of(group), :]
        return remote(source, target, ys, yr.at[half, group], {"rad": other})

    def far_copy(some_rows, some, place):
        source = halo.at[near_slot, some_rows, some, :]
        target = halo.at[minor, some_rows, some, :]
        return remote(source, target, zs, zr.at[place], {"rad": ahead})

    every = slice(0, rows)
    small = [
        pltpu.make_async_copy(kin_main, kin, small_sem.at[0]),
        pltpu.make_async_copy(chan_main, chan_l, small_sem.at[1]),
    ]
    for part in range(len(LOADS)):
        for which in range(2):
            load(which, part).start()

    barrier = pltpu.get_barrier_semaphore()
    for step in range(1, chips):
        pl.semaphore_signal(
            barrier, inc=1, device_id={"chan": chip_peer(step)}, device_id_type=MESH
        )
    pl.semaphore_signal(barrier, inc=1, device_id={"chan": partner}, device_id_type=MESH)
    pl.semaphore_signal(barrier, inc=1, device_id={"rad": other}, device_id_type=MESH)

    @pl.when(has_ahead)
    def _():
        pl.semaphore_signal(barrier, inc=1, device_id={"rad": ahead}, device_id_type=MESH)

    @pl.when(has_behind)
    def _():
        pl.semaphore_signal(barrier, inc=1, device_id={"rad": behind}, device_id_type=MESH)

    def form(group):
        for part in range(2):
            first = pbuf.at[part].reshape(chans * rows, width)
            second = kbuf.at[part].reshape(chans * rows, width)
            cut = slice(part * width, (part + 1) * width)
            for row in range(rows):
                place = (pl.ds(group * GROUP * rows + row, GROUP, stride=rows), slice(None))
                value = first[place] + 0.5 * second[place]
                sec[row, cut_of(group), cut] = value
                xg[row, block_cut(chan_at, group), cut] = value.astype(jnp.bfloat16)

    def send_group(group):
        for half in range(2):
            side_copy(group, half).start()
        for step in range(1, chips):
            lead_copy(step, block_cut(chan_at, group), chan_at).start()

    def arrive(part):
        for which in range(2):
            load(which, part).wait()

    arrive(0)
    form(jnp.int32(0))
    pl.semaphore_wait(
        barrier, chips + 1 + has_ahead.astype(jnp.int32) + has_behind.astype(jnp.int32)
    )
    send_group(0)
    arrive(1)
    form(jnp.int32(1))

    def form_next(group, carry):
        form(group)
        send_group(group - 1)
        return carry

    for part in range(2, len(LOADS)):
        arrive(part)
        lax.fori_loop(LOADS[part][0], LOADS[part][1], form_next, 0)
    for copy in small:
        copy.start()
    for order in range(orders):
        load_weight(order).start()

    send_group(groups - 1)
    for row in range(lead, rows):
        for step in range(1, chips):
            chip_copy(step, row, chan_at, row - lead).start()
    for index in range(4):
        core_copy(slice(index * lead, (index + 1) * lead), chan_at).start()

    def forward(group, half):
        side_copy(group, half).wait_recv()

        @pl.when(has_ahead)
        def _():
            far_copy(half_of(half), cut_of(group), group).start()

    forward(0, 0)
    for copy in small:
        copy.wait()
    kin_high, kin_low = split_bf16(kin[...])
    both = jnp.concatenate([kin_high, kin_low], axis=1)
    kk[0:width, :] = both
    kk[width : 2 * width, :] = both

    band = kin[pl.ds(pl.multiple_of(rad_at * rows, rows), rows), :]
    size = rows * GROUP
    tall = jnp.broadcast_to(band[:, None, :], (rows, GROUP, width)).reshape(size, width)
    tall_high, tall_low = split_bf16(tall)
    at_row = lax.broadcasted_iota(jnp.int32, (size, size), 0)
    at_col = lax.broadcasted_iota(jnp.int32, (size, size), 1)
    same = (at_row % GROUP) == (at_col % GROUP)
    from_j = lax.broadcasted_iota(jnp.int32, (width, size), 0)
    to_col = lax.broadcasted_iota(jnp.int32, (width, size), 1)
    for side in range(3):
        pick = from_j == (rad_at + side - 1) * rows + to_col // GROUP
        pick = jnp.where(pick, 1.0, 0.0).astype(jnp.bfloat16)
        for level, source in enumerate((tall_high, tall_low)):
            wide = jnp.dot(source, pick, preferred_element_type=jnp.float32)
            wr1[side, level * size : (level + 1) * size, :] = jnp.where(same, wide, 0.0).astype(
                jnp.bfloat16
            )

    @pl.when(jnp.logical_not(has_behind))
    def _():
        halo[far_slot] = jnp.zeros(halo.shape[1:], halo.dtype)

    second_r = 1.0 + 8.0 * (
        lax.broadcasted_iota(jnp.int32, (1, lanes), 1) % width
    ).astype(jnp.float32) / width
    inner_r = second_r[:, :width]
    lvals = chan_l[...].astype(jnp.float32).astype(jnp.bfloat16)
    first = lax.broadcasted_iota(jnp.int32, (2, lanes), 0)
    spread = first == lax.broadcasted_iota(jnp.int32, (2, lanes), 1) // width
    spread = jnp.where(spread, 1.0, 0.0).astype(jnp.bfloat16)
    lwide = lax.dot_general(
        lvals, spread, (((0,), (0,)), ((), ())), preferred_element_type=jnp.float32
    )
    lwide = lwide * (lwide + 1.0)
    lmul[...] = lwide[:, :width]
    langle[...] = lwide[:, width:] / (2.0 * inner_r * inner_r) - 2.0 / inner_r

    def radius(row):
        place = jnp.full((1, lanes), rad_at * rows + row, jnp.int32)
        return 1.0 + 8.0 * place.astype(jnp.float32) / width

    def local_row(row):
        first_r = radius(row)[:, :width]
        scale = 1.0 / (2.0 * first_r * first_r)
        shift = 2.0 / first_r
        potential = lmul[...] * scale + langle[...] - shift
        for part in range(2):
            cut = slice(part * width, (part + 1) * width)
            value = sec[row, :, cut]
            high = xg[row, block(chan_at), cut]
            low = (value - high.astype(jnp.float32)).astype(jnp.bfloat16)
            both = jnp.dot(
                jnp.concatenate([high, low], axis=1), kk[...], preferred_element_type=jnp.float32
            )
            acc[row, :, cut] = both[:, :width] + both[:, width:] + potential * value

    def mix(side, value):
        both = jnp.dot(wr1[side], value, preferred_element_type=jnp.float32)
        return both[:size] + both[size:]

    def own_group(index):
        first = pl.multiple_of(index * GROUP, GROUP)
        start = pl.multiple_of(chan_at * chans + first, GROUP)
        high = xg[:, pl.ds(start, GROUP), :].reshape(size, lanes)
        value = sec[:, pl.ds(first, GROUP), :].reshape(size, lanes)
        low = (value - high.astype(jnp.float32)).astype(jnp.bfloat16)
        total = mix(1, high) + jnp.dot(
            wr1[1, 0:size, :], low, preferred_element_type=jnp.float32
        )
        acc1[:, pl.ds(first, GROUP), :] = total.reshape(rows, GROUP, lanes)

    def side_group(index):
        first = pl.multiple_of(index * GROUP, GROUP)
        cut = pl.ds(first, GROUP)
        total = mix(0, halo[0, :, cut, :].reshape(size, lanes)) + mix(
            2, halo[1, :, cut, :].reshape(size, lanes)
        )
        acc1[:, cut, :] = acc1[:, cut, :] + total.reshape(rows, GROUP, lanes)

    def couple(row):
        first_r = radius(row)
        inverse = 1.0 / jnp.maximum(first_r, second_r)
        ratio = jnp.minimum(first_r, second_r) * inverse
        factors = [inverse]
        for _ in range(orders - 2):
            factors.append(factors[-1] * ratio)
        factors.append(field[0] * (first_r + second_r))
        step = chans // 2
        for first in range(0, chans, step):
            total = jnp.zeros((step, lanes), jnp.float32)
            for order in range(orders):
                total = total + factors[order] * jnp.dot(
                    weights[order, first : first + step, :],
                    xg[row],
                    preferred_element_type=jnp.float32,
                )
            acc[row, first : first + step, :] = acc[row, first : first + step, :] + total.astype(
                jnp.bfloat16
            ).astype(jnp.float32)

    def relay(row):
        for step in range(1, chips):
            chip_copy(step, row, chip_source(step), row - lead).wait_recv()
            relay_copy(step, row, chip_source(step), row - lead).start()

    def take_row(row):
        for step in range(1, chips):
            owner = chip_source(step) + 1 - 2 * core
            relay_copy(step, row, owner, row - lead).wait_recv()
        couple(row)

    def take_side(group):
        @pl.when(has_behind)
        def _():
            far_copy(every, cut_of(group), group).wait_recv()

        side_group(group)

    forward(0, 1)
    for index in range(2):
        own_group(index)
    for index in range(3):
        local_row(index)

    def phase(index, carry):
        for half in range(2):
            forward(index + 1, half)
            for place in range(2):
                own_group(index * 4 + half * 2 + place + 2)
            for place in range(3 - half):
                local_row(index * 5 + half * 3 + place + 3)
        return carry

    lax.fori_loop(0, 2, phase, 0)
    for step in range(1, chips):
        lead_copy(step, block(chip_source(step)), chip_source(step)).wait_recv()
        relay_lead(step, chip_source(step)).start()
    pltpu.make_async_copy(weights, weights, small_sem.at[2]).wait()
    core_copy(every, partner).wait_recv()
    for index in range(2):
        own_group(index + 10)

    def main(index, carry):
        start = index * lead

        def when_first(work, *args):
            @pl.when(index == 1)
            def _():
                work(*args)

        def lead_or_row(row):
            @pl.when(index == 1)
            def _():
                couple(row)

            @pl.when(index > 1)
            def _():
                take_row(row)

        forward(3 * index, 0)

        @pl.when(index == 1)
        def _():
            for row in range(13, rows):
                local_row(row)
            for step in range(1, chips):
                relay_lead(step, chip_source(step) + 1 - 2 * core).wait_recv()

        lead_or_row(start - 2)
        forward(3 * index, 1)
        relay(start)
        take_side(3 * index - 2)
        lead_or_row(start - 1)
        forward(3 * index + 1, 0)
        relay(start + 1)
        take_side(3 * index - 1)
        when_first(take_side, 0)
        when_first(couple, 0)
        forward(3 * index + 1, 1)
        take_row(start)
        forward(3 * index + 2, 0)
        relay(start + 2)
        take_row(start + 1)
        forward(3 * index + 2, 1)
        relay(start + 3)
        take_side(3 * index)
        when_first(couple, 1)
        return carry

    lax.fori_loop(1, 4, main, 0)

    def merge(group, some_rows):
        cut = cut_of(group)
        first = out.at[0].reshape(chans * rows, width)
        second = out.at[1].reshape(chans * rows, width)
        for row in some_rows:
            value = acc[row, cut, :] + acc1[row, cut, :]
            place = (pl.ds(group * GROUP * rows + row, GROUP, stride=rows), slice(None))
            first[place] = value[:, width:]
            second[place] = -value[:, :width]

    def merge_most(group, carry):
        merge(group, range(rows - 1))
        return carry

    def merge_last(group, carry):
        merge(group, range(rows - 1, rows))
        return carry

    take_row(rows - 2)
    lax.fori_loop(0, groups - 2, merge_most, 0)
    take_side(groups - 2)
    merge(groups - 2, range(rows - 1))
    take_row(rows - 1)
    lax.fori_loop(0, groups - 1, merge_last, 0)
    take_side(groups - 1)
    merge(groups - 1, range(rows))

    core_copy(every, chan_at).wait_send()
    for step in range(1, chips):
        lead_copy(step, block(chan_at), chan_at).wait_send()
        chip_copy(step, slice(lead, rows), chan_at, 0).wait_send()
        relay_copy(step, every, chip_source(step), 0).wait_send()
    remote(xg.at[:, block(chan_at), :], halo.at[minor], ys, yr.at[0, 0], {"rad": other}).wait_send()

    @pl.when(has_ahead)
    def _():
        far_copy(every, slice(0, chans), 0).wait_send()


def device_step(peers, rads, psi, k_prev, gaunt, dipole, kinetic, chan_l, field_amp):
    _, chans, rows, width = psi.shape
    fits = (
        chans == 3 * 4 * GROUP
        and rows == GROUP
        and peers % 2 == 0
        and rads % 2 == 0
        and width == rads * rows
        and width == 128
    )
    if not fits:
        return on_device(psi, k_prev, gaunt, dipole, kinetic, chan_l, field_amp)
    orders = gaunt.shape[0] + 1
    chips = peers // 2
    groups = chans // GROUP
    lanes = 2 * width
    size = rows * GROUP
    f32, bf16, dma = (jnp.float32, jnp.bfloat16, pltpu.SemaphoreType.DMA)
    main_memory = pl.BlockSpec(memory_space=pltpu.HBM)
    vmem = pl.BlockSpec(memory_space=pltpu.VMEM)
    psi, k_prev, gaunt, dipole, kinetic, chan_l = (
        pltpu.with_memory_space_constraint(value, pltpu.HBM)
        for value in (psi, k_prev, gaunt, dipole, kinetic, chan_l.T)
    )
    return pl.pallas_call(
        functools.partial(fused_kernel, peers, rads),
        out_shape=jax.ShapeDtypeStruct(psi.shape, f32),
        in_specs=[main_memory] * 6 + [pl.BlockSpec(memory_space=pltpu.SMEM)],
        out_specs=vmem,
        scratch_shapes=[
            pltpu.VMEM(kinetic.shape, f32),
            pltpu.VMEM((2, chans), jnp.int32),
            pltpu.VMEM((2, chans, rows, width), f32),
            pltpu.VMEM((2, chans, rows, width), f32),
            pltpu.VMEM((rows, chans, lanes), f32),
            pltpu.VMEM((rows, peers * chans, lanes), bf16),
            pltpu.VMEM((2, rows, chans, lanes), bf16),
            pltpu.VMEM((rows, chans, lanes), f32),
            pltpu.VMEM((rows, chans, lanes), f32),
            pltpu.VMEM((orders, chans, peers * chans), bf16),
            pltpu.VMEM((3, 2 * size, size), bf16),
            pltpu.VMEM((lanes, lanes), bf16),
            pltpu.VMEM((chans, width), f32),
            pltpu.VMEM((chans, width), f32),
            dma((2, len(LOADS))),
            dma((3,)),
            dma((chips - 1,)),
            dma((chips - 1,)),
            dma((chips - 1,)),
            dma((chips - 1, rows - rows // 4)),
            dma,
            dma,
            dma((chips - 1,)),
            dma((chips - 1,)),
            dma((chips - 1, rows - rows // 4)),
            dma,
            dma((2, groups)),
            dma,
            dma((groups,)),
        ],
        compiler_params=pltpu.CompilerParams(
            collective_id=0, has_side_effects=True, vmem_limit_bytes=36 * 1024 * 1024
        ),
    )(psi, k_prev, gaunt, dipole, kinetic, chan_l, field_amp)


def solution(mesh):
    placed = (
        P(None, "chan", "rad", None),
        P(None, "chan", "rad", None),
        P(),
        P(),
        P(),
        P("chan", None),
        P(),
    )
    return jax.shard_map(
        functools.partial(device_step, mesh.shape["chan"], mesh.shape["rad"]),
        mesh=mesh,
        in_specs=placed,
        out_specs=P(None, "chan", "rad", None),
        check_vma=False,
    )
```

```python
import functools

import jax
import jax.numpy as jnp
from jax import lax
from jax.experimental import pallas as pl
from jax.experimental.pallas import tpu as pltpu
from jax.sharding import PartitionSpec as P


def extended(array, sides, width):
    for axis, dim in sides:
        peers, length = (lax.axis_size(axis), array.shape[dim])
        up = [(i, (i + 1) % peers) for i in range(peers - 1)]
        down = [(j, i) for i, j in up]
        last = lax.slice_in_dim(array, length - width, length, axis=dim)
        initial = lax.slice_in_dim(array, 0, width, axis=dim)
        before = lax.ppermute(last, axis, up)
        after = lax.ppermute(initial, axis, down)
        array = jnp.concatenate([before, array, after], axis=dim)
    return array


def on_device(psi, k_prev, gaunt, dipole, kinetic, chan_l, field_amp):
    highest = lax.Precision.HIGHEST
    section = psi + 0.5 * k_prev
    local_chan = section.shape[1]
    rows = section.shape[2]
    width = section.shape[3]
    rad_at = lax.axis_index("rad")
    first_r = (
        1.0 + 8.0 * (rad_at * rows + jnp.arange(rows, dtype=jnp.int32)).astype(jnp.float32) / width
    )
    second_r = 1.0 + 8.0 * jnp.arange(width, dtype=jnp.float32) / width
    along_r2 = jnp.einsum("acij,kj->acik", section, kinetic, precision=highest)
    padded = extended(section.astype(jnp.bfloat16), (("rad", 2),), rows).astype(section.dtype)
    band = lax.dynamic_slice_in_dim(kinetic, rad_at * rows, rows, 0)
    widened = jnp.pad(band, ((0, 0), (rows, rows)))
    local_band = lax.dynamic_slice_in_dim(widened, rad_at * rows, 3 * rows, 1)
    along_r1 = jnp.einsum("ij,acjk->acik", local_band, padded, precision=highest)
    lvals = chan_l.astype(jnp.float32)
    first_l = lvals[:, 0] * (lvals[:, 0] + 1.0)
    second_l = lvals[:, 1] * (lvals[:, 1] + 1.0)
    potential = (
        first_l[:, None, None] / (2.0 * first_r * first_r)[None, :, None]
        + second_l[:, None, None] / (2.0 * second_r * second_r)[None, None, :]
        - 2.0 / first_r[None, :, None]
        - 2.0 / second_r[None, None, :]
    )
    sent = section.astype(jnp.bfloat16).reshape(2, local_chan, rows * width)
    chan_at = lax.axis_index("chan")
    block = lax.all_to_all(sent, "chan", split_axis=2, concat_axis=1, tiled=True)
    count = block.shape[2]
    place = chan_at * count + jnp.arange(count, dtype=jnp.int32)
    row_r = 1.0 + 8.0 * (rad_at * rows + place // width).astype(jnp.float32) / width
    col_r = 1.0 + 8.0 * (place % width).astype(jnp.float32) / width
    far = jnp.maximum(row_r, col_r)
    near = jnp.minimum(row_r, col_r)
    inverse = 1.0 / far
    ratio = near * inverse
    power = inverse
    total = jnp.zeros(block.shape, jnp.float32)
    for order in range(gaunt.shape[0]):
        mixed = jnp.einsum("cd,adq->acq", gaunt[order], block, preferred_element_type=jnp.float32)
        total = total + power[None, None, :] * mixed
        power = power * ratio
    mixed = jnp.einsum("cd,adq->acq", dipole, block, preferred_element_type=jnp.float32)
    total = total + (field_amp[0] * (row_r + col_r))[None, None, :] * mixed
    coupled = lax.all_to_all(
        total.astype(jnp.bfloat16), "chan", split_axis=1, concat_axis=2, tiled=True
    )
    coupled = coupled.reshape(coupled.shape[0], local_chan, rows, width)
    ham = along_r1 + along_r2 + potential[None] * section + coupled.astype(jnp.float32)
    return jnp.stack([ham[1], -ham[0]])


MESH = pl.DeviceIdType.MESH
GROUP = 16
LOADS = ((0, 1), (1, 2), (2, 4), (4, 8), (8, 12))


def split_bf16(value):
    high = value.astype(jnp.bfloat16)
    return high, (value - high.astype(jnp.float32)).astype(jnp.bfloat16)


def fused_kernel(
    peers,
    rads,
    psi,
    k_prev,
    gaunt,
    dipole,
    kin_main,
    chan_main,
    field,
    out,
    kin,
    chan_l,
    pk,
    sec,
    xg,
    xp,
    coupled,
    back,
    halo,
    acc,
    acc1,
    weights,
    peer_weights,
    wr1,
    kk,
    lmul,
    langle,
    load_sem,
    small_sem,
    hs,
    hr,
    xs,
    xr,
    cs,
    cr,
    fs,
    fl,
    fr,
    ys,
    yr,
    zs,
    zr,
    vs,
    vr,
    via,
):
    rows, chans, lanes = sec.shape
    width = lanes // 2
    orders = weights.shape[0]
    chips = peers // 2
    groups = chans // GROUP
    lead = rows // 4
    chan_at = lax.axis_index("chan")
    rad_at = lax.axis_index("rad")
    core = chan_at % 2
    chip = chan_at // 2
    partner = chan_at + 1 - 2 * core
    minor = rad_at % 2
    other = rad_at + 1 - 2 * minor
    ahead = rad_at + 2 - 4 * minor
    behind = rad_at - 2 + 4 * minor
    has_ahead = jnp.logical_and(ahead >= 0, ahead < rads)
    has_behind = jnp.logical_and(behind >= 0, behind < rads)
    near_slot = 1 - minor
    far_slot = minor
    whole = rows - 2
    peer = lax.rem(chip + 1, chips) * 2 + core

    def block(owner):
        return pl.ds(pl.multiple_of(owner * chans, GROUP), chans)

    def cut_of(group):
        return pl.ds(pl.multiple_of(group * GROUP, GROUP), GROUP)

    def block_cut(owner, group):
        return pl.ds(pl.multiple_of(owner * chans + group * GROUP, GROUP), GROUP)

    def chip_peer(step):
        return lax.rem(chip + step, chips) * 2 + core

    def chip_source(step):
        return lax.rem(chip - step + chips, chips) * 2 + core

    def load(which, part):
        first, last = LOADS[part]
        cut = slice(first * GROUP, last * GROUP)
        return pltpu.make_async_copy(
            (psi, k_prev)[which].at[:, cut, :, :], pk.at[which, :, cut, :, :], load_sem.at[part]
        )

    def arrive(part):
        first, last = LOADS[part]
        view = pk.at[:, :, first * GROUP : last * GROUP, :, :]
        pltpu.make_async_copy(view, view, load_sem.at[part]).wait()

    def load_weight(order):
        source = gaunt.at[order] if order < orders - 1 else dipole
        return pltpu.make_async_copy(
            source.at[block(chan_at), :], weights.at[order], small_sem.at[2]
        )

    def load_peer_weight(order):
        source = gaunt.at[order] if order < orders - 1 else dipole
        return pltpu.make_async_copy(
            source.at[block(peer), :], peer_weights.at[order], small_sem.at[3]
        )

    def remote(source, target, send, recv, device):
        return pltpu.make_async_remote_copy(
            src_ref=source,
            dst_ref=target,
            send_sem=send,
            recv_sem=recv,
            device_id=device,
            device_id_type=MESH,
        )

    def lead_copy(some):
        view = xg.at[0:lead, some, :]
        return remote(view, view, hs, hr, {"chan": peer})

    def chip_copy(row, owner):
        view = xg.at[row, block(owner), :]
        return remote(view, view, xs, xr.at[row - lead], {"chan": peer})

    def part_copy(part, owner):
        view = xp.at[part, block(owner), :]
        return remote(view, view, xs, xr.at[whole - lead], {"chan": peer})

    def back_copy(part):
        return remote(back, coupled.at[part], xs, xr.at[whole - lead + 1], {"chan": peer})

    def core_copy(some_rows, owner):
        view = xg.at[some_rows, block(owner), :]
        return remote(view, view, cs, cr.at[0], {"chan": partner})

    def core_part(owner):
        view = xp.at[chip, block(owner), :]
        return remote(view, view, cs, cr.at[1], {"chan": partner})

    def relay_lead(owner):
        view = xg.at[0:lead, block(owner), :]
        return remote(view, view, fs, fl, {"chan": partner})

    def relay_copy(row, owner):
        view = xg.at[row, block(owner), :]
        return remote(view, view, fs, fr.at[row - lead], {"chan": partner})

    def relay_part(owner):
        view = xp.at[chip, block(owner), :]
        return remote(view, view, fs, fr.at[whole - lead], {"chan": partner})

    def sent(count, sem, device):
        view = xg.at[0:count, block(chan_at), :]
        remote(view, view, sem, fl, device).wait_send()

    def half_of(half):
        return slice(half * (rows // 2), (half + 1) * (rows // 2))

    def side_copy(group, half):
        source = xg.at[half_of(half), block_cut(chan_at, group), :]
        target = halo.at[minor, half_of(half), cut_of(group), :]
        return remote(source, target, ys, yr.at[half, group], {"rad": other})

    def far_copy(some_rows, some, place):
        source = halo.at[near_slot, some_rows, some, :]
        target = halo.at[minor, some_rows, some, :]
        return remote(source, target, zs, zr.at[place], {"rad": ahead})

    def via_copy():
        source = xg.at[half_of(1), block_cut(chan_at, groups - 1), :]
        return remote(source, via, vs.at[0], vr.at[0], {"rad": behind})

    def via_forward():
        target = halo.at[near_slot, half_of(1), cut_of(groups - 1), :]
        return remote(via, target, vs.at[1], vr.at[1], {"rad": other})

    every = slice(0, rows)
    small = [
        pltpu.make_async_copy(kin_main, kin, small_sem.at[0]),
        pltpu.make_async_copy(chan_main, chan_l, small_sem.at[1]),
    ]
    for part in range(len(LOADS)):
        for which in range(2):
            load(which, part).start()

    barrier = pltpu.get_barrier_semaphore()
    for step in range(1, chips):
        pl.semaphore_signal(
            barrier, inc=1, device_id={"chan": chip_peer(step)}, device_id_type=MESH
        )
    pl.semaphore_signal(barrier, inc=1, device_id={"chan": partner}, device_id_type=MESH)
    pl.semaphore_signal(barrier, inc=1, device_id={"rad": other}, device_id_type=MESH)

    @pl.when(has_ahead)
    def _():
        pl.semaphore_signal(barrier, inc=1, device_id={"rad": ahead}, device_id_type=MESH)

    @pl.when(has_behind)
    def _():
        pl.semaphore_signal(barrier, inc=1, device_id={"rad": behind}, device_id_type=MESH)

    def form(group):
        for part in range(2):
            first = pk.at[0, part].reshape(chans * rows, width)
            second = pk.at[1, part].reshape(chans * rows, width)
            cut = slice(part * width, (part + 1) * width)
            for row in range(rows):
                place = (pl.ds(group * GROUP * rows + row, GROUP, stride=rows), slice(None))
                value = first[place] + 0.5 * second[place]
                sec[row, cut_of(group), cut] = value
                rounded = value.astype(jnp.bfloat16)
                xg[row, block_cut(chan_at, group), cut] = rounded
                if row >= whole:
                    lane = slice((row - whole) * width, (row - whole + 1) * width)
                    xp[part, block_cut(chan_at, group), lane] = rounded

    def send_group(group):
        for half in range(2):
            side_copy(group, half).start()
        lead_copy(block_cut(chan_at, group)).start()

    arrive(0)
    form(jnp.int32(0))
    pl.semaphore_wait(
        barrier, chips + 1 + has_ahead.astype(jnp.int32) + has_behind.astype(jnp.int32)
    )
    send_group(0)
    arrive(1)
    form(jnp.int32(1))

    def form_next(group, carry):
        form(group)
        send_group(group - 1)
        return carry

    for part in range(2, len(LOADS)):
        arrive(part)
        lax.fori_loop(LOADS[part][0], LOADS[part][1], form_next, 0)
    for copy in small:
        copy.start()
    for order in range(orders):
        load_weight(order).start()
        load_peer_weight(order).start()

    send_group(groups - 1)

    @pl.when(has_behind)
    def _():
        via_copy().start()

    part_copy(1 - chip, chan_at).start()
    for row in range(lead, whole):
        chip_copy(row, chan_at).start()
    for index in range(0, whole, lead):
        core_copy(slice(index, min(index + lead, whole)), chan_at).start()
    core_part(chan_at).start()

    def forward(group, half):
        side_copy(group, half).wait_recv()

        @pl.when(has_ahead)
        def _():
            far_copy(half_of(half), cut_of(group), group).start()

    @pl.when(core == 1)
    def _():
        forward(0, 0)

    for copy in small:
        copy.wait()
    kin_high, kin_low = split_bf16(kin[...])
    both = jnp.concatenate([kin_high, kin_low], axis=1)
    kk[0:width, :] = both
    kk[width : 2 * width, :] = both

    band = kin[pl.ds(pl.multiple_of(rad_at * rows, rows), rows), :]
    size = rows * GROUP
    tall = jnp.broadcast_to(band[:, None, :], (rows, GROUP, width)).reshape(size, width)
    tall_high, tall_low = split_bf16(tall)
    at_row = lax.broadcasted_iota(jnp.int32, (size, size), 0)
    at_col = lax.broadcasted_iota(jnp.int32, (size, size), 1)
    same = (at_row % GROUP) == (at_col % GROUP)
    from_j = lax.broadcasted_iota(jnp.int32, (width, size), 0)
    to_col = lax.broadcasted_iota(jnp.int32, (width, size), 1)
    for side in range(3):
        pick = from_j == (rad_at + side - 1) * rows + to_col // GROUP
        pick = jnp.where(pick, 1.0, 0.0).astype(jnp.bfloat16)
        for level, source in enumerate((tall_high, tall_low)):
            wide = jnp.dot(source, pick, preferred_element_type=jnp.float32)
            wr1[side, level * size : (level + 1) * size, :] = jnp.where(same, wide, 0.0).astype(
                jnp.bfloat16
            )

    @pl.when(jnp.logical_not(has_behind))
    def _():
        halo[far_slot] = jnp.zeros(halo.shape[1:], halo.dtype)

    second_r = 1.0 + 8.0 * (
        lax.broadcasted_iota(jnp.int32, (1, lanes), 1) % width
    ).astype(jnp.float32) / width
    inner_r = second_r[:, :width]
    lvals = chan_l[...].astype(jnp.float32).astype(jnp.bfloat16)
    first = lax.broadcasted_iota(jnp.int32, (2, lanes), 0)
    spread = first == lax.broadcasted_iota(jnp.int32, (2, lanes), 1) // width
    spread = jnp.where(spread, 1.0, 0.0).astype(jnp.bfloat16)
    lwide = lax.dot_general(
        lvals, spread, (((0,), (0,)), ((), ())), preferred_element_type=jnp.float32
    )
    lwide = lwide * (lwide + 1.0)
    lmul[...] = lwide[:, :width]
    langle[...] = lwide[:, width:] / (2.0 * inner_r * inner_r) - 2.0 / inner_r

    def radius(row):
        place = jnp.full((1, lanes), rad_at * rows + row, jnp.int32)
        return 1.0 + 8.0 * place.astype(jnp.float32) / width

    def local_row(row):
        first_r = radius(row)[:, :width]
        scale = 1.0 / (2.0 * first_r * first_r)
        shift = 2.0 / first_r
        potential = lmul[...] * scale + langle[...] - shift
        for part in range(2):
            cut = slice(part * width, (part + 1) * width)
            value = sec[row, :, cut]
            high = xg[row, block(chan_at), cut]
            low = (value - high.astype(jnp.float32)).astype(jnp.bfloat16)
            both = jnp.dot(
                jnp.concatenate([high, low], axis=1), kk[...], preferred_element_type=jnp.float32
            )
            acc[row, :, cut] = both[:, :width] + both[:, width:] + potential * value

    def mix(side, value):
        both = jnp.dot(wr1[side], value, preferred_element_type=jnp.float32)
        return both[:size] + both[size:]

    def own_group(index):
        first = pl.multiple_of(index * GROUP, GROUP)
        start = pl.multiple_of(chan_at * chans + first, GROUP)
        high = xg[:, pl.ds(start, GROUP), :].reshape(size, lanes)
        value = sec[:, pl.ds(first, GROUP), :].reshape(size, lanes)
        low = (value - high.astype(jnp.float32)).astype(jnp.bfloat16)
        total = mix(1, high) + jnp.dot(
            wr1[1, 0:size, :], low, preferred_element_type=jnp.float32
        )
        acc1[:, pl.ds(first, GROUP), :] = total.reshape(rows, GROUP, lanes)

    def side_group(index):
        first = pl.multiple_of(index * GROUP, GROUP)
        cut = pl.ds(first, GROUP)
        total = mix(0, halo[0, :, cut, :].reshape(size, lanes)) + mix(
            2, halo[1, :, cut, :].reshape(size, lanes)
        )
        acc1[:, cut, :] = acc1[:, cut, :] + total.reshape(rows, GROUP, lanes)

    def factors_of(first_r):
        inverse = 1.0 / jnp.maximum(first_r, second_r)
        ratio = jnp.minimum(first_r, second_r) * inverse
        factors = [inverse]
        for _ in range(orders - 2):
            factors.append(factors[-1] * ratio)
        factors.append(field[0] * (first_r + second_r))
        return factors

    def summed(factors, matrices, source, some):
        total = jnp.zeros((chans // 2, lanes), jnp.float32)
        for order in range(orders):
            total = total + factors[order] * jnp.dot(
                matrices[order, some, :], source[...], preferred_element_type=jnp.float32
            )
        return total.astype(jnp.bfloat16)

    cuts = (slice(0, chans // 2), slice(chans // 2, chans))

    def couple(row):
        factors = factors_of(radius(row))
        for some in cuts:
            total = summed(factors, weights, xg.at[row], some)
            acc[row, some, :] = acc[row, some, :] + total.astype(jnp.float32)

    def couple_parts(matrices, target):
        place = lax.broadcasted_iota(jnp.int32, (1, lanes), 1) // width
        place = place + (rad_at * rows + whole)
        factors = factors_of(1.0 + 8.0 * place.astype(jnp.float32) / width)
        for some in cuts:
            target[some, :] = summed(factors, matrices, xp.at[chip], some)

    def couple_peer():
        couple_parts(peer_weights, back)

    def couple_own():
        back_copy(chip).start()
        couple_parts(weights, coupled.at[chip])

    def relay(row):
        chip_copy(row, peer).wait_recv()
        relay_copy(row, peer).start()

    def take_row(row):
        relay_copy(row, peer + 1 - 2 * core).wait_recv()
        couple(row)

    def take_side(group):
        @pl.when(has_behind)
        def _():
            far_copy(every, cut_of(group), group).wait_recv()

        side_group(group)

    def mix_slot(slot, cut):
        value = halo[slot, :, cut, :].reshape(size, lanes)
        total = mix(2 * slot, value).reshape(rows, GROUP, lanes)
        acc1[:, cut, :] = acc1[:, cut, :] + total

    @pl.when(core == 0)
    def _():
        forward(0, 0)

    for index in range(2):
        own_group(index)
    for index in range(2):
        local_row(index)
    forward(0, 1)
    local_row(2)

    def phase(index, carry):
        for half in range(2):
            forward(index + 1, half)
            for place in range(2):
                own_group(index * 4 + half * 2 + place + 2)
            for place in range(3 - half):
                local_row(index * 5 + half * 3 + place + 3)
        return carry

    def merge(group, some_rows):
        cut = cut_of(group)
        targets = [out.at[1 - part].reshape(chans * rows, width) for part in range(2)]
        for row in some_rows:
            value = acc[row, cut, :] + acc1[row, cut, :]
            place = (pl.ds(group * GROUP * rows + row, GROUP, stride=rows), slice(None))
            for part in range(2):
                piece = value[:, part * width : (part + 1) * width]
                if row >= whole:
                    lane = slice((row - whole) * width, (row - whole + 1) * width)
                    piece = piece + coupled[part, cut, lane].astype(jnp.float32)
                targets[part][place] = piece if part == 1 else -piece

    def merge_groups(first, last, some_rows):
        def step(group, carry):
            merge(group, some_rows)
            return carry

        lax.fori_loop(first, last, step, 0)

    lax.fori_loop(0, 2, phase, 0)
    lead_copy(block(peer)).wait_recv()
    relay_lead(peer).start()
    pltpu.make_async_copy(weights, weights, small_sem.at[2]).wait()
    pltpu.make_async_copy(peer_weights, peer_weights, small_sem.at[3]).wait()
    core_copy(slice(0, whole), partner).wait_recv()
    core_part(partner).wait_recv()
    for index in range(2):
        own_group(index + 10)

    @pl.when(has_ahead)
    def _():
        via_copy().wait_recv()
        via_forward().start()

    def main(index, carry):
        start = index * lead

        def at(turn, work, *args):
            @pl.when(index == turn)
            def _():
                work(*args)

        forward(3 * index, 0)

        @pl.when(index == 1)
        def _():
            for row in range(13, rows):
                local_row(row)
            part_copy(chip, peer).wait_recv()
            relay_part(peer).start()
            relay_lead(peer + 1 - 2 * core).wait_recv()
            couple(0)

        @pl.when(index > 1)
        def _():
            take_row(start - 2)
            relay(start - 1)

        forward(3 * index, 1)
        take_side(3 * index - 3)
        at(1, couple, 1)

        @pl.when(index == 2)
        def _():
            relay_part(peer + 1 - 2 * core).wait_recv()
            couple_peer()

        forward(3 * index + 1, 0)
        relay(start)
        take_side(3 * index - 2)
        at(1, couple, 2)

        @pl.when(index > 1)
        def _():
            take_row(start - 1)

        forward(3 * index + 1, 1)
        take_row(start)
        relay(start + 1)
        forward(3 * index + 2, 0)
        take_side(3 * index - 1)
        at(1, couple, 3)
        at(2, couple_own)
        at(3, merge_groups, 0, groups - 3, range(whole - 1))

        @pl.when(index < 3)
        def _():
            forward(3 * index + 2, 1)
            relay(start + 2)
            take_row(start + 1)

        return carry

    lax.fori_loop(1, 4, main, 0)

    take_side(groups - 3)
    take_row(whole - 1)
    merge_groups(0, groups - 3, range(whole - 1, whole))
    merge(groups - 3, range(whole))
    back_copy(1 - chip).wait_recv()
    merge_groups(0, groups - 2, range(whole, rows))
    take_side(groups - 2)
    merge(groups - 2, range(rows))
    side_copy(groups - 1, 1).wait_recv()
    mix_slot(near_slot, cut_of(groups - 1))

    @pl.when(has_behind)
    def _():
        far_copy(half_of(0), cut_of(groups - 1), groups - 1).wait_recv()
        via_forward().wait_recv()

    mix_slot(far_slot, cut_of(groups - 1))
    merge(groups - 1, range(rows))

    core_copy(slice(0, whole), chan_at).wait_send()
    core_part(chan_at).wait_send()
    sent(lead, hs, {"chan": peer})
    sent(rows - lead, xs, {"chan": peer})
    sent(rows - 1, fs, {"chan": partner})
    sent(rows, ys, {"rad": other})

    @pl.when(has_ahead)
    def _():
        view = xg.at[0 : rows // 2, 0 : (2 * groups - 1) * GROUP, :]
        remote(view, view, zs, zr.at[0], {"rad": ahead}).wait_send()
        via_forward().wait_send()

    @pl.when(has_behind)
    def _():
        via_copy().wait_send()


def device_step(peers, rads, psi, k_prev, gaunt, dipole, kinetic, chan_l, field_amp):
    _, chans, rows, width = psi.shape
    fits = (
        chans == 3 * 4 * GROUP
        and rows == GROUP
        and peers == 4
        and rads % 2 == 0
        and width == rads * rows
        and width == 128
    )
    if not fits:
        return on_device(psi, k_prev, gaunt, dipole, kinetic, chan_l, field_amp)
    orders = gaunt.shape[0] + 1
    chips = peers // 2
    groups = chans // GROUP
    lanes = 2 * width
    size = rows * GROUP
    f32, bf16, dma = (jnp.float32, jnp.bfloat16, pltpu.SemaphoreType.DMA)
    main_memory = pl.BlockSpec(memory_space=pltpu.HBM)
    vmem = pl.BlockSpec(memory_space=pltpu.VMEM)
    psi, k_prev, gaunt, dipole, kinetic, chan_l = (
        pltpu.with_memory_space_constraint(value, pltpu.HBM)
        for value in (psi, k_prev, gaunt, dipole, kinetic, chan_l.T)
    )
    return pl.pallas_call(
        functools.partial(fused_kernel, peers, rads),
        out_shape=jax.ShapeDtypeStruct(psi.shape, f32),
        in_specs=[main_memory] * 6 + [pl.BlockSpec(memory_space=pltpu.SMEM)],
        out_specs=vmem,
        scratch_shapes=[
            pltpu.VMEM(kinetic.shape, f32),
            pltpu.VMEM((2, chans), jnp.int32),
            pltpu.VMEM((2, 2, chans, rows, width), f32),
            pltpu.VMEM((rows, chans, lanes), f32),
            pltpu.VMEM((rows, peers * chans, lanes), bf16),
            pltpu.VMEM((2, peers * chans, lanes), bf16),
            pltpu.VMEM((2, chans, lanes), bf16),
            pltpu.VMEM((chans, lanes), bf16),
            pltpu.VMEM((2, rows, chans, lanes), bf16),
            pltpu.VMEM((rows, chans, lanes), f32),
            pltpu.VMEM((rows, chans, lanes), f32),
            pltpu.VMEM((orders, chans, peers * chans), bf16),
            pltpu.VMEM((orders, chans, peers * chans), bf16),
            pltpu.VMEM((3, 2 * size, size), bf16),
            pltpu.VMEM((lanes, lanes), bf16),
            pltpu.VMEM((chans, width), f32),
            pltpu.VMEM((chans, width), f32),
            dma((len(LOADS),)),
            dma((4,)),
            dma,
            dma,
            dma,
            dma((rows - rows // 4,)),
            dma,
            dma((2,)),
            dma,
            dma,
            dma((rows - rows // 4 - 1,)),
            dma,
            dma((2, groups)),
            dma,
            dma((groups,)),
            dma((2,)),
            dma((2,)),
            pltpu.VMEM((rows // 2, GROUP, lanes), bf16),
        ],
        compiler_params=pltpu.CompilerParams(
            collective_id=0, has_side_effects=True, vmem_limit_bytes=36 * 1024 * 1024
        ),
    )(psi, k_prev, gaunt, dipole, kinetic, chan_l, field_amp)


def solution(mesh):
    placed = (
        P(None, "chan", "rad", None),
        P(None, "chan", "rad", None),
        P(),
        P(),
        P(),
        P("chan", None),
        P(),
    )
    return jax.shard_map(
        functools.partial(device_step, mesh.shape["chan"], mesh.shape["rad"]),
        mesh=mesh,
        in_specs=placed,
        out_specs=P(None, "chan", "rad", None),
        check_vma=False,
    )
```

```python
import functools

import jax
import jax.numpy as jnp
from jax import lax
from jax.experimental import pallas as pl
from jax.experimental.pallas import tpu as pltpu
from jax.sharding import PartitionSpec as P


def extended(array, sides, width):
    for axis, dim in sides:
        peers, length = (lax.axis_size(axis), array.shape[dim])
        up = [(i, (i + 1) % peers) for i in range(peers - 1)]
        down = [(j, i) for i, j in up]
        last = lax.slice_in_dim(array, length - width, length, axis=dim)
        initial = lax.slice_in_dim(array, 0, width, axis=dim)
        before = lax.ppermute(last, axis, up)
        after = lax.ppermute(initial, axis, down)
        array = jnp.concatenate([before, array, after], axis=dim)
    return array


def on_device(psi, k_prev, gaunt, dipole, kinetic, chan_l, field_amp):
    highest = lax.Precision.HIGHEST
    section = psi + 0.5 * k_prev
    local_chan = section.shape[1]
    rows = section.shape[2]
    width = section.shape[3]
    rad_at = lax.axis_index("rad")
    first_r = (
        1.0 + 8.0 * (rad_at * rows + jnp.arange(rows, dtype=jnp.int32)).astype(jnp.float32) / width
    )
    second_r = 1.0 + 8.0 * jnp.arange(width, dtype=jnp.float32) / width
    along_r2 = jnp.einsum("acij,kj->acik", section, kinetic, precision=highest)
    padded = extended(section.astype(jnp.bfloat16), (("rad", 2),), rows).astype(section.dtype)
    band = lax.dynamic_slice_in_dim(kinetic, rad_at * rows, rows, 0)
    widened = jnp.pad(band, ((0, 0), (rows, rows)))
    local_band = lax.dynamic_slice_in_dim(widened, rad_at * rows, 3 * rows, 1)
    along_r1 = jnp.einsum("ij,acjk->acik", local_band, padded, precision=highest)
    lvals = chan_l.astype(jnp.float32)
    first_l = lvals[:, 0] * (lvals[:, 0] + 1.0)
    second_l = lvals[:, 1] * (lvals[:, 1] + 1.0)
    potential = (
        first_l[:, None, None] / (2.0 * first_r * first_r)[None, :, None]
        + second_l[:, None, None] / (2.0 * second_r * second_r)[None, None, :]
        - 2.0 / first_r[None, :, None]
        - 2.0 / second_r[None, None, :]
    )
    sent = section.astype(jnp.bfloat16).reshape(2, local_chan, rows * width)
    chan_at = lax.axis_index("chan")
    block = lax.all_to_all(sent, "chan", split_axis=2, concat_axis=1, tiled=True)
    count = block.shape[2]
    place = chan_at * count + jnp.arange(count, dtype=jnp.int32)
    row_r = 1.0 + 8.0 * (rad_at * rows + place // width).astype(jnp.float32) / width
    col_r = 1.0 + 8.0 * (place % width).astype(jnp.float32) / width
    far = jnp.maximum(row_r, col_r)
    near = jnp.minimum(row_r, col_r)
    inverse = 1.0 / far
    ratio = near * inverse
    power = inverse
    total = jnp.zeros(block.shape, jnp.float32)
    for order in range(gaunt.shape[0]):
        mixed = jnp.einsum("cd,adq->acq", gaunt[order], block, preferred_element_type=jnp.float32)
        total = total + power[None, None, :] * mixed
        power = power * ratio
    mixed = jnp.einsum("cd,adq->acq", dipole, block, preferred_element_type=jnp.float32)
    total = total + (field_amp[0] * (row_r + col_r))[None, None, :] * mixed
    coupled = lax.all_to_all(
        total.astype(jnp.bfloat16), "chan", split_axis=1, concat_axis=2, tiled=True
    )
    coupled = coupled.reshape(coupled.shape[0], local_chan, rows, width)
    ham = along_r1 + along_r2 + potential[None] * section + coupled.astype(jnp.float32)
    return jnp.stack([ham[1], -ham[0]])


MESH = pl.DeviceIdType.MESH
GROUP = 16
LOADS = ((0, 1), (1, 4), (4, 12))


def split_bf16(value):
    high = value.astype(jnp.bfloat16)
    return high, (value - high.astype(jnp.float32)).astype(jnp.bfloat16)


def merge(acc, target, group, some_rows):
    width = acc.shape[2] // 2
    chans, height = target.shape[1:3]
    cut = pl.ds(pl.multiple_of(group * GROUP, GROUP), GROUP)
    views = [target.at[part].reshape(chans * height, width) for part in range(2)]
    for row in some_rows:
        value = acc[row, cut, :]
        place = (pl.ds(group * GROUP * height + row, GROUP, stride=height), slice(None))
        views[0][place] = value[:, width:]
        views[1][place] = -value[:, :width]


def finish_kernel(acc, top, out, whole, sem):
    rows, chans, _ = acc.shape
    upper = rows // 2
    done = chans - 2 * GROUP

    def store(source, cut, some_rows):
        return pltpu.make_async_copy(source, out.at[:, cut, some_rows, :], sem)

    store(top.at[:, 0:done], slice(0, done), slice(0, upper)).start()
    for first in range(0, done, 2 * GROUP):
        for group in range(first // GROUP, first // GROUP + 2):
            merge(acc, whole, group, range(upper, rows))
        cut, low = (slice(first, first + 2 * GROUP), slice(upper, rows))
        store(whole.at[:, cut, low, :], cut, low).start()
    for group in range(done // GROUP, chans // GROUP):
        merge(acc, whole, group, range(rows))
    cut = slice(done, chans)
    store(whole.at[:, cut], cut, slice(0, rows)).start()
    pltpu.make_async_copy(whole, out, sem).wait()


def fused_kernel(
    peers,
    rads,
    psi,
    k_prev,
    gaunt,
    dipole,
    kin_main,
    chan_main,
    field,
    acc,
    top,
    kin,
    chan_l,
    pk,
    sec,
    xg,
    xp,
    coupled,
    back,
    halo,
    weights,
    peer_weights,
    wr1,
    kk,
    lmul,
    langle,
    load_sem,
    small_sem,
    hs,
    hr,
    xs,
    xr,
    cs,
    cr,
    fs,
    fl,
    fr,
    ys,
    yr,
    zs,
    zr,
    vs,
    vr,
    via,
):
    rows, chans, lanes = sec.shape
    width = lanes // 2
    orders = weights.shape[0]
    chips = peers // 2
    groups = chans // GROUP
    lead = rows // 4
    chan_at = lax.axis_index("chan")
    rad_at = lax.axis_index("rad")
    core = chan_at % 2
    chip = chan_at // 2
    partner = chan_at + 1 - 2 * core
    minor = rad_at % 2
    other = rad_at + 1 - 2 * minor
    ahead = rad_at + 2 - 4 * minor
    behind = rad_at - 2 + 4 * minor
    has_ahead = jnp.logical_and(ahead >= 0, ahead < rads)
    has_behind = jnp.logical_and(behind >= 0, behind < rads)
    near_slot = 1 - minor
    far_slot = minor
    whole = rows - 2
    peer = lax.rem(chip + 1, chips) * 2 + core

    def block(owner):
        return pl.ds(pl.multiple_of(owner * chans, GROUP), chans)

    def cut_of(group):
        return pl.ds(pl.multiple_of(group * GROUP, GROUP), GROUP)

    def block_cut(owner, group):
        return pl.ds(pl.multiple_of(owner * chans + group * GROUP, GROUP), GROUP)

    def chip_peer(step):
        return lax.rem(chip + step, chips) * 2 + core

    def chip_source(step):
        return lax.rem(chip - step + chips, chips) * 2 + core

    def load(which, part):
        first, last = LOADS[part]
        cut = slice(first * GROUP, last * GROUP)
        return pltpu.make_async_copy(
            (psi, k_prev)[which].at[:, cut, :, :], pk.at[which, :, cut, :, :], load_sem.at[part]
        )

    def arrive(part):
        first, last = LOADS[part]
        view = pk.at[:, :, first * GROUP : last * GROUP, :, :]
        pltpu.make_async_copy(view, view, load_sem.at[part]).wait()

    def load_weight(order):
        source = gaunt.at[order] if order < orders - 1 else dipole
        return pltpu.make_async_copy(
            source.at[block(chan_at), :], weights.at[order], small_sem.at[2]
        )

    def load_peer_weight(order):
        source = gaunt.at[order] if order < orders - 1 else dipole
        return pltpu.make_async_copy(
            source.at[block(peer), :], peer_weights.at[order], small_sem.at[3]
        )

    def remote(source, target, send, recv, device):
        return pltpu.make_async_remote_copy(
            src_ref=source,
            dst_ref=target,
            send_sem=send,
            recv_sem=recv,
            device_id=device,
            device_id_type=MESH,
        )

    def lead_copy(some):
        view = xg.at[0:lead, some, :]
        return remote(view, view, hs, hr, {"chan": peer})

    def chip_copy(row, owner):
        view = xg.at[row, block(owner), :]
        return remote(view, view, xs, xr.at[row - lead], {"chan": peer})

    def part_copy(part, owner):
        view = xp.at[part, block(owner), :]
        return remote(view, view, xs, xr.at[whole - lead], {"chan": peer})

    def back_copy(part):
        return remote(back, coupled.at[part], xs, xr.at[whole - lead + 1], {"chan": peer})

    def core_copy(some_rows, owner):
        view = xg.at[some_rows, block(owner), :]
        return remote(view, view, cs, cr.at[0], {"chan": partner})

    def core_part(owner):
        view = xp.at[chip, block(owner), :]
        return remote(view, view, cs, cr.at[1], {"chan": partner})

    def relay_lead(owner):
        view = xg.at[0:lead, block(owner), :]
        return remote(view, view, fs, fl, {"chan": partner})

    def relay_copy(row, owner):
        view = xg.at[row, block(owner), :]
        return remote(view, view, fs, fr.at[row - lead], {"chan": partner})

    def relay_part(owner):
        view = xp.at[chip, block(owner), :]
        return remote(view, view, fs, fr.at[whole - lead], {"chan": partner})

    def sent(count, sem, device):
        view = xg.at[0:count, block(chan_at), :]
        remote(view, view, sem, fl, device).wait_send()

    def half_of(half):
        return slice(half * (rows // 2), (half + 1) * (rows // 2))

    def side_copy(group, half):
        source = xg.at[half_of(half), block_cut(chan_at, group), :]
        target = halo.at[minor, half_of(half), cut_of(group), :]
        return remote(source, target, ys, yr.at[half, group], {"rad": other})

    def far_copy(some_rows, some, place):
        source = halo.at[near_slot, some_rows, some, :]
        target = halo.at[minor, some_rows, some, :]
        return remote(source, target, zs, zr.at[place], {"rad": ahead})

    def via_copy():
        source = xg.at[half_of(1), block_cut(chan_at, groups - 1), :]
        return remote(source, via, vs.at[0], vr.at[0], {"rad": behind})

    def via_forward():
        target = halo.at[near_slot, half_of(1), cut_of(groups - 1), :]
        return remote(via, target, vs.at[1], vr.at[1], {"rad": other})

    every = slice(0, rows)
    small = [
        pltpu.make_async_copy(kin_main, kin, small_sem.at[0]),
        pltpu.make_async_copy(chan_main, chan_l, small_sem.at[1]),
    ]
    for part in range(len(LOADS)):
        for which in range(2):
            load(which, part).start()

    barrier = pltpu.get_barrier_semaphore()
    for step in range(1, chips):
        pl.semaphore_signal(
            barrier, inc=1, device_id={"chan": chip_peer(step)}, device_id_type=MESH
        )
    pl.semaphore_signal(barrier, inc=1, device_id={"chan": partner}, device_id_type=MESH)
    pl.semaphore_signal(barrier, inc=1, device_id={"rad": other}, device_id_type=MESH)

    @pl.when(has_ahead)
    def _():
        pl.semaphore_signal(barrier, inc=1, device_id={"rad": ahead}, device_id_type=MESH)

    @pl.when(has_behind)
    def _():
        pl.semaphore_signal(barrier, inc=1, device_id={"rad": behind}, device_id_type=MESH)

    def form(group):
        for part in range(2):
            first = pk.at[0, part].reshape(chans * rows, width)
            second = pk.at[1, part].reshape(chans * rows, width)
            cut = slice(part * width, (part + 1) * width)
            for row in range(rows):
                place = (pl.ds(group * GROUP * rows + row, GROUP, stride=rows), slice(None))
                value = first[place] + 0.5 * second[place]
                sec[row, cut_of(group), cut] = value
                rounded = value.astype(jnp.bfloat16)
                xg[row, block_cut(chan_at, group), cut] = rounded
                if row >= whole:
                    lane = slice((row - whole) * width, (row - whole + 1) * width)
                    xp[part, block_cut(chan_at, group), lane] = rounded

    def send_group(group):
        for half in range(2):
            side_copy(group, half).start()
        lead_copy(block_cut(chan_at, group)).start()

    arrive(0)
    form(jnp.int32(0))
    pl.semaphore_wait(
        barrier, chips + 1 + has_ahead.astype(jnp.int32) + has_behind.astype(jnp.int32)
    )
    send_group(0)
    arrive(1)
    form(jnp.int32(1))

    def form_next(group, carry):
        form(group)
        send_group(group - 1)
        return carry

    lax.fori_loop(2, LOADS[1][1], form_next, 0)
    for part in range(2, len(LOADS)):
        arrive(part)
        lax.fori_loop(LOADS[part][0], LOADS[part][1], form_next, 0)
    for copy in small:
        copy.start()
    for order in range(orders):
        load_weight(order).start()
        load_peer_weight(order).start()

    send_group(groups - 1)

    @pl.when(has_behind)
    def _():
        via_copy().start()

    part_copy(1 - chip, chan_at).start()
    for row in range(lead, whole):
        chip_copy(row, chan_at).start()
    for index in range(0, whole, lead):
        core_copy(slice(index, min(index + lead, whole)), chan_at).start()
    core_part(chan_at).start()

    def pass_on(group, half):
        side_copy(group, half).wait_recv()
        last = jnp.logical_and(group == groups - 1, half == 1)

        @pl.when(jnp.logical_and(has_ahead, jnp.logical_not(last)))
        def _():
            far_copy(half_of(half), cut_of(group), group).start()

    def forward(group, half):
        @pl.when(group + core < groups)
        def _():
            pass_on(group + core, half)

    @pl.when(core == 1)
    def _():
        pass_on(0, 0)

    for copy in small:
        copy.wait()
    kin_high, kin_low = split_bf16(kin[...])
    both = jnp.concatenate([kin_high, kin_low], axis=1)
    kk[0:width, :] = both
    kk[width : 2 * width, :] = both

    band = kin[pl.ds(pl.multiple_of(rad_at * rows, rows), rows), :]
    size = rows * GROUP
    tall = jnp.broadcast_to(band[:, None, :], (rows, GROUP, width)).reshape(size, width)
    tall_high, tall_low = split_bf16(tall)
    at_row = lax.broadcasted_iota(jnp.int32, (size, size), 0)
    at_col = lax.broadcasted_iota(jnp.int32, (size, size), 1)
    same = (at_row % GROUP) == (at_col % GROUP)
    from_j = lax.broadcasted_iota(jnp.int32, (width, size), 0)
    to_col = lax.broadcasted_iota(jnp.int32, (width, size), 1)
    for side in range(3):
        pick = from_j == (rad_at + side - 1) * rows + to_col // GROUP
        pick = jnp.where(pick, 1.0, 0.0).astype(jnp.bfloat16)
        for level, source in enumerate((tall_high, tall_low)):
            wide = jnp.dot(source, pick, preferred_element_type=jnp.float32)
            wr1[side, level * size : (level + 1) * size, :] = jnp.where(same, wide, 0.0).astype(
                jnp.bfloat16
            )

    @pl.when(core == 1)
    def _():
        pass_on(0, 1)

    @pl.when(jnp.logical_not(has_behind))
    def _():
        halo[far_slot] = jnp.zeros(halo.shape[1:], halo.dtype)

    second_r = 1.0 + 8.0 * (
        lax.broadcasted_iota(jnp.int32, (1, lanes), 1) % width
    ).astype(jnp.float32) / width
    inner_r = second_r[:, :width]
    lvals = chan_l[...].astype(jnp.float32).astype(jnp.bfloat16)
    first = lax.broadcasted_iota(jnp.int32, (2, lanes), 0)
    spread = first == lax.broadcasted_iota(jnp.int32, (2, lanes), 1) // width
    spread = jnp.where(spread, 1.0, 0.0).astype(jnp.bfloat16)
    lwide = lax.dot_general(
        lvals, spread, (((0,), (0,)), ((), ())), preferred_element_type=jnp.float32
    )
    lwide = lwide * (lwide + 1.0)
    lmul[...] = lwide[:, :width]
    langle[...] = lwide[:, width:] / (2.0 * inner_r * inner_r) - 2.0 / inner_r

    def radius(row):
        place = jnp.full((1, lanes), rad_at * rows + row, jnp.int32)
        return 1.0 + 8.0 * place.astype(jnp.float32) / width

    def local_row(row):
        first_r = radius(row)[:, :width]
        scale = 1.0 / (2.0 * first_r * first_r)
        shift = 2.0 / first_r
        potential = lmul[...] * scale + langle[...] - shift
        for part in range(2):
            cut = slice(part * width, (part + 1) * width)
            value = sec[row, :, cut]
            high = xg[row, block(chan_at), cut]
            low = (value - high.astype(jnp.float32)).astype(jnp.bfloat16)
            both = jnp.dot(
                jnp.concatenate([high, low], axis=1), kk[...], preferred_element_type=jnp.float32
            )
            total = both[:, :width] + both[:, width:] + potential * value
            acc[row, :, cut] = acc[row, :, cut] + total

    def mix(side, value):
        both = jnp.dot(wr1[side], value, preferred_element_type=jnp.float32)
        return both[:size] + both[size:]

    def own_group(index):
        first = pl.multiple_of(index * GROUP, GROUP)
        start = pl.multiple_of(chan_at * chans + first, GROUP)
        high = xg[:, pl.ds(start, GROUP), :].reshape(size, lanes)
        value = sec[:, pl.ds(first, GROUP), :].reshape(size, lanes)
        low = (value - high.astype(jnp.float32)).astype(jnp.bfloat16)
        total = mix(1, high) + jnp.dot(
            wr1[1, 0:size, :], low, preferred_element_type=jnp.float32
        )
        acc[:, pl.ds(first, GROUP), :] = total.reshape(rows, GROUP, lanes)

    def side_group(index):
        first = pl.multiple_of(index * GROUP, GROUP)
        cut = pl.ds(first, GROUP)
        total = mix(0, halo[0, :, cut, :].reshape(size, lanes)) + mix(
            2, halo[1, :, cut, :].reshape(size, lanes)
        )
        acc[:, cut, :] = acc[:, cut, :] + total.reshape(rows, GROUP, lanes)

    def factors_of(first_r):
        inverse = 1.0 / jnp.maximum(first_r, second_r)
        ratio = jnp.minimum(first_r, second_r) * inverse
        factors = [inverse]
        for _ in range(orders - 2):
            factors.append(factors[-1] * ratio)
        factors.append(field[0] * (first_r + second_r))
        return factors

    def summed(factors, matrices, source, some):
        total = jnp.zeros((chans // 2, lanes), jnp.float32)
        for order in range(orders):
            total = total + factors[order] * jnp.dot(
                matrices[order, some, :], source[...], preferred_element_type=jnp.float32
            )
        return total.astype(jnp.bfloat16)

    cuts = (slice(0, chans // 2), slice(chans // 2, chans))

    def couple(row):
        factors = factors_of(radius(row))
        for some in cuts:
            total = summed(factors, weights, xg.at[row], some)
            acc[row, some, :] = acc[row, some, :] + total.astype(jnp.float32)

    def couple_parts(matrices, target):
        place = lax.broadcasted_iota(jnp.int32, (1, lanes), 1) // width
        place = place + (rad_at * rows + whole)
        factors = factors_of(1.0 + 8.0 * place.astype(jnp.float32) / width)
        for some in cuts:
            target[some, :] = summed(factors, matrices, xp.at[chip], some)

    def couple_peer():
        relay_part(peer + 1 - 2 * core).wait_recv()
        couple_parts(peer_weights, back)

    def couple_own():
        back_copy(chip).start()
        couple_parts(weights, coupled.at[chip])

    def relay(base):
        row = base + core

        @pl.when(jnp.logical_and(row >= lead, row < whole))
        def _():
            chip_copy(row, peer).wait_recv()
            relay_copy(row, peer).start()

    def take_row(row):
        @pl.when(row >= lead)
        def _():
            relay_copy(row, peer + 1 - 2 * core).wait_recv()

        couple(row)

    def take_side(group):
        @pl.when(has_behind)
        def _():
            far_copy(every, cut_of(group), group).wait_recv()

        side_group(group)

    def mix_slot(slot, cut):
        value = halo[slot, :, cut, :].reshape(size, lanes)
        total = mix(2 * slot, value).reshape(rows, GROUP, lanes)
        acc[:, cut, :] = acc[:, cut, :] + total

    def each_of(first, last, work):
        def step(index, carry):
            work(index)
            return carry

        lax.fori_loop(first, last, step, 0)

    def merge_top(first, last):
        each_of(first, last, lambda group: merge(acc, top, group, range(rows // 2)))

    def take_lead(turn):
        @pl.when(core == turn)
        def _():
            lead_copy(block(peer)).wait_recv()
            relay_lead(peer).start()

    forward(0, 0)
    each_of(0, 3, own_group)
    forward(0, 1)
    each_of(3, 4, own_group)
    for half in range(2):
        forward(1, half)
        each_of(4 + 4 * half, 8 + 4 * half, own_group)
    for half in range(2):
        forward(2, half)
        take_lead(1 - half)
        each_of(6 * half, 6 + 6 * half, local_row)
    pltpu.make_async_copy(weights, weights, small_sem.at[2]).wait()
    pltpu.make_async_copy(peer_weights, peer_weights, small_sem.at[3]).wait()
    core_copy(slice(0, whole), partner).wait_recv()
    core_part(partner).wait_recv()
    each_of(12, rows - 1, local_row)

    @pl.when(has_ahead)
    def _():
        via_copy().wait_recv()
        via_forward().start()

    def main(index, carry):
        start = index * lead

        def each(first, second):
            return (1 - core) * first + core * second

        def when(condition, work, *args):
            @pl.when(condition)
            def _():
                work(*args)

        even, odd = (core == 0, core == 1)
        started, ended = (index == 1, index == 3)
        forward(3 * index, 0)

        @pl.when(started)
        def _():
            part_copy(chip, peer).wait_recv()
            relay_part(peer).start()
            local_row(rows - 1)
            relay_lead(peer + 1 - 2 * core).wait_recv()

        when(jnp.logical_or(odd, index != 2), take_row, each(index - 1, start - 2))
        when(jnp.logical_and(even, index == 2), couple_peer)
        relay(start - 1)
        forward(3 * index, 1)
        take_side(3 * index - 2)
        when(jnp.logical_or(even, started), take_row, each(start - 1, 0))
        when(jnp.logical_and(odd, index == 2), couple_peer)
        forward(3 * index + 1, 0)
        relay(start)
        take_row(start - core)
        when(ended, merge_top, 0, groups - 4)
        when(started, take_side, 0)
        forward(3 * index + 1, 1)
        when(jnp.logical_or(odd, started), take_row, each(1, start))
        when(jnp.logical_and(even, index == 2), couple_own)
        take_side(3 * index - 1)
        relay(start + 1)
        forward(3 * index + 2, 0)
        when(jnp.logical_or(even, started), take_row, each(start + 1, 1))
        when(jnp.logical_and(odd, index == 2), couple_own)
        when(index < 3, forward, 3 * index + 2, 1)
        relay(start + 2)
        take_side(3 * index)
        when(start + 2 - core < whole, take_row, start + 2 - core)
        return carry

    lax.fori_loop(1, 4, main, 0)

    merge_top(groups - 4, groups - 2)
    back_copy(1 - chip).wait_recv()
    for place in range(rows - whole):
        for part in range(2):
            lane = slice(part * width, (part + 1) * width)
            value = coupled[part, :, place * width : (place + 1) * width].astype(jnp.float32)
            acc[whole + place, :, lane] = acc[whole + place, :, lane] + value
    forward(groups - 1, 1)
    mix_slot(near_slot, cut_of(groups - 1))
    take_side(groups - 2)

    @pl.when(has_behind)
    def _():
        far_copy(half_of(0), cut_of(groups - 1), groups - 1).wait_recv()
        via_forward().wait_recv()

    mix_slot(far_slot, cut_of(groups - 1))

    core_copy(slice(0, whole), chan_at).wait_send()
    core_part(chan_at).wait_send()
    sent(lead, hs, {"chan": peer})
    sent(rows - lead, xs, {"chan": peer})
    sent(rows - 1, fs, {"chan": partner})
    sent(rows, ys, {"rad": other})

    @pl.when(has_ahead)
    def _():
        view = xg.at[0 : rows // 2, 0 : (2 * groups - 1) * GROUP, :]
        remote(view, view, zs, zr.at[0], {"rad": ahead}).wait_send()
        via_forward().wait_send()

    @pl.when(has_behind)
    def _():
        via_copy().wait_send()


def device_step(peers, rads, psi, k_prev, gaunt, dipole, kinetic, chan_l, field_amp):
    _, chans, rows, width = psi.shape
    fits = (
        chans == 3 * 4 * GROUP
        and rows == GROUP
        and peers == 4
        and rads % 2 == 0
        and width == rads * rows
        and width == 128
    )
    if not fits:
        return on_device(psi, k_prev, gaunt, dipole, kinetic, chan_l, field_amp)
    orders = gaunt.shape[0] + 1
    chips = peers // 2
    groups = chans // GROUP
    lanes = 2 * width
    size = rows * GROUP
    f32, bf16, dma = (jnp.float32, jnp.bfloat16, pltpu.SemaphoreType.DMA)
    main_memory = pl.BlockSpec(memory_space=pltpu.HBM)
    vmem = pl.BlockSpec(memory_space=pltpu.VMEM)
    summed = jax.ShapeDtypeStruct((rows, chans, lanes), f32)
    top = jax.ShapeDtypeStruct((2, chans, rows // 2, width), f32)
    psi, k_prev, gaunt, dipole, kinetic, chan_l = (
        pltpu.with_memory_space_constraint(value, pltpu.HBM)
        for value in (psi, k_prev, gaunt, dipole, kinetic, chan_l.T)
    )
    parts = pl.pallas_call(
        functools.partial(fused_kernel, peers, rads),
        out_shape=(summed, top),
        in_specs=[main_memory] * 6 + [pl.BlockSpec(memory_space=pltpu.SMEM)],
        out_specs=(vmem, vmem),
        scratch_shapes=[
            pltpu.VMEM(kinetic.shape, f32),
            pltpu.VMEM((2, chans), jnp.int32),
            pltpu.VMEM((2, 2, chans, rows, width), f32),
            pltpu.VMEM((rows, chans, lanes), f32),
            pltpu.VMEM((rows, peers * chans, lanes), bf16),
            pltpu.VMEM((2, peers * chans, lanes), bf16),
            pltpu.VMEM((2, chans, lanes), bf16),
            pltpu.VMEM((chans, lanes), bf16),
            pltpu.VMEM((2, rows, chans, lanes), bf16),
            pltpu.VMEM((orders, chans, peers * chans), bf16),
            pltpu.VMEM((orders, chans, peers * chans), bf16),
            pltpu.VMEM((3, 2 * size, size), bf16),
            pltpu.VMEM((lanes, lanes), bf16),
            pltpu.VMEM((chans, width), f32),
            pltpu.VMEM((chans, width), f32),
            dma((len(LOADS),)),
            dma((4,)),
            dma,
            dma,
            dma,
            dma((rows - rows // 4,)),
            dma,
            dma((2,)),
            dma,
            dma,
            dma((rows - rows // 4 - 1,)),
            dma,
            dma((2, groups)),
            dma,
            dma((groups,)),
            dma((2,)),
            dma((2,)),
            pltpu.VMEM((rows // 2, GROUP, lanes), bf16),
        ],
        compiler_params=pltpu.CompilerParams(
            collective_id=0, has_side_effects=True, vmem_limit_bytes=36 * 1024 * 1024
        ),
    )(psi, k_prev, gaunt, dipole, kinetic, chan_l, field_amp)
    return pl.pallas_call(
        finish_kernel,
        out_shape=jax.ShapeDtypeStruct(psi.shape, f32),
        in_specs=[vmem, vmem],
        out_specs=main_memory,
        scratch_shapes=[pltpu.VMEM(psi.shape, f32), dma],
        compiler_params=pltpu.CompilerParams(vmem_limit_bytes=8 * 1024 * 1024),
    )(*parts)


def solution(mesh):
    placed = (
        P(None, "chan", "rad", None),
        P(None, "chan", "rad", None),
        P(),
        P(),
        P(),
        P("chan", None),
        P(),
    )
    return jax.shard_map(
        functools.partial(device_step, mesh.shape["chan"], mesh.shape["rad"]),
        mesh=mesh,
        in_specs=placed,
        out_specs=P(None, "chan", "rad", None),
        check_vma=False,
    )
```

```python
import functools

import jax
import jax.numpy as jnp
from jax import lax
from jax.experimental import pallas as pl
from jax.experimental.pallas import tpu as pltpu
from jax.sharding import PartitionSpec as P


def extended(array, sides, width):
    for axis, dim in sides:
        peers, length = (lax.axis_size(axis), array.shape[dim])
        up = [(i, (i + 1) % peers) for i in range(peers - 1)]
        down = [(j, i) for i, j in up]
        last = lax.slice_in_dim(array, length - width, length, axis=dim)
        initial = lax.slice_in_dim(array, 0, width, axis=dim)
        before = lax.ppermute(last, axis, up)
        after = lax.ppermute(initial, axis, down)
        array = jnp.concatenate([before, array, after], axis=dim)
    return array


def on_device(psi, k_prev, gaunt, dipole, kinetic, chan_l, field_amp):
    highest = lax.Precision.HIGHEST
    section = psi + 0.5 * k_prev
    local_chan = section.shape[1]
    rows = section.shape[2]
    width = section.shape[3]
    rad_at = lax.axis_index("rad")
    first_r = (
        1.0 + 8.0 * (rad_at * rows + jnp.arange(rows, dtype=jnp.int32)).astype(jnp.float32) / width
    )
    second_r = 1.0 + 8.0 * jnp.arange(width, dtype=jnp.float32) / width
    along_r2 = jnp.einsum("acij,kj->acik", section, kinetic, precision=highest)
    padded = extended(section.astype(jnp.bfloat16), (("rad", 2),), rows).astype(section.dtype)
    band = lax.dynamic_slice_in_dim(kinetic, rad_at * rows, rows, 0)
    widened = jnp.pad(band, ((0, 0), (rows, rows)))
    local_band = lax.dynamic_slice_in_dim(widened, rad_at * rows, 3 * rows, 1)
    along_r1 = jnp.einsum("ij,acjk->acik", local_band, padded, precision=highest)
    lvals = chan_l.astype(jnp.float32)
    first_l = lvals[:, 0] * (lvals[:, 0] + 1.0)
    second_l = lvals[:, 1] * (lvals[:, 1] + 1.0)
    potential = (
        first_l[:, None, None] / (2.0 * first_r * first_r)[None, :, None]
        + second_l[:, None, None] / (2.0 * second_r * second_r)[None, None, :]
        - 2.0 / first_r[None, :, None]
        - 2.0 / second_r[None, None, :]
    )
    sent = section.astype(jnp.bfloat16).reshape(2, local_chan, rows * width)
    chan_at = lax.axis_index("chan")
    block = lax.all_to_all(sent, "chan", split_axis=2, concat_axis=1, tiled=True)
    count = block.shape[2]
    place = chan_at * count + jnp.arange(count, dtype=jnp.int32)
    row_r = 1.0 + 8.0 * (rad_at * rows + place // width).astype(jnp.float32) / width
    col_r = 1.0 + 8.0 * (place % width).astype(jnp.float32) / width
    far = jnp.maximum(row_r, col_r)
    near = jnp.minimum(row_r, col_r)
    inverse = 1.0 / far
    ratio = near * inverse
    power = inverse
    total = jnp.zeros(block.shape, jnp.float32)
    for order in range(gaunt.shape[0]):
        mixed = jnp.einsum("cd,adq->acq", gaunt[order], block, preferred_element_type=jnp.float32)
        total = total + power[None, None, :] * mixed
        power = power * ratio
    mixed = jnp.einsum("cd,adq->acq", dipole, block, preferred_element_type=jnp.float32)
    total = total + (field_amp[0] * (row_r + col_r))[None, None, :] * mixed
    coupled = lax.all_to_all(
        total.astype(jnp.bfloat16), "chan", split_axis=1, concat_axis=2, tiled=True
    )
    coupled = coupled.reshape(coupled.shape[0], local_chan, rows, width)
    ham = along_r1 + along_r2 + potential[None] * section + coupled.astype(jnp.float32)
    return jnp.stack([ham[1], -ham[0]])


MESH = pl.DeviceIdType.MESH
GROUP = 16
PAIRS = 2
TAIL = 2
LOADS = ((0, 1), (1, 4), (4, 12))


def split_bf16(value):
    high = value.astype(jnp.bfloat16)
    return high, (value - high.astype(jnp.float32)).astype(jnp.bfloat16)


def lay_out(target, group, row, value):
    _, chans, height, width = target.shape
    place = (pl.ds(group * GROUP * height + row, GROUP, stride=height), slice(None))
    target.at[0].reshape(chans * height, width)[place] = value[:, width:]
    target.at[1].reshape(chans * height, width)[place] = -value[:, :width]


def finish_kernel(rads, acc, early, far_tail, wr1, out, late, sem):
    rows, chans, lanes = acc.shape
    size = rows * GROUP
    done = chans - TAIL * GROUP
    rad_at = lax.axis_index("rad")
    minor = rad_at % 2
    behind = rad_at - 2 + 4 * minor
    has_behind = jnp.logical_and(behind >= 0, behind < rads)
    pltpu.make_async_copy(early.at[:, 0:done], out.at[:, 0:done], sem).start()

    for group in range(TAIL):
        cut = slice(group * GROUP, (group + 1) * GROUP)
        there = slice(done + group * GROUP, done + (group + 1) * GROUP)

        @pl.when(has_behind)
        def _():
            value = far_tail[:, cut, :].reshape(size, lanes)
            both = jnp.dot(wr1[2 * minor], value, preferred_element_type=jnp.float32)
            total = (both[:size] + both[size:]).reshape(rows, GROUP, lanes)
            for row in range(rows):
                lay_out(late, group, row, acc[row, there, :] + total[row])

        @pl.when(jnp.logical_not(has_behind))
        def _():
            for row in range(rows):
                lay_out(late, group, row, acc[row, there, :])

        pltpu.make_async_copy(late.at[:, cut], out.at[:, there], sem).start()
    pltpu.make_async_copy(early, out, sem).wait()


def fused_kernel(
    peers,
    rads,
    psi,
    k_prev,
    gaunt,
    dipole,
    kin_main,
    chan_main,
    field,
    acc,
    early,
    far_tail,
    wr1,
    kin,
    chan_l,
    pk,
    sec,
    xg,
    xp,
    coupled,
    halo,
    weights,
    kk,
    lmul,
    langle,
    load_sem,
    small_sem,
    hr,
    xs,
    xr,
    cr,
    fl,
    fr,
    yr,
    zs,
    zr,
    vs,
    vr,
    via,
):
    rows, chans, lanes = sec.shape
    width = lanes // 2
    orders = weights.shape[1]
    chips = peers // 2
    groups = chans // GROUP
    lead = rows // 4
    chan_at = lax.axis_index("chan")
    rad_at = lax.axis_index("rad")
    core = chan_at % 2
    chip = chan_at // 2
    partner = chan_at + 1 - 2 * core
    minor = rad_at % 2
    other = rad_at + 1 - 2 * minor
    ahead = rad_at + 2 - 4 * minor
    behind = rad_at - 2 + 4 * minor
    has_ahead = jnp.logical_and(ahead >= 0, ahead < rads)
    has_behind = jnp.logical_and(behind >= 0, behind < rads)
    near_slot = 1 - minor
    far_slot = minor
    whole = rows - 2 * PAIRS
    back = 2
    peer = lax.rem(chip + 1, chips) * 2 + core

    def block(owner):
        return pl.ds(pl.multiple_of(owner * chans, GROUP), chans)

    def cut_of(group):
        return pl.ds(pl.multiple_of(group * GROUP, GROUP), GROUP)

    def block_cut(owner, group):
        return pl.ds(pl.multiple_of(owner * chans + group * GROUP, GROUP), GROUP)

    def chip_peer(step):
        return lax.rem(chip + step, chips) * 2 + core

    def chip_source(step):
        return lax.rem(chip - step + chips, chips) * 2 + core

    def load(which, part):
        first, last = LOADS[part]
        cut = slice(first * GROUP, last * GROUP)
        return pltpu.make_async_copy(
            (psi, k_prev)[which].at[:, cut, :, :], pk.at[which, :, cut, :, :], load_sem.at[part]
        )

    def arrive(part):
        first, last = LOADS[part]
        view = pk.at[:, :, first * GROUP : last * GROUP, :, :]
        pltpu.make_async_copy(view, view, load_sem.at[part]).wait()

    def load_weight(kind, order):
        source = gaunt.at[order] if order < orders - 1 else dipole
        owner = (peer, chan_at)[kind]
        return pltpu.make_async_copy(
            source.at[block(owner), :], weights.at[kind, order], small_sem.at[2]
        )

    def remote(source, target, send, recv, device):
        return pltpu.make_async_remote_copy(
            src_ref=source,
            dst_ref=target,
            send_sem=send,
            recv_sem=recv,
            device_id=device,
            device_id_type=MESH,
        )

    def lead_copy(some):
        view = xg.at[0:lead, some, :]
        return remote(view, view, xs, hr, {"chan": peer})

    def chip_copy(row, owner):
        view = xg.at[row, block(owner), :]
        return remote(view, view, xs, xr.at[row - lead], {"chan": peer})

    def part_copy(part, owner):
        view = xp.at[part, :, block(owner), :]
        return remote(view, view, xs, xr.at[whole - lead], {"chan": peer})

    def back_copy(part):
        source, target = (coupled.at[back], coupled.at[part])
        return remote(source, target, xs, xr.at[whole - lead + 1], {"chan": peer})

    def core_copy(some_rows, owner):
        view = xg.at[some_rows, block(owner), :]
        return remote(view, view, xs, cr, {"chan": partner})

    def core_part(owner):
        view = xp.at[chip, :, block(owner), :]
        return remote(view, view, xs, cr, {"chan": partner})

    def relay_lead(owner):
        view = xg.at[0:lead, block(owner), :]
        return remote(view, view, xs, fl, {"chan": partner})

    def relay_copy(row, owner):
        view = xg.at[row, block(owner), :]
        return remote(view, view, xs, fr.at[row - lead], {"chan": partner})

    def relay_part(owner):
        view = xp.at[chip, :, block(owner), :]
        return remote(view, view, xs, fr.at[whole - lead], {"chan": partner})

    def half_of(half):
        return slice(half * (rows // 2), (half + 1) * (rows // 2))

    def side_copy(group, half):
        source = xg.at[half_of(half), block_cut(chan_at, group), :]
        target = halo.at[minor, half_of(half), cut_of(group), :]
        return remote(source, target, xs, yr.at[half, group], {"rad": other})

    def far_copy(some_rows, some, place):
        source = halo.at[near_slot, some_rows, some, :]
        target = halo.at[minor, some_rows, some, :]
        return remote(source, target, zs, zr.at[place], {"rad": ahead})

    def tail_cut(group):
        return pl.ds(pl.multiple_of((group - groups + TAIL) * GROUP, GROUP), GROUP)

    def tail_copy(some_rows, group):
        source = halo.at[near_slot, some_rows, cut_of(group), :]
        target = far_tail.at[some_rows, tail_cut(group), :]
        return remote(source, target, zs, zr.at[group], {"rad": ahead})

    def via_copy(some_rows):
        source = xg.at[some_rows, block_cut(chan_at, groups - 1), :]
        return remote(source, via.at[some_rows], vs, vr.at[0], {"rad": behind})

    def via_forward(some_rows):
        target = far_tail.at[some_rows, tail_cut(groups - 1), :]
        return remote(via.at[some_rows], target, zs, vr.at[1], {"rad": other})

    def by_core(condition, work):
        for at, some_rows in enumerate((every, half_of(1))):

            @pl.when(jnp.logical_and(core == at, condition))
            def _():
                work(some_rows)

    every = slice(0, rows)
    small = [
        pltpu.make_async_copy(kin_main, kin, small_sem.at[0]),
        pltpu.make_async_copy(chan_main, chan_l, small_sem.at[1]),
    ]
    for part in range(len(LOADS)):
        for which in range(2):
            load(which, part).start()

    barrier = pltpu.get_barrier_semaphore()
    for step in range(1, chips):
        pl.semaphore_signal(
            barrier, inc=1, device_id={"chan": chip_peer(step)}, device_id_type=MESH
        )
    pl.semaphore_signal(barrier, inc=1, device_id={"chan": partner}, device_id_type=MESH)
    pl.semaphore_signal(barrier, inc=1, device_id={"rad": other}, device_id_type=MESH)

    @pl.when(has_ahead)
    def _():
        pl.semaphore_signal(barrier, inc=1, device_id={"rad": ahead}, device_id_type=MESH)

    @pl.when(has_behind)
    def _():
        pl.semaphore_signal(barrier, inc=1, device_id={"rad": behind}, device_id_type=MESH)

    def form(group):
        for part in range(2):
            first = pk.at[0, part].reshape(chans * rows, width)
            second = pk.at[1, part].reshape(chans * rows, width)
            cut = slice(part * width, (part + 1) * width)
            for row in range(rows):
                place = (pl.ds(group * GROUP * rows + row, GROUP, stride=rows), slice(None))
                value = first[place] + 0.5 * second[place]
                sec[row, cut_of(group), cut] = value
                rounded = value.astype(jnp.bfloat16)
                xg[row, block_cut(chan_at, group), cut] = rounded
                if row >= whole:
                    pair, turn = divmod(row - whole, 2)
                    lane = slice(turn * width, (turn + 1) * width)
                    xp[part, pair, block_cut(chan_at, group), lane] = rounded

    def send_group(group):
        for half in range(2):
            side_copy(group, half).start()
        lead_copy(block_cut(chan_at, group)).start()

    arrive(0)
    form(jnp.int32(0))
    pl.semaphore_wait(
        barrier, chips + 1 + has_ahead.astype(jnp.int32) + has_behind.astype(jnp.int32)
    )
    send_group(0)
    arrive(1)
    form(jnp.int32(1))

    def form_next(group, carry):
        form(group)
        send_group(group - 1)
        return carry

    lax.fori_loop(2, LOADS[1][1], form_next, 0)
    for part in range(2, len(LOADS)):
        arrive(part)
        lax.fori_loop(LOADS[part][0], LOADS[part][1], form_next, 0)
    for copy in small:
        copy.start()
    for order in range(orders):
        for kind in range(2):
            load_weight(kind, order).start()

    send_group(groups - 1)

    by_core(has_behind, lambda some_rows: via_copy(some_rows).start())

    part_copy(1 - chip, chan_at).start()
    for row in range(lead, whole):
        chip_copy(row, chan_at).start()
    for index in range(0, whole, lead):
        core_copy(slice(index, min(index + lead, whole)), chan_at).start()
    core_part(chan_at).start()

    def pass_on(group, half):
        side_copy(group, half).wait_recv()

        @pl.when(jnp.logical_and(has_ahead, group < groups - TAIL))
        def _():
            far_copy(half_of(half), cut_of(group), group).start()

        late = jnp.logical_and(group >= groups - TAIL, group < groups - 1 + core * (1 - half))

        @pl.when(jnp.logical_and(has_ahead, late))
        def _():
            tail_copy(half_of(half), group).start()

    def forward(group, half):
        @pl.when(group + core < groups)
        def _():
            pass_on(group + core, half)

    @pl.when(core == 1)
    def _():
        pass_on(0, 0)

    for copy in small:
        copy.wait()
    kin_high, kin_low = split_bf16(kin[...])
    both = jnp.concatenate([kin_high, kin_low], axis=1)
    kk[0:width, :] = both
    kk[width : 2 * width, :] = both

    band = kin[pl.ds(pl.multiple_of(rad_at * rows, rows), rows), :]
    size = rows * GROUP
    tall = jnp.broadcast_to(band[:, None, :], (rows, GROUP, width)).reshape(size, width)
    tall_high, tall_low = split_bf16(tall)
    at_row = lax.broadcasted_iota(jnp.int32, (size, size), 0)
    at_col = lax.broadcasted_iota(jnp.int32, (size, size), 1)
    same = (at_row % GROUP) == (at_col % GROUP)
    from_j = lax.broadcasted_iota(jnp.int32, (width, size), 0)
    to_col = lax.broadcasted_iota(jnp.int32, (width, size), 1)
    for side in range(3):
        pick = from_j == (rad_at + side - 1) * rows + to_col // GROUP
        pick = jnp.where(pick, 1.0, 0.0).astype(jnp.bfloat16)
        for level, source in enumerate((tall_high, tall_low)):
            wide = jnp.dot(source, pick, preferred_element_type=jnp.float32)
            wr1[side, level * size : (level + 1) * size, :] = jnp.where(same, wide, 0.0).astype(
                jnp.bfloat16
            )

    @pl.when(core == 1)
    def _():
        pass_on(0, 1)

    second_r = 1.0 + 8.0 * (
        lax.broadcasted_iota(jnp.int32, (1, lanes), 1) % width
    ).astype(jnp.float32) / width
    inner_r = second_r[:, :width]
    lvals = chan_l[...].astype(jnp.float32).astype(jnp.bfloat16)
    first = lax.broadcasted_iota(jnp.int32, (2, lanes), 0)
    spread = first == lax.broadcasted_iota(jnp.int32, (2, lanes), 1) // width
    spread = jnp.where(spread, 1.0, 0.0).astype(jnp.bfloat16)
    lwide = lax.dot_general(
        lvals, spread, (((0,), (0,)), ((), ())), preferred_element_type=jnp.float32
    )
    lwide = lwide * (lwide + 1.0)
    lmul[...] = lwide[:, :width]
    langle[...] = lwide[:, width:] / (2.0 * inner_r * inner_r) - 2.0 / inner_r

    def radius(row):
        place = jnp.full((1, lanes), rad_at * rows + row, jnp.int32)
        return 1.0 + 8.0 * place.astype(jnp.float32) / width

    def local_row(row):
        first_r = radius(row)[:, :width]
        scale = 1.0 / (2.0 * first_r * first_r)
        shift = 2.0 / first_r
        potential = lmul[...] * scale + langle[...] - shift
        for part in range(2):
            cut = slice(part * width, (part + 1) * width)
            value = sec[row, :, cut]
            high = xg[row, block(chan_at), cut]
            low = (value - high.astype(jnp.float32)).astype(jnp.bfloat16)
            both = jnp.dot(
                jnp.concatenate([high, low], axis=1), kk[...], preferred_element_type=jnp.float32
            )
            total = both[:, :width] + both[:, width:] + potential * value
            acc[row, :, cut] = acc[row, :, cut] + total

    def mix(side, value):
        both = jnp.dot(wr1[side], value, preferred_element_type=jnp.float32)
        return both[:size] + both[size:]

    def own_group(index):
        first = pl.multiple_of(index * GROUP, GROUP)
        start = pl.multiple_of(chan_at * chans + first, GROUP)
        high = xg[:, pl.ds(start, GROUP), :].reshape(size, lanes)
        value = sec[:, pl.ds(first, GROUP), :].reshape(size, lanes)
        low = (value - high.astype(jnp.float32)).astype(jnp.bfloat16)
        total = mix(1, high) + jnp.dot(
            wr1[1, 0:size, :], low, preferred_element_type=jnp.float32
        )
        acc[:, pl.ds(first, GROUP), :] = total.reshape(rows, GROUP, lanes)

    def side_group(index):
        first = pl.multiple_of(index * GROUP, GROUP)
        cut = pl.ds(first, GROUP)
        total = mix(0, halo[0, :, cut, :].reshape(size, lanes)) + mix(
            2, halo[1, :, cut, :].reshape(size, lanes)
        )
        acc[:, cut, :] = acc[:, cut, :] + total.reshape(rows, GROUP, lanes)

    def factors_of(first_r):
        inverse = 1.0 / jnp.maximum(first_r, second_r)
        ratio = jnp.minimum(first_r, second_r) * inverse
        factors = [inverse]
        for _ in range(orders - 2):
            factors.append(factors[-1] * ratio)
        factors.append(field[0] * (first_r + second_r))
        return factors

    def summed(factors, matrices, source, some):
        total = jnp.zeros((chans // 2, lanes), jnp.float32)
        for order in range(orders):
            total = total + factors[order] * jnp.dot(
                matrices[order, some, :], source[...], preferred_element_type=jnp.float32
            )
        return total.astype(jnp.bfloat16)

    cuts = (slice(0, chans // 2), slice(chans // 2, chans))

    def couple(row):
        factors = factors_of(radius(row))
        for some in cuts:
            total = summed(factors, weights.at[1], xg.at[row], some)
            acc[row, some, :] = acc[row, some, :] + total.astype(jnp.float32)

    def couple_parts(kind, pair):
        place = lax.broadcasted_iota(jnp.int32, (1, lanes), 1) // width
        place = place + (rad_at * rows + whole + 2 * pair)
        factors = factors_of(1.0 + 8.0 * place.astype(jnp.float32) / width)
        target = kind * chip + (1 - kind) * back
        for some in cuts:
            total = summed(factors, weights.at[kind], xp.at[chip, pair], some)
            coupled[target, pair, some, :] = total

    def take_parts(unit):
        @pl.when(unit == 0)
        def _():
            relay_part(peer + 1 - 2 * core).wait_recv()

        @pl.when(unit == PAIRS)
        def _():
            back_copy(chip).start()

        couple_parts(unit // PAIRS, unit % PAIRS)

    def relay(base):
        row = base + core

        @pl.when(jnp.logical_and(row >= lead, row < whole))
        def _():
            chip_copy(row, peer).wait_recv()
            relay_copy(row, peer).start()

    def take_row(row):
        @pl.when(row >= lead)
        def _():
            relay_copy(row, peer + 1 - 2 * core).wait_recv()

        couple(row)

    def take_side(group):
        @pl.when(has_behind)
        def _():
            far_copy(every, cut_of(group), group).wait_recv()
            side_group(group)

        @pl.when(jnp.logical_not(has_behind))
        def _():
            mix_slot(near_slot, cut_of(group))

    def mix_slot(slot, cut):
        value = halo[slot, :, cut, :].reshape(size, lanes)
        total = mix(2 * slot, value).reshape(rows, GROUP, lanes)
        acc[:, cut, :] = acc[:, cut, :] + total

    def each_of(first, last, work):
        def step(index, carry):
            work(index)
            return carry

        lax.fori_loop(first, last, step, 0)

    def merge(first, last, some_rows):
        def one(group):
            for row in some_rows:
                lay_out(early, group, row, acc[row, cut_of(group), :])

        each_of(first, last, one)

    def take_lead(turn):
        @pl.when(core == turn)
        def _():
            lead_copy(block(peer)).wait_recv()
            relay_lead(peer).start()

    forward(0, 0)
    each_of(0, 3, own_group)
    forward(0, 1)
    each_of(3, 4, own_group)
    for half in range(2):
        forward(1, half)
        each_of(4 + 4 * half, 8 + 4 * half, own_group)
    for half in range(2):
        forward(2, half)
        take_lead(1 - half)
        each_of(6 * half, 6 + 6 * half, local_row)
    pltpu.make_async_copy(weights, weights, small_sem.at[2]).wait()
    core_copy(slice(0, whole + PAIRS), partner).wait_recv()
    each_of(12, rows - 1, local_row)

    def pass_via(some_rows):
        via_copy(some_rows).wait_recv()
        via_forward(some_rows).start()

    by_core(has_ahead, pass_via)

    def main(index, carry):
        start = index * lead - 1

        def each(first, second):
            return (1 - core) * first + core * second

        def when(condition, work, *args):
            @pl.when(condition)
            def _():
                work(*args)

        even, odd = (core == 0, core == 1)
        started, ended = (index == 1, index == 3)
        forward(3 * index, 0)

        @pl.when(started)
        def _():
            local_row(rows - 1)
            relay_lead(peer + 1 - 2 * core).wait_recv()

        when(jnp.logical_or(odd, started), take_row, each(0, start - 2))
        when(jnp.logical_and(even, index > 1), take_parts, 2 * index - 4)
        relay(start - 1)
        forward(3 * index, 1)
        take_side(3 * index - 2)
        when(jnp.logical_or(even, started), take_row, each(start - 1, 0))
        when(jnp.logical_and(odd, index > 1), take_parts, 2 * index - 3)
        forward(3 * index + 1, 0)
        relay(start)

        @pl.when(started)
        def _():
            part_copy(chip, peer).wait_recv()
            relay_part(peer).start()

        take_row(start - core)
        when(started, take_side, 0)
        when(ended, merge, 0, groups - 4, range(rows // 2))
        forward(3 * index + 1, 1)
        when(jnp.logical_or(odd, started), take_row, each(1, start))
        when(jnp.logical_and(even, index > 1), take_parts, 2 * index - 3)
        take_side(3 * index - 1)
        relay(start + 1)
        when(index < 3, forward, 3 * index + 2, 0)
        when(jnp.logical_and(even, index < 3), take_row, start + 1)
        when(jnp.logical_and(odd, index < 3), take_parts, 2 * index - 2)
        when(ended, merge, 0, groups - 4, range(rows // 2, whole))
        when(index < 3, forward, 3 * index + 2, 1)
        relay(start + 2)
        take_side(3 * index)
        when(index < 3, take_row, start + 2 - core)
        return carry

    lax.fori_loop(1, 4, main, 0)

    merge(groups - 4, groups - TAIL, range(whole))
    back_copy(1 - chip).wait_recv()
    for place in range(rows - whole):
        pair, turn = divmod(place, 2)
        for part in range(2):
            lane = slice(part * width, (part + 1) * width)
            value = coupled[part, pair, :, turn * width : (turn + 1) * width]
            acc[whole + place, :, lane] = acc[whole + place, :, lane] + value.astype(jnp.float32)
    merge(0, groups - TAIL, range(whole, rows))
    for half in range(2):
        forward(groups - 1, half)
    for group in range(groups - TAIL, groups):
        mix_slot(near_slot, cut_of(group))

    @pl.when(has_behind)
    def _():
        tail_copy(every, groups - 2).wait_recv()

    @pl.when(jnp.logical_and(core == 1, has_behind))
    def _():
        tail_copy(half_of(0), groups - 1).wait_recv()

    by_core(has_behind, lambda some_rows: via_forward(some_rows).wait_recv())

    def sent(owners, some_rows, sem):
        view = xg.at[some_rows, 0 : owners * chans, :]
        remote(view, view, sem, fl, {"chan": partner}).wait_send()

    sent(peers, slice(0, rows - 1), xs)

    @pl.when(has_ahead)
    def _():
        sent(1, every, zs)

    by_core(has_behind, lambda some_rows: via_copy(some_rows).wait_send())


def device_step(peers, rads, psi, k_prev, gaunt, dipole, kinetic, chan_l, field_amp):
    _, chans, rows, width = psi.shape
    fits = (
        chans == 3 * 4 * GROUP
        and rows == GROUP
        and peers == 4
        and rads % 2 == 0
        and width == rads * rows
        and width == 128
    )
    if not fits:
        return on_device(psi, k_prev, gaunt, dipole, kinetic, chan_l, field_amp)
    orders = gaunt.shape[0] + 1
    chips = peers // 2
    groups = chans // GROUP
    lanes = 2 * width
    size = rows * GROUP
    f32, bf16, dma = (jnp.float32, jnp.bfloat16, pltpu.SemaphoreType.DMA)
    main_memory = pl.BlockSpec(memory_space=pltpu.HBM)
    vmem = pl.BlockSpec(memory_space=pltpu.VMEM)
    summed = jax.ShapeDtypeStruct((rows, chans, lanes), f32)
    early = jax.ShapeDtypeStruct(psi.shape, f32)
    far_tail = jax.ShapeDtypeStruct((rows, TAIL * GROUP, lanes), bf16)
    mixing = jax.ShapeDtypeStruct((3, 2 * size, size), bf16)
    psi, k_prev, gaunt, dipole, kinetic, chan_l = (
        pltpu.with_memory_space_constraint(value, pltpu.HBM)
        for value in (psi, k_prev, gaunt, dipole, kinetic, chan_l.T)
    )
    parts = pl.pallas_call(
        functools.partial(fused_kernel, peers, rads),
        out_shape=(summed, early, far_tail, mixing),
        in_specs=[main_memory] * 6 + [pl.BlockSpec(memory_space=pltpu.SMEM)],
        out_specs=(vmem,) * 4,
        scratch_shapes=[
            pltpu.VMEM(kinetic.shape, f32),
            pltpu.VMEM((2, chans), jnp.int32),
            pltpu.VMEM((2, 2, chans, rows, width), f32),
            pltpu.VMEM((rows, chans, lanes), f32),
            pltpu.VMEM((rows, peers * chans, lanes), bf16),
            pltpu.VMEM((2, PAIRS, peers * chans, lanes), bf16),
            pltpu.VMEM((3, PAIRS, chans, lanes), bf16),
            pltpu.VMEM((2, rows, chans, lanes), bf16),
            pltpu.VMEM((2, orders, chans, peers * chans), bf16),
            pltpu.VMEM((lanes, lanes), bf16),
            pltpu.VMEM((chans, width), f32),
            pltpu.VMEM((chans, width), f32),
            dma((len(LOADS),)),
            dma((3,)),
            dma,
            dma,
            dma((rows - rows // 4 - 2 * PAIRS + 2,)),
            dma,
            dma,
            dma((rows - rows // 4 - 2 * PAIRS + 1,)),
            dma((2, groups)),
            dma,
            dma((groups,)),
            dma,
            dma((2,)),
            pltpu.VMEM((rows, GROUP, lanes), bf16),
        ],
        compiler_params=pltpu.CompilerParams(
            collective_id=0, has_side_effects=True, vmem_limit_bytes=36 * 1024 * 1024
        ),
    )(psi, k_prev, gaunt, dipole, kinetic, chan_l, field_amp)
    return pl.pallas_call(
        functools.partial(finish_kernel, rads),
        out_shape=jax.ShapeDtypeStruct(psi.shape, f32),
        in_specs=[vmem] * 4,
        out_specs=main_memory,
        scratch_shapes=[pltpu.VMEM((2, TAIL * GROUP, rows, width), f32), dma],
        compiler_params=pltpu.CompilerParams(vmem_limit_bytes=8 * 1024 * 1024),
    )(*parts)


def solution(mesh):
    placed = (
        P(None, "chan", "rad", None),
        P(None, "chan", "rad", None),
        P(),
        P(),
        P(),
        P("chan", None),
        P(),
    )
    return jax.shard_map(
        functools.partial(device_step, mesh.shape["chan"], mesh.shape["rad"]),
        mesh=mesh,
        in_specs=placed,
        out_specs=P(None, "chan", "rad", None),
        check_vma=False,
    )
```

```python
import functools

import jax
import jax.numpy as jnp
from jax import lax
from jax.experimental import pallas as pl
from jax.experimental.pallas import tpu as pltpu
from jax.sharding import PartitionSpec as P


def extended(array, sides, width):
    for axis, dim in sides:
        peers, length = (lax.axis_size(axis), array.shape[dim])
        up = [(i, (i + 1) % peers) for i in range(peers - 1)]
        down = [(j, i) for i, j in up]
        last = lax.slice_in_dim(array, length - width, length, axis=dim)
        initial = lax.slice_in_dim(array, 0, width, axis=dim)
        before = lax.ppermute(last, axis, up)
        after = lax.ppermute(initial, axis, down)
        array = jnp.concatenate([before, array, after], axis=dim)
    return array


def on_device(psi, k_prev, gaunt, dipole, kinetic, chan_l, field_amp):
    highest = lax.Precision.HIGHEST
    section = psi + 0.5 * k_prev
    local_chan = section.shape[1]
    rows = section.shape[2]
    width = section.shape[3]
    rad_at = lax.axis_index("rad")
    first_r = (
        1.0 + 8.0 * (rad_at * rows + jnp.arange(rows, dtype=jnp.int32)).astype(jnp.float32) / width
    )
    second_r = 1.0 + 8.0 * jnp.arange(width, dtype=jnp.float32) / width
    along_r2 = jnp.einsum("acij,kj->acik", section, kinetic, precision=highest)
    padded = extended(section.astype(jnp.bfloat16), (("rad", 2),), rows).astype(section.dtype)
    band = lax.dynamic_slice_in_dim(kinetic, rad_at * rows, rows, 0)
    widened = jnp.pad(band, ((0, 0), (rows, rows)))
    local_band = lax.dynamic_slice_in_dim(widened, rad_at * rows, 3 * rows, 1)
    along_r1 = jnp.einsum("ij,acjk->acik", local_band, padded, precision=highest)
    lvals = chan_l.astype(jnp.float32)
    first_l = lvals[:, 0] * (lvals[:, 0] + 1.0)
    second_l = lvals[:, 1] * (lvals[:, 1] + 1.0)
    potential = (
        first_l[:, None, None] / (2.0 * first_r * first_r)[None, :, None]
        + second_l[:, None, None] / (2.0 * second_r * second_r)[None, None, :]
        - 2.0 / first_r[None, :, None]
        - 2.0 / second_r[None, None, :]
    )
    sent = section.astype(jnp.bfloat16).reshape(2, local_chan, rows * width)
    chan_at = lax.axis_index("chan")
    block = lax.all_to_all(sent, "chan", split_axis=2, concat_axis=1, tiled=True)
    count = block.shape[2]
    place = chan_at * count + jnp.arange(count, dtype=jnp.int32)
    row_r = 1.0 + 8.0 * (rad_at * rows + place // width).astype(jnp.float32) / width
    col_r = 1.0 + 8.0 * (place % width).astype(jnp.float32) / width
    far = jnp.maximum(row_r, col_r)
    near = jnp.minimum(row_r, col_r)
    inverse = 1.0 / far
    ratio = near * inverse
    power = inverse
    total = jnp.zeros(block.shape, jnp.float32)
    for order in range(gaunt.shape[0]):
        mixed = jnp.einsum("cd,adq->acq", gaunt[order], block, preferred_element_type=jnp.float32)
        total = total + power[None, None, :] * mixed
        power = power * ratio
    mixed = jnp.einsum("cd,adq->acq", dipole, block, preferred_element_type=jnp.float32)
    total = total + (field_amp[0] * (row_r + col_r))[None, None, :] * mixed
    coupled = lax.all_to_all(
        total.astype(jnp.bfloat16), "chan", split_axis=1, concat_axis=2, tiled=True
    )
    coupled = coupled.reshape(coupled.shape[0], local_chan, rows, width)
    ham = along_r1 + along_r2 + potential[None] * section + coupled.astype(jnp.float32)
    return jnp.stack([ham[1], -ham[0]])


MESH = pl.DeviceIdType.MESH
GROUP = 16
PAIRS = 2
TAIL = 2
LOADS = ((0, 1), (1, 4), (4, 12))


def split_bf16(value):
    high = value.astype(jnp.bfloat16)
    return high, (value - high.astype(jnp.float32)).astype(jnp.bfloat16)


def lay_out(target, group, row, value):
    _, chans, height, width = target.shape
    start = group * GROUP * height + row % height
    place = (pl.ds(start, GROUP, stride=height), slice(None))
    target.at[0].reshape(chans * height, width)[place] = value[:, width:]
    target.at[1].reshape(chans * height, width)[place] = -value[:, :width]


def finish_kernel(rads, acc, early, far_tail, wr1, out, lower, late, sem):
    rows, chans, lanes = acc.shape
    size = rows * GROUP
    done = chans - TAIL * GROUP
    rad_at = lax.axis_index("rad")
    minor = rad_at % 2
    behind = rad_at - 2 + 4 * minor
    has_behind = jnp.logical_and(behind >= 0, behind < rads)
    half = rows // 2
    pltpu.make_async_copy(early.at[:, 0:done], out.at[:, 0:done, 0:half, :], sem).start()
    for first in range(0, done, 2 * GROUP):
        for group in range(first // GROUP, first // GROUP + 2):
            for row in range(half, rows):
                value = acc[row, group * GROUP : (group + 1) * GROUP, :]
                lay_out(lower, group, row, value)
        cut = slice(first, first + 2 * GROUP)
        pltpu.make_async_copy(lower.at[:, cut], out.at[:, cut, half:rows, :], sem).start()

    for group in range(TAIL):
        cut = slice(group * GROUP, (group + 1) * GROUP)
        there = slice(done + group * GROUP, done + (group + 1) * GROUP)

        @pl.when(has_behind)
        def _():
            value = far_tail[:, cut, :].reshape(size, lanes)
            both = jnp.dot(wr1[2 * minor], value, preferred_element_type=jnp.float32)
            total = (both[:size] + both[size:]).reshape(rows, GROUP, lanes)
            for row in range(rows):
                lay_out(late, group, row, acc[row, there, :] + total[row])

        @pl.when(jnp.logical_not(has_behind))
        def _():
            for row in range(rows):
                lay_out(late, group, row, acc[row, there, :])

        pltpu.make_async_copy(late.at[:, cut], out.at[:, there], sem).start()
    pltpu.make_async_copy(out, out, sem).wait()


def fused_kernel(
    peers,
    rads,
    psi,
    k_prev,
    gaunt,
    dipole,
    kin_main,
    chan_main,
    field,
    acc,
    early,
    far_tail,
    wr1,
    kin,
    chan_l,
    pk,
    sec,
    xg,
    xp,
    coupled,
    halo,
    weights,
    kk,
    lmul,
    langle,
    load_sem,
    small_sem,
    hr,
    xs,
    xr,
    cr,
    fl,
    fr,
    yr,
    zs,
    zr,
    vs,
    vr,
    via,
):
    rows, chans, lanes = sec.shape
    width = lanes // 2
    orders = weights.shape[1]
    chips = peers // 2
    groups = chans // GROUP
    lead = rows // 4
    chan_at = lax.axis_index("chan")
    rad_at = lax.axis_index("rad")
    core = chan_at % 2
    chip = chan_at // 2
    partner = chan_at + 1 - 2 * core
    minor = rad_at % 2
    other = rad_at + 1 - 2 * minor
    ahead = rad_at + 2 - 4 * minor
    behind = rad_at - 2 + 4 * minor
    has_ahead = jnp.logical_and(ahead >= 0, ahead < rads)
    has_behind = jnp.logical_and(behind >= 0, behind < rads)
    near_slot = 1 - minor
    far_slot = minor
    whole = rows - 2 * PAIRS
    back = 2
    peer = lax.rem(chip + 1, chips) * 2 + core

    def block(owner):
        return pl.ds(pl.multiple_of(owner * chans, GROUP), chans)

    def cut_of(group):
        return pl.ds(pl.multiple_of(group * GROUP, GROUP), GROUP)

    def block_cut(owner, group):
        return pl.ds(pl.multiple_of(owner * chans + group * GROUP, GROUP), GROUP)

    def chip_peer(step):
        return lax.rem(chip + step, chips) * 2 + core

    def chip_source(step):
        return lax.rem(chip - step + chips, chips) * 2 + core

    def load(which, part):
        first, last = LOADS[part]
        cut = slice(first * GROUP, last * GROUP)
        return pltpu.make_async_copy(
            (psi, k_prev)[which].at[:, cut, :, :], pk.at[which, :, cut, :, :], load_sem.at[part]
        )

    def arrive(part):
        first, last = LOADS[part]
        view = pk.at[:, :, first * GROUP : last * GROUP, :, :]
        pltpu.make_async_copy(view, view, load_sem.at[part]).wait()

    def load_weight(kind, order):
        source = gaunt.at[order] if order < orders - 1 else dipole
        owner = (peer, chan_at)[kind]
        return pltpu.make_async_copy(
            source.at[block(owner), :], weights.at[kind, order], small_sem.at[2]
        )

    def remote(source, target, send, recv, device):
        return pltpu.make_async_remote_copy(
            src_ref=source,
            dst_ref=target,
            send_sem=send,
            recv_sem=recv,
            device_id=device,
            device_id_type=MESH,
        )

    def lead_copy(some):
        view = xg.at[0:lead, some, :]
        return remote(view, view, xs, hr, {"chan": peer})

    def chip_copy(row, owner):
        view = xg.at[row, block(owner), :]
        return remote(view, view, xs, xr.at[row - lead], {"chan": peer})

    def part_copy(part, owner):
        view = xp.at[part, :, block(owner), :]
        return remote(view, view, xs, xr.at[whole - lead], {"chan": peer})

    def back_copy(part):
        source, target = (coupled.at[back], coupled.at[part])
        return remote(source, target, xs, xr.at[whole - lead + 1], {"chan": peer})

    def core_copy(some_rows, owner):
        view = xg.at[some_rows, block(owner), :]
        return remote(view, view, xs, cr, {"chan": partner})

    def core_part(owner):
        view = xp.at[chip, :, block(owner), :]
        return remote(view, view, xs, cr, {"chan": partner})

    def relay_lead(owner):
        view = xg.at[0:lead, block(owner), :]
        return remote(view, view, xs, fl, {"chan": partner})

    def relay_copy(row, owner):
        view = xg.at[row, block(owner), :]
        return remote(view, view, xs, fr.at[row - lead], {"chan": partner})

    def relay_part(owner):
        view = xp.at[chip, :, block(owner), :]
        return remote(view, view, xs, fr.at[whole - lead], {"chan": partner})

    def half_of(half):
        return slice(half * (rows // 2), (half + 1) * (rows // 2))

    def side_copy(group, half):
        source = xg.at[half_of(half), block_cut(chan_at, group), :]
        target = halo.at[minor, half_of(half), cut_of(group), :]
        return remote(source, target, xs, yr.at[half, group], {"rad": other})

    def far_copy(some_rows, some, place):
        source = halo.at[near_slot, some_rows, some, :]
        target = halo.at[minor, some_rows, some, :]
        return remote(source, target, zs, zr.at[place], {"rad": ahead})

    def tail_cut(group):
        return pl.ds(pl.multiple_of((group - groups + TAIL) * GROUP, GROUP), GROUP)

    def tail_copy(some_rows, group):
        source = halo.at[near_slot, some_rows, cut_of(group), :]
        target = far_tail.at[some_rows, tail_cut(group), :]
        return remote(source, target, zs, zr.at[group], {"rad": ahead})

    def via_copy(some_rows):
        source = xg.at[some_rows, block_cut(chan_at, groups - 1), :]
        return remote(source, via.at[some_rows], vs, vr.at[0], {"rad": behind})

    def via_forward(some_rows):
        target = far_tail.at[some_rows, tail_cut(groups - 1), :]
        return remote(via.at[some_rows], target, zs, vr.at[1], {"rad": other})

    def by_core(condition, work):
        for at, some_rows in enumerate((every, half_of(1))):

            @pl.when(jnp.logical_and(core == at, condition))
            def _():
                work(some_rows)

    every = slice(0, rows)
    small = [
        pltpu.make_async_copy(kin_main, kin, small_sem.at[0]),
        pltpu.make_async_copy(chan_main, chan_l, small_sem.at[1]),
    ]
    for part in range(len(LOADS)):
        for which in range(2):
            load(which, part).start()

    barrier = pltpu.get_barrier_semaphore()
    for step in range(1, chips):
        pl.semaphore_signal(
            barrier, inc=1, device_id={"chan": chip_peer(step)}, device_id_type=MESH
        )
    pl.semaphore_signal(barrier, inc=1, device_id={"chan": partner}, device_id_type=MESH)
    pl.semaphore_signal(barrier, inc=1, device_id={"rad": other}, device_id_type=MESH)

    @pl.when(has_ahead)
    def _():
        pl.semaphore_signal(barrier, inc=1, device_id={"rad": ahead}, device_id_type=MESH)

    @pl.when(has_behind)
    def _():
        pl.semaphore_signal(barrier, inc=1, device_id={"rad": behind}, device_id_type=MESH)

    def form(group):
        for part in range(2):
            first = pk.at[0, part].reshape(chans * rows, width)
            second = pk.at[1, part].reshape(chans * rows, width)
            cut = slice(part * width, (part + 1) * width)
            for row in range(rows):
                place = (pl.ds(group * GROUP * rows + row, GROUP, stride=rows), slice(None))
                value = first[place] + 0.5 * second[place]
                sec[row, cut_of(group), cut] = value
                rounded = value.astype(jnp.bfloat16)
                xg[row, block_cut(chan_at, group), cut] = rounded
                if row >= whole:
                    pair, turn = divmod(row - whole, 2)
                    lane = slice(turn * width, (turn + 1) * width)
                    xp[part, pair, block_cut(chan_at, group), lane] = rounded

    def send_group(group):
        for half in range(2):
            side_copy(group, half).start()
        lead_copy(block_cut(chan_at, group)).start()

    arrive(0)
    form(jnp.int32(0))
    pl.semaphore_wait(
        barrier, chips + 1 + has_ahead.astype(jnp.int32) + has_behind.astype(jnp.int32)
    )
    send_group(0)
    arrive(1)
    form(jnp.int32(1))

    def form_next(group, carry):
        form(group)
        send_group(group - 1)
        return carry

    lax.fori_loop(2, LOADS[1][1], form_next, 0)
    for part in range(2, len(LOADS)):
        arrive(part)
        lax.fori_loop(LOADS[part][0], LOADS[part][1], form_next, 0)
    for copy in small:
        copy.start()
    for order in range(orders):
        for kind in range(2):
            load_weight(kind, order).start()

    send_group(groups - 1)

    by_core(has_behind, lambda some_rows: via_copy(some_rows).start())

    part_copy(1 - chip, chan_at).start()
    for row in range(lead, whole):
        chip_copy(row, chan_at).start()
    for index in range(0, whole, lead):
        core_copy(slice(index, min(index + lead, whole)), chan_at).start()
    core_part(chan_at).start()

    def pass_on(group, half):
        side_copy(group, half).wait_recv()

        @pl.when(jnp.logical_and(has_ahead, group < groups - TAIL))
        def _():
            far_copy(half_of(half), cut_of(group), group).start()

        late = jnp.logical_and(group >= groups - TAIL, group < groups - 1 + core * (1 - half))

        @pl.when(jnp.logical_and(has_ahead, late))
        def _():
            tail_copy(half_of(half), group).start()

    def forward(group, half):
        @pl.when(group + core < groups)
        def _():
            pass_on(group + core, half)

    @pl.when(core == 1)
    def _():
        pass_on(0, 0)

    for copy in small:
        copy.wait()
    kin_high, kin_low = split_bf16(kin[...])
    both = jnp.concatenate([kin_high, kin_low], axis=1)
    kk[0:width, :] = both
    kk[width : 2 * width, :] = both

    band = kin[pl.ds(pl.multiple_of(rad_at * rows, rows), rows), :]
    size = rows * GROUP
    tall = jnp.broadcast_to(band[:, None, :], (rows, GROUP, width)).reshape(size, width)
    tall_high, tall_low = split_bf16(tall)
    at_row = lax.broadcasted_iota(jnp.int32, (size, size), 0)
    at_col = lax.broadcasted_iota(jnp.int32, (size, size), 1)
    same = (at_row % GROUP) == (at_col % GROUP)
    from_j = lax.broadcasted_iota(jnp.int32, (width, size), 0)
    to_col = lax.broadcasted_iota(jnp.int32, (width, size), 1)
    for side in range(3):
        pick = from_j == (rad_at + side - 1) * rows + to_col // GROUP
        pick = jnp.where(pick, 1.0, 0.0).astype(jnp.bfloat16)
        for level, source in enumerate((tall_high, tall_low)):
            wide = jnp.dot(source, pick, preferred_element_type=jnp.float32)
            wr1[side, level * size : (level + 1) * size, :] = jnp.where(same, wide, 0.0).astype(
                jnp.bfloat16
            )

    @pl.when(core == 1)
    def _():
        pass_on(0, 1)

    second_r = 1.0 + 8.0 * (
        lax.broadcasted_iota(jnp.int32, (1, lanes), 1) % width
    ).astype(jnp.float32) / width
    inner_r = second_r[:, :width]
    lvals = chan_l[...].astype(jnp.float32).astype(jnp.bfloat16)
    first = lax.broadcasted_iota(jnp.int32, (2, lanes), 0)
    spread = first == lax.broadcasted_iota(jnp.int32, (2, lanes), 1) // width
    spread = jnp.where(spread, 1.0, 0.0).astype(jnp.bfloat16)
    lwide = lax.dot_general(
        lvals, spread, (((0,), (0,)), ((), ())), preferred_element_type=jnp.float32
    )
    lwide = lwide * (lwide + 1.0)
    lmul[...] = lwide[:, :width]
    langle[...] = lwide[:, width:] / (2.0 * inner_r * inner_r) - 2.0 / inner_r

    def radius(row):
        place = jnp.full((1, lanes), rad_at * rows + row, jnp.int32)
        return 1.0 + 8.0 * place.astype(jnp.float32) / width

    def local_row(row):
        first_r = radius(row)[:, :width]
        scale = 1.0 / (2.0 * first_r * first_r)
        shift = 2.0 / first_r
        potential = lmul[...] * scale + langle[...] - shift
        for part in range(2):
            cut = slice(part * width, (part + 1) * width)
            value = sec[row, :, cut]
            high = xg[row, block(chan_at), cut]
            low = (value - high.astype(jnp.float32)).astype(jnp.bfloat16)
            both = jnp.dot(
                jnp.concatenate([high, low], axis=1), kk[...], preferred_element_type=jnp.float32
            )
            total = both[:, :width] + both[:, width:] + potential * value
            acc[row, :, cut] = acc[row, :, cut] + total

    def mix(side, value):
        both = jnp.dot(wr1[side], value, preferred_element_type=jnp.float32)
        return both[:size] + both[size:]

    def own_group(index):
        first = pl.multiple_of(index * GROUP, GROUP)
        start = pl.multiple_of(chan_at * chans + first, GROUP)
        high = xg[:, pl.ds(start, GROUP), :].reshape(size, lanes)
        value = sec[:, pl.ds(first, GROUP), :].reshape(size, lanes)
        low = (value - high.astype(jnp.float32)).astype(jnp.bfloat16)
        total = mix(1, high) + jnp.dot(
            wr1[1, 0:size, :], low, preferred_element_type=jnp.float32
        )
        acc[:, pl.ds(first, GROUP), :] = total.reshape(rows, GROUP, lanes)

    def side_group(index):
        first = pl.multiple_of(index * GROUP, GROUP)
        cut = pl.ds(first, GROUP)
        total = mix(0, halo[0, :, cut, :].reshape(size, lanes)) + mix(
            2, halo[1, :, cut, :].reshape(size, lanes)
        )
        acc[:, cut, :] = acc[:, cut, :] + total.reshape(rows, GROUP, lanes)

    def factors_of(first_r):
        inverse = 1.0 / jnp.maximum(first_r, second_r)
        ratio = jnp.minimum(first_r, second_r) * inverse
        factors = [inverse]
        for _ in range(orders - 2):
            factors.append(factors[-1] * ratio)
        factors.append(field[0] * (first_r + second_r))
        return factors

    def summed(factors, matrices, source, some):
        total = jnp.zeros((chans // 2, lanes), jnp.float32)
        for order in range(orders):
            total = total + factors[order] * jnp.dot(
                matrices[order, some, :], source[...], preferred_element_type=jnp.float32
            )
        return total.astype(jnp.bfloat16)

    cuts = (slice(0, chans // 2), slice(chans // 2, chans))

    def couple(row):
        factors = factors_of(radius(row))
        for some in cuts:
            total = summed(factors, weights.at[1], xg.at[row], some)
            acc[row, some, :] = acc[row, some, :] + total.astype(jnp.float32)

    def couple_parts(kind, pair):
        place = lax.broadcasted_iota(jnp.int32, (1, lanes), 1) // width
        place = place + (rad_at * rows + whole + 2 * pair)
        factors = factors_of(1.0 + 8.0 * place.astype(jnp.float32) / width)
        target = kind * chip + (1 - kind) * back
        for some in cuts:
            total = summed(factors, weights.at[kind], xp.at[chip, pair], some)
            coupled[target, pair, some, :] = total

    def take_parts(unit):
        @pl.when(unit == 0)
        def _():
            relay_part(peer + 1 - 2 * core).wait_recv()

        @pl.when(unit == 2 * PAIRS - 1)
        def _():
            back_copy(chip).start()

        couple_parts(unit // PAIRS, unit % PAIRS)

    def relay(base):
        row = base + core

        @pl.when(jnp.logical_and(row >= lead, row < whole))
        def _():
            chip_copy(row, peer).wait_recv()
            relay_copy(row, peer).start()

    def take_row(row):
        @pl.when(row >= lead)
        def _():
            relay_copy(row, peer + 1 - 2 * core).wait_recv()

        couple(row)

    def take_side(group):
        @pl.when(has_behind)
        def _():
            far_copy(every, cut_of(group), group).wait_recv()
            side_group(group)

        @pl.when(jnp.logical_not(has_behind))
        def _():
            mix_slot(near_slot, cut_of(group))

    def mix_slot(slot, cut):
        value = halo[slot, :, cut, :].reshape(size, lanes)
        total = mix(2 * slot, value).reshape(rows, GROUP, lanes)
        acc[:, cut, :] = acc[:, cut, :] + total

    def each_of(first, last, work):
        def step(index, carry):
            work(index)
            return carry

        lax.fori_loop(first, last, step, 0)

    def merge(first, last):
        def one(group):
            for row in range(rows // 2):
                lay_out(early, group, row, acc[row, cut_of(group), :])

        each_of(first, last, one)

    def take_lead(turn):
        @pl.when(core == turn)
        def _():
            lead_copy(block(peer)).wait_recv()
            relay_lead(peer).start()

    forward(0, 0)
    each_of(0, 3, own_group)
    forward(0, 1)
    each_of(3, 4, own_group)
    for half in range(2):
        forward(1, half)
        each_of(4 + 4 * half, 8 + 4 * half, own_group)
    for half in range(2):
        forward(2, half)
        take_lead(1 - half)
        each_of(6 * half, 6 + 6 * half, local_row)
    pltpu.make_async_copy(weights, weights, small_sem.at[2]).wait()
    core_copy(slice(0, whole + PAIRS), partner).wait_recv()
    each_of(12, rows - 1, local_row)

    def pass_via(some_rows):
        via_copy(some_rows).wait_recv()
        via_forward(some_rows).start()

    by_core(has_ahead, pass_via)

    def main(index, carry):
        start = index * lead - 1

        def each(first, second):
            return (1 - core) * first + core * second

        def when(condition, work, *args):
            @pl.when(condition)
            def _():
                work(*args)

        even, odd = (core == 0, core == 1)
        started, ended = (index == 1, index == 3)
        forward(3 * index, 0)

        @pl.when(started)
        def _():
            local_row(rows - 1)
            relay_lead(peer + 1 - 2 * core).wait_recv()

        when(jnp.logical_or(odd, started), take_row, each(0, start - 2))
        when(jnp.logical_and(even, index > 1), take_parts, 3 * index - 6)
        relay(start - 1)
        forward(3 * index, 1)
        take_side(3 * index - 2)
        when(jnp.logical_or(even, started), take_row, each(start - 1, 0))
        when(jnp.logical_and(odd, index > 1), take_parts, 2 * index - 3)
        forward(3 * index + 1, 0)
        relay(start)

        @pl.when(started)
        def _():
            part_copy(chip, peer).wait_recv()
            relay_part(peer).start()

        take_row(start - core)
        when(started, take_side, 0)
        when(jnp.logical_and(even, index == 2), take_parts, 1)
        when(ended, merge, 0, groups - 4)
        forward(3 * index + 1, 1)
        when(jnp.logical_or(odd, started), take_row, each(1, start))
        when(jnp.logical_and(even, index == 2), take_parts, 2)
        take_side(3 * index - 1)
        relay(start + 1)
        when(index < 3, forward, 3 * index + 2, 0)
        when(jnp.logical_and(even, index < 3), take_row, start + 1)
        when(jnp.logical_and(odd, index < 3), take_parts, 2 * index - 2)
        when(index < 3, forward, 3 * index + 2, 1)
        relay(start + 2)
        take_side(3 * index)
        when(index < 3, take_row, start + 2 - core)
        return carry

    lax.fori_loop(1, 4, main, 0)

    def take_back():
        back_copy(1 - chip).wait_recv()
        for place in range(rows - whole):
            pair, turn = divmod(place, 2)
            for part in range(2):
                lane = slice(part * width, (part + 1) * width)
                value = coupled[part, pair, :, turn * width : (turn + 1) * width]
                acc[whole + place, :, lane] = acc[whole + place, :, lane] + value.astype(
                    jnp.float32
                )

    merge(groups - 4, groups - TAIL)
    for group in range(groups - TAIL, groups):
        if group == groups - 1:
            for half in range(2):
                forward(group, half)
        mix_slot(near_slot, cut_of(group))
    take_back()

    @pl.when(has_behind)
    def _():
        tail_copy(every, groups - 2).wait_recv()

    @pl.when(jnp.logical_and(core == 1, has_behind))
    def _():
        tail_copy(half_of(0), groups - 1).wait_recv()

    by_core(has_behind, lambda some_rows: via_forward(some_rows).wait_recv())

    def sent(owners, some_rows, sem):
        view = xg.at[some_rows, 0 : owners * chans, :]
        remote(view, view, sem, fl, {"chan": partner}).wait_send()

    sent(peers, slice(0, rows - 1), xs)

    @pl.when(has_ahead)
    def _():
        sent(1, every, zs)

    by_core(has_behind, lambda some_rows: via_copy(some_rows).wait_send())


def device_step(peers, rads, psi, k_prev, gaunt, dipole, kinetic, chan_l, field_amp):
    _, chans, rows, width = psi.shape
    fits = (
        chans == 3 * 4 * GROUP
        and rows == GROUP
        and peers == 4
        and rads % 2 == 0
        and width == rads * rows
        and width == 128
    )
    if not fits:
        return on_device(psi, k_prev, gaunt, dipole, kinetic, chan_l, field_amp)
    orders = gaunt.shape[0] + 1
    chips = peers // 2
    groups = chans // GROUP
    lanes = 2 * width
    size = rows * GROUP
    f32, bf16, dma = (jnp.float32, jnp.bfloat16, pltpu.SemaphoreType.DMA)
    main_memory = pl.BlockSpec(memory_space=pltpu.HBM)
    vmem = pl.BlockSpec(memory_space=pltpu.VMEM)
    summed = jax.ShapeDtypeStruct((rows, chans, lanes), f32)
    early = jax.ShapeDtypeStruct((2, chans, rows // 2, width), f32)
    far_tail = jax.ShapeDtypeStruct((rows, TAIL * GROUP, lanes), bf16)
    mixing = jax.ShapeDtypeStruct((3, 2 * size, size), bf16)
    psi, k_prev, gaunt, dipole, kinetic, chan_l = (
        pltpu.with_memory_space_constraint(value, pltpu.HBM)
        for value in (psi, k_prev, gaunt, dipole, kinetic, chan_l.T)
    )
    parts = pl.pallas_call(
        functools.partial(fused_kernel, peers, rads),
        out_shape=(summed, early, far_tail, mixing),
        in_specs=[main_memory] * 6 + [pl.BlockSpec(memory_space=pltpu.SMEM)],
        out_specs=(vmem,) * 4,
        scratch_shapes=[
            pltpu.VMEM(kinetic.shape, f32),
            pltpu.VMEM((2, chans), jnp.int32),
            pltpu.VMEM((2, 2, chans, rows, width), f32),
            pltpu.VMEM((rows, chans, lanes), f32),
            pltpu.VMEM((rows, peers * chans, lanes), bf16),
            pltpu.VMEM((2, PAIRS, peers * chans, lanes), bf16),
            pltpu.VMEM((3, PAIRS, chans, lanes), bf16),
            pltpu.VMEM((2, rows, chans, lanes), bf16),
            pltpu.VMEM((2, orders, chans, peers * chans), bf16),
            pltpu.VMEM((lanes, lanes), bf16),
            pltpu.VMEM((chans, width), f32),
            pltpu.VMEM((chans, width), f32),
            dma((len(LOADS),)),
            dma((3,)),
            dma,
            dma,
            dma((rows - rows // 4 - 2 * PAIRS + 2,)),
            dma,
            dma,
            dma((rows - rows // 4 - 2 * PAIRS + 1,)),
            dma((2, groups)),
            dma,
            dma((groups,)),
            dma,
            dma((2,)),
            pltpu.VMEM((rows, GROUP, lanes), bf16),
        ],
        compiler_params=pltpu.CompilerParams(
            collective_id=0, has_side_effects=True, vmem_limit_bytes=36 * 1024 * 1024
        ),
    )(psi, k_prev, gaunt, dipole, kinetic, chan_l, field_amp)
    return pl.pallas_call(
        functools.partial(finish_kernel, rads),
        out_shape=jax.ShapeDtypeStruct(psi.shape, f32),
        in_specs=[vmem] * 4,
        out_specs=main_memory,
        scratch_shapes=[
            pltpu.VMEM((2, chans - TAIL * GROUP, rows // 2, width), f32),
            pltpu.VMEM((2, TAIL * GROUP, rows, width), f32),
            dma,
        ],
        compiler_params=pltpu.CompilerParams(vmem_limit_bytes=8 * 1024 * 1024),
    )(*parts)


def solution(mesh):
    placed = (
        P(None, "chan", "rad", None),
        P(None, "chan", "rad", None),
        P(),
        P(),
        P(),
        P("chan", None),
        P(),
    )
    return jax.shard_map(
        functools.partial(device_step, mesh.shape["chan"], mesh.shape["rad"]),
        mesh=mesh,
        in_specs=placed,
        out_specs=P(None, "chan", "rad", None),
        check_vma=False,
    )
```

```python
import functools

import jax
import jax.numpy as jnp
from jax import lax
from jax.experimental import pallas as pl
from jax.experimental.pallas import tpu as pltpu
from jax.sharding import PartitionSpec as P


def extended(array, sides, width):
    for axis, dim in sides:
        peers, length = (lax.axis_size(axis), array.shape[dim])
        up = [(i, (i + 1) % peers) for i in range(peers - 1)]
        down = [(j, i) for i, j in up]
        last = lax.slice_in_dim(array, length - width, length, axis=dim)
        initial = lax.slice_in_dim(array, 0, width, axis=dim)
        before = lax.ppermute(last, axis, up)
        after = lax.ppermute(initial, axis, down)
        array = jnp.concatenate([before, array, after], axis=dim)
    return array


def on_device(psi, k_prev, gaunt, dipole, kinetic, chan_l, field_amp):
    highest = lax.Precision.HIGHEST
    section = psi + 0.5 * k_prev
    local_chan = section.shape[1]
    rows = section.shape[2]
    width = section.shape[3]
    rad_at = lax.axis_index("rad")
    first_r = (
        1.0 + 8.0 * (rad_at * rows + jnp.arange(rows, dtype=jnp.int32)).astype(jnp.float32) / width
    )
    second_r = 1.0 + 8.0 * jnp.arange(width, dtype=jnp.float32) / width
    along_r2 = jnp.einsum("acij,kj->acik", section, kinetic, precision=highest)
    padded = extended(section.astype(jnp.bfloat16), (("rad", 2),), rows).astype(section.dtype)
    band = lax.dynamic_slice_in_dim(kinetic, rad_at * rows, rows, 0)
    widened = jnp.pad(band, ((0, 0), (rows, rows)))
    local_band = lax.dynamic_slice_in_dim(widened, rad_at * rows, 3 * rows, 1)
    along_r1 = jnp.einsum("ij,acjk->acik", local_band, padded, precision=highest)
    lvals = chan_l.astype(jnp.float32)
    first_l = lvals[:, 0] * (lvals[:, 0] + 1.0)
    second_l = lvals[:, 1] * (lvals[:, 1] + 1.0)
    potential = (
        first_l[:, None, None] / (2.0 * first_r * first_r)[None, :, None]
        + second_l[:, None, None] / (2.0 * second_r * second_r)[None, None, :]
        - 2.0 / first_r[None, :, None]
        - 2.0 / second_r[None, None, :]
    )
    sent = section.astype(jnp.bfloat16).reshape(2, local_chan, rows * width)
    chan_at = lax.axis_index("chan")
    block = lax.all_to_all(sent, "chan", split_axis=2, concat_axis=1, tiled=True)
    count = block.shape[2]
    place = chan_at * count + jnp.arange(count, dtype=jnp.int32)
    row_r = 1.0 + 8.0 * (rad_at * rows + place // width).astype(jnp.float32) / width
    col_r = 1.0 + 8.0 * (place % width).astype(jnp.float32) / width
    far = jnp.maximum(row_r, col_r)
    near = jnp.minimum(row_r, col_r)
    inverse = 1.0 / far
    ratio = near * inverse
    power = inverse
    total = jnp.zeros(block.shape, jnp.float32)
    for order in range(gaunt.shape[0]):
        mixed = jnp.einsum("cd,adq->acq", gaunt[order], block, preferred_element_type=jnp.float32)
        total = total + power[None, None, :] * mixed
        power = power * ratio
    mixed = jnp.einsum("cd,adq->acq", dipole, block, preferred_element_type=jnp.float32)
    total = total + (field_amp[0] * (row_r + col_r))[None, None, :] * mixed
    coupled = lax.all_to_all(
        total.astype(jnp.bfloat16), "chan", split_axis=1, concat_axis=2, tiled=True
    )
    coupled = coupled.reshape(coupled.shape[0], local_chan, rows, width)
    ham = along_r1 + along_r2 + potential[None] * section + coupled.astype(jnp.float32)
    return jnp.stack([ham[1], -ham[0]])


MESH = pl.DeviceIdType.MESH
GROUP = 16
PAIRS = 2
TAIL = 2
LOADS = ((0, 1), (1, 3), (3, 6), (6, 9), (9, 12))


def split_bf16(value):
    high = value.astype(jnp.bfloat16)
    return high, (value - high.astype(jnp.float32)).astype(jnp.bfloat16)


def lay_out(target, group, row, value):
    _, chans, height, width = target.shape
    start = group * GROUP * height + row % height
    place = (pl.ds(start, GROUP, stride=height), slice(None))
    target.at[0].reshape(chans * height, width)[place] = value[:, width:]
    target.at[1].reshape(chans * height, width)[place] = -value[:, :width]


def finish_kernel(rads, acc, early, far_tail, wr1, out, lower, late, sem):
    rows, chans, lanes = acc.shape
    size = rows * GROUP
    done = chans - TAIL * GROUP
    rad_at = lax.axis_index("rad")
    minor = rad_at % 2
    behind = rad_at - 2 + 4 * minor
    has_behind = jnp.logical_and(behind >= 0, behind < rads)
    half = rows // 2
    pltpu.make_async_copy(early.at[:, 0:done], out.at[:, 0:done, 0:half, :], sem).start()
    for first in range(0, done, 2 * GROUP):
        for group in range(first // GROUP, first // GROUP + 2):
            for row in range(half, rows):
                value = acc[row, group * GROUP : (group + 1) * GROUP, :]
                lay_out(lower, group, row, value)
        cut = slice(first, first + 2 * GROUP)
        pltpu.make_async_copy(lower.at[:, cut], out.at[:, cut, half:rows, :], sem).start()

    for group in range(TAIL):
        cut = slice(group * GROUP, (group + 1) * GROUP)
        there = slice(done + group * GROUP, done + (group + 1) * GROUP)

        @pl.when(has_behind)
        def _():
            value = far_tail[:, cut, :].reshape(size, lanes)
            both = jnp.dot(wr1[2 * minor], value, preferred_element_type=jnp.float32)
            total = (both[:size] + both[size:]).reshape(rows, GROUP, lanes)
            for row in range(rows):
                lay_out(late, group, row, acc[row, there, :] + total[row])

        @pl.when(jnp.logical_not(has_behind))
        def _():
            for row in range(rows):
                lay_out(late, group, row, acc[row, there, :])

        pltpu.make_async_copy(late.at[:, cut], out.at[:, there], sem).start()
    pltpu.make_async_copy(out, out, sem).wait()


def fused_kernel(
    peers,
    rads,
    psi,
    k_prev,
    gaunt,
    dipole,
    kin_main,
    chan_main,
    field,
    acc,
    early,
    far_tail,
    wr1,
    kin,
    chan_l,
    pk,
    sec,
    xg,
    xp,
    coupled,
    halo,
    weights,
    kk,
    lmul,
    langle,
    load_sem,
    small_sem,
    hr,
    xs,
    xr,
    cr,
    fl,
    fr,
    yr,
    zs,
    zr,
    vs,
    vr,
    via,
):
    rows, chans, lanes = sec.shape
    width = lanes // 2
    orders = weights.shape[1]
    chips = peers // 2
    groups = chans // GROUP
    lead = rows // 4
    chan_at = lax.axis_index("chan")
    rad_at = lax.axis_index("rad")
    core = chan_at % 2
    chip = chan_at // 2
    partner = chan_at + 1 - 2 * core
    minor = rad_at % 2
    other = rad_at + 1 - 2 * minor
    ahead = rad_at + 2 - 4 * minor
    behind = rad_at - 2 + 4 * minor
    has_ahead = jnp.logical_and(ahead >= 0, ahead < rads)
    has_behind = jnp.logical_and(behind >= 0, behind < rads)
    near_slot = 1 - minor
    far_slot = minor
    whole = rows - 2 * PAIRS
    back = 2
    peer = lax.rem(chip + 1, chips) * 2 + core

    def block(owner):
        return pl.ds(pl.multiple_of(owner * chans, GROUP), chans)

    def cut_of(group):
        return pl.ds(pl.multiple_of(group * GROUP, GROUP), GROUP)

    def block_cut(owner, group):
        return pl.ds(pl.multiple_of(owner * chans + group * GROUP, GROUP), GROUP)

    def chip_peer(step):
        return lax.rem(chip + step, chips) * 2 + core

    def chip_source(step):
        return lax.rem(chip - step + chips, chips) * 2 + core

    def load(which, part):
        first, last = LOADS[part]
        cut = slice(first * GROUP, last * GROUP)
        return pltpu.make_async_copy(
            (psi, k_prev)[which].at[:, cut, :, :], pk.at[which, :, cut, :, :], load_sem.at[part]
        )

    def arrive(part):
        first, last = LOADS[part]
        view = pk.at[:, :, first * GROUP : last * GROUP, :, :]
        pltpu.make_async_copy(view, view, load_sem.at[part]).wait()

    def load_weight(kind, order):
        source = gaunt.at[order] if order < orders - 1 else dipole
        owner = (peer, chan_at)[kind]
        return pltpu.make_async_copy(
            source.at[block(owner), :], weights.at[kind, order], small_sem.at[2]
        )

    def remote(source, target, send, recv, device):
        return pltpu.make_async_remote_copy(
            src_ref=source,
            dst_ref=target,
            send_sem=send,
            recv_sem=recv,
            device_id=device,
            device_id_type=MESH,
        )

    def lead_copy(some):
        view = xg.at[0:lead, some, :]
        return remote(view, view, xs, hr, {"chan": peer})

    def chip_copy(row, owner):
        view = xg.at[row, block(owner), :]
        return remote(view, view, xs, xr.at[row - lead], {"chan": peer})

    def part_copy(part, owner):
        view = xp.at[part, :, block(owner), :]
        return remote(view, view, xs, xr.at[whole - lead], {"chan": peer})

    def back_copy(part):
        source, target = (coupled.at[back], coupled.at[part])
        return remote(source, target, xs, xr.at[whole - lead + 1], {"chan": peer})

    def core_copy(some_rows, owner):
        view = xg.at[some_rows, block(owner), :]
        return remote(view, view, xs, cr, {"chan": partner})

    def core_part(owner):
        view = xp.at[chip, :, block(owner), :]
        return remote(view, view, xs, cr, {"chan": partner})

    def relay_lead(owner):
        view = xg.at[0:lead, block(owner), :]
        return remote(view, view, xs, fl, {"chan": partner})

    def relay_copy(row, owner):
        view = xg.at[row, block(owner), :]
        return remote(view, view, xs, fr.at[row - lead], {"chan": partner})

    def relay_part(owner):
        view = xp.at[chip, :, block(owner), :]
        return remote(view, view, xs, fr.at[whole - lead], {"chan": partner})

    def half_of(half):
        return slice(half * (rows // 2), (half + 1) * (rows // 2))

    def side_copy(group, half):
        source = xg.at[half_of(half), block_cut(chan_at, group), :]
        target = halo.at[minor, half_of(half), cut_of(group), :]
        return remote(source, target, xs, yr.at[half, group], {"rad": other})

    def far_copy(some_rows, some, place):
        source = halo.at[near_slot, some_rows, some, :]
        target = halo.at[minor, some_rows, some, :]
        return remote(source, target, zs, zr.at[place], {"rad": ahead})

    def tail_cut(group):
        return pl.ds(pl.multiple_of((group - groups + TAIL) * GROUP, GROUP), GROUP)

    def tail_copy(some_rows, group):
        source = halo.at[near_slot, some_rows, cut_of(group), :]
        target = far_tail.at[some_rows, tail_cut(group), :]
        return remote(source, target, zs, zr.at[group], {"rad": ahead})

    def via_copy(some_rows):
        source = xg.at[some_rows, block_cut(chan_at, groups - 1), :]
        return remote(source, via.at[some_rows], vs, vr.at[0], {"rad": behind})

    def via_forward(some_rows):
        target = far_tail.at[some_rows, tail_cut(groups - 1), :]
        return remote(via.at[some_rows], target, zs, vr.at[1], {"rad": other})

    def by_core(condition, work):
        for at, some_rows in enumerate((every, half_of(1))):

            @pl.when(jnp.logical_and(core == at, condition))
            def _():
                work(some_rows)

    every = slice(0, rows)
    small = [
        pltpu.make_async_copy(kin_main, kin, small_sem.at[0]),
        pltpu.make_async_copy(chan_main, chan_l, small_sem.at[1]),
    ]
    barrier = pltpu.get_barrier_semaphore()
    for step in range(1, chips):
        pl.semaphore_signal(
            barrier, inc=1, device_id={"chan": chip_peer(step)}, device_id_type=MESH
        )
    pl.semaphore_signal(barrier, inc=1, device_id={"chan": partner}, device_id_type=MESH)
    pl.semaphore_signal(barrier, inc=1, device_id={"rad": other}, device_id_type=MESH)

    @pl.when(has_ahead)
    def _():
        pl.semaphore_signal(barrier, inc=1, device_id={"rad": ahead}, device_id_type=MESH)

    @pl.when(has_behind)
    def _():
        pl.semaphore_signal(barrier, inc=1, device_id={"rad": behind}, device_id_type=MESH)

    for part in range(len(LOADS)):
        for which in range(2):
            load(which, part).start()

    def form(group):
        for part in range(2):
            first = pk.at[0, part].reshape(chans * rows, width)
            second = pk.at[1, part].reshape(chans * rows, width)
            cut = slice(part * width, (part + 1) * width)
            for row in range(rows):
                place = (pl.ds(group * GROUP * rows + row, GROUP, stride=rows), slice(None))
                value = first[place] + 0.5 * second[place]
                sec[row, cut_of(group), cut] = value
                rounded = value.astype(jnp.bfloat16)
                xg[row, block_cut(chan_at, group), cut] = rounded
                if row >= whole:
                    pair, turn = divmod(row - whole, 2)
                    lane = slice(turn * width, (turn + 1) * width)
                    xp[part, pair, block_cut(chan_at, group), lane] = rounded

    def send_group(group):
        for half in range(2):
            side_copy(group, half).start()
        lead_copy(block_cut(chan_at, group)).start()

    arrive(0)
    form(jnp.int32(0))
    pl.semaphore_wait(
        barrier, chips + 1 + has_ahead.astype(jnp.int32) + has_behind.astype(jnp.int32)
    )
    send_group(0)
    arrive(1)
    form(jnp.int32(1))

    def form_next(group, carry):
        form(group)
        send_group(group - 1)
        return carry

    lax.fori_loop(2, LOADS[1][1], form_next, 0)
    for part in range(2, len(LOADS)):
        arrive(part)
        lax.fori_loop(LOADS[part][0], LOADS[part][1], form_next, 0)
    for copy in small:
        copy.start()
    for order in range(orders):
        for kind in range(2):
            load_weight(kind, order).start()

    send_group(groups - 1)

    by_core(has_behind, lambda some_rows: via_copy(some_rows).start())

    part_copy(1 - chip, chan_at).start()
    for row in range(lead, whole):
        chip_copy(row, chan_at).start()
    for index in range(0, whole, lead):
        core_copy(slice(index, min(index + lead, whole)), chan_at).start()
    core_part(chan_at).start()

    def pass_on(group, half):
        side_copy(group, half).wait_recv()

        @pl.when(jnp.logical_and(has_ahead, group < groups - TAIL))
        def _():
            far_copy(half_of(half), cut_of(group), group).start()

        late = jnp.logical_and(group >= groups - TAIL, group < groups - 1 + core * (1 - half))

        @pl.when(jnp.logical_and(has_ahead, late))
        def _():
            tail_copy(half_of(half), group).start()

    def forward(group, half):
        @pl.when(group + core < groups)
        def _():
            pass_on(group + core, half)

    @pl.when(core == 1)
    def _():
        pass_on(0, 0)

    for copy in small:
        copy.wait()
    kin_high, kin_low = split_bf16(kin[...])
    both = jnp.concatenate([kin_high, kin_low], axis=1)
    kk[0:width, :] = both
    kk[width : 2 * width, :] = both

    band = kin[pl.ds(pl.multiple_of(rad_at * rows, rows), rows), :]
    size = rows * GROUP
    tall = jnp.broadcast_to(band[:, None, :], (rows, GROUP, width)).reshape(size, width)
    tall_high, tall_low = split_bf16(tall)
    at_row = lax.broadcasted_iota(jnp.int32, (size, size), 0)
    at_col = lax.broadcasted_iota(jnp.int32, (size, size), 1)
    same = (at_row % GROUP) == (at_col % GROUP)
    from_j = lax.broadcasted_iota(jnp.int32, (width, size), 0)
    to_col = lax.broadcasted_iota(jnp.int32, (width, size), 1)
    for side in range(3):
        pick = from_j == (rad_at + side - 1) * rows + to_col // GROUP
        pick = jnp.where(pick, 1.0, 0.0).astype(jnp.bfloat16)
        for level, source in enumerate((tall_high, tall_low)):
            wide = jnp.dot(source, pick, preferred_element_type=jnp.float32)
            wr1[side, level * size : (level + 1) * size, :] = jnp.where(same, wide, 0.0).astype(
                jnp.bfloat16
            )

    @pl.when(core == 0)
    def _():
        pass_on(0, 0)

    @pl.when(core == 1)
    def _():
        pass_on(0, 1)

    second_r = 1.0 + 8.0 * (
        lax.broadcasted_iota(jnp.int32, (1, lanes), 1) % width
    ).astype(jnp.float32) / width
    inner_r = second_r[:, :width]
    lvals = chan_l[...].astype(jnp.float32).astype(jnp.bfloat16)
    first = lax.broadcasted_iota(jnp.int32, (2, lanes), 0)
    spread = first == lax.broadcasted_iota(jnp.int32, (2, lanes), 1) // width
    spread = jnp.where(spread, 1.0, 0.0).astype(jnp.bfloat16)
    lwide = lax.dot_general(
        lvals, spread, (((0,), (0,)), ((), ())), preferred_element_type=jnp.float32
    )
    lwide = lwide * (lwide + 1.0)
    lmul[...] = lwide[:, :width]
    langle[...] = lwide[:, width:] / (2.0 * inner_r * inner_r) - 2.0 / inner_r

    def radius(row):
        place = jnp.full((1, lanes), rad_at * rows + row, jnp.int32)
        return 1.0 + 8.0 * place.astype(jnp.float32) / width

    def local_row(row):
        first_r = radius(row)[:, :width]
        scale = 1.0 / (2.0 * first_r * first_r)
        shift = 2.0 / first_r
        potential = lmul[...] * scale + langle[...] - shift
        for part in range(2):
            cut = slice(part * width, (part + 1) * width)
            value = sec[row, :, cut]
            high = xg[row, block(chan_at), cut]
            low = (value - high.astype(jnp.float32)).astype(jnp.bfloat16)
            both = jnp.dot(
                jnp.concatenate([high, low], axis=1), kk[...], preferred_element_type=jnp.float32
            )
            total = both[:, :width] + both[:, width:] + potential * value
            acc[row, :, cut] = acc[row, :, cut] + total

    def mix(side, value):
        both = jnp.dot(wr1[side], value, preferred_element_type=jnp.float32)
        return both[:size] + both[size:]

    def own_group(index):
        first = pl.multiple_of(index * GROUP, GROUP)
        start = pl.multiple_of(chan_at * chans + first, GROUP)
        high = xg[:, pl.ds(start, GROUP), :].reshape(size, lanes)
        value = sec[:, pl.ds(first, GROUP), :].reshape(size, lanes)
        low = (value - high.astype(jnp.float32)).astype(jnp.bfloat16)
        total = mix(1, high) + jnp.dot(
            wr1[1, 0:size, :], low, preferred_element_type=jnp.float32
        )
        acc[:, pl.ds(first, GROUP), :] = total.reshape(rows, GROUP, lanes)

    def side_group(index):
        first = pl.multiple_of(index * GROUP, GROUP)
        cut = pl.ds(first, GROUP)
        total = mix(0, halo[0, :, cut, :].reshape(size, lanes)) + mix(
            2, halo[1, :, cut, :].reshape(size, lanes)
        )
        acc[:, cut, :] = acc[:, cut, :] + total.reshape(rows, GROUP, lanes)

    def factors_of(first_r):
        inverse = 1.0 / jnp.maximum(first_r, second_r)
        ratio = jnp.minimum(first_r, second_r) * inverse
        factors = [inverse]
        for _ in range(orders - 2):
            factors.append(factors[-1] * ratio)
        factors.append(field[0] * (first_r + second_r))
        return factors

    def summed(factors, matrices, source, some):
        total = jnp.zeros((chans // 2, lanes), jnp.float32)
        for order in range(orders):
            total = total + factors[order] * jnp.dot(
                matrices[order, some, :], source[...], preferred_element_type=jnp.float32
            )
        return total.astype(jnp.bfloat16)

    cuts = (slice(0, chans // 2), slice(chans // 2, chans))

    def couple(row):
        factors = factors_of(radius(row))
        for some in cuts:
            total = summed(factors, weights.at[1], xg.at[row], some)
            acc[row, some, :] = acc[row, some, :] + total.astype(jnp.float32)

    def couple_parts(kind, pair):
        place = lax.broadcasted_iota(jnp.int32, (1, lanes), 1) // width
        place = place + (rad_at * rows + whole + 2 * pair)
        factors = factors_of(1.0 + 8.0 * place.astype(jnp.float32) / width)
        target = kind * chip + (1 - kind) * back
        for some in cuts:
            total = summed(factors, weights.at[kind], xp.at[chip, pair], some)
            coupled[target, pair, some, :] = total

    def take_parts(unit):
        @pl.when(unit == 0)
        def _():
            relay_part(peer + 1 - 2 * core).wait_recv()

        @pl.when(unit == 2 * PAIRS - 1)
        def _():
            back_copy(chip).start()

        couple_parts(unit // PAIRS, unit % PAIRS)

    def relay(base):
        row = base + core

        @pl.when(jnp.logical_and(row >= lead, row < whole))
        def _():
            chip_copy(row, peer).wait_recv()
            relay_copy(row, peer).start()

    def take_row(row):
        @pl.when(row >= lead)
        def _():
            relay_copy(row, peer + 1 - 2 * core).wait_recv()

        couple(row)

    def take_side(group):
        @pl.when(has_behind)
        def _():
            far_copy(every, cut_of(group), group).wait_recv()
            side_group(group)

        @pl.when(jnp.logical_not(has_behind))
        def _():
            mix_slot(near_slot, cut_of(group))

    def mix_slot(slot, cut):
        value = halo[slot, :, cut, :].reshape(size, lanes)
        total = mix(2 * slot, value).reshape(rows, GROUP, lanes)
        acc[:, cut, :] = acc[:, cut, :] + total

    def each_of(first, last, work):
        def step(index, carry):
            work(index)
            return carry

        lax.fori_loop(first, last, step, 0)

    def merge(first, last):
        def one(group):
            for row in range(rows // 2):
                lay_out(early, group, row, acc[row, cut_of(group), :])

        each_of(first, last, one)

    def take_lead(turn):
        @pl.when(core == turn)
        def _():
            lead_copy(block(peer)).wait_recv()
            relay_lead(peer).start()

    @pl.when(core == 1)
    def _():
        pass_on(1, 0)

    each_of(0, 3, own_group)
    forward(0, 1)
    each_of(3, 4, own_group)
    for half in range(2):
        forward(1, half)
        each_of(4 + 4 * half, 8 + 4 * half, own_group)
    for half in range(2):
        forward(2, half)
        take_lead(1 - half)
        each_of(6 * half, 6 + 6 * half, local_row)
    pltpu.make_async_copy(weights, weights, small_sem.at[2]).wait()
    core_copy(slice(0, whole + PAIRS), partner).wait_recv()
    each_of(12, rows - 1, local_row)

    def pass_via(some_rows):
        via_copy(some_rows).wait_recv()
        via_forward(some_rows).start()

    by_core(has_ahead, pass_via)

    def main(index, carry):
        start = index * lead - 1

        def each(first, second):
            return (1 - core) * first + core * second

        def when(condition, work, *args):
            @pl.when(condition)
            def _():
                work(*args)

        even, odd = (core == 0, core == 1)
        started, ended = (index == 1, index == 3)
        forward(3 * index, 0)

        @pl.when(started)
        def _():
            local_row(rows - 1)
            relay_lead(peer + 1 - 2 * core).wait_recv()

        when(jnp.logical_or(odd, started), take_row, each(0, start - 2))
        when(jnp.logical_and(even, index > 1), take_parts, 3 * index - 6)
        relay(start - 1)
        forward(3 * index, 1)
        take_side(3 * index - 2)
        when(jnp.logical_or(even, started), take_row, each(start - 1, 0))
        when(jnp.logical_and(odd, index > 1), take_parts, 2 * index - 3)
        forward(3 * index + 1, 0)
        relay(start)

        @pl.when(started)
        def _():
            part_copy(chip, peer).wait_recv()
            relay_part(peer).start()

        take_row(start - core)
        when(started, take_side, 0)
        when(jnp.logical_and(even, index == 2), take_parts, 1)
        when(ended, merge, 0, groups - 4)
        forward(3 * index + 1, 1)
        when(jnp.logical_or(odd, started), take_row, each(1, start))
        when(jnp.logical_and(even, index == 2), take_parts, 2)
        take_side(3 * index - 1)
        relay(start + 1)
        when(index < 3, forward, 3 * index + 2, 0)
        when(jnp.logical_and(even, index < 3), take_row, start + 1)
        when(jnp.logical_and(odd, index < 3), take_parts, 2 * index - 2)
        when(index < 3, forward, 3 * index + 2, 1)
        relay(start + 2)
        take_side(3 * index)
        when(index < 3, take_row, start + 2 - core)
        return carry

    lax.fori_loop(1, 4, main, 0)

    def take_back():
        back_copy(1 - chip).wait_recv()
        for place in range(rows - whole):
            pair, turn = divmod(place, 2)
            for part in range(2):
                lane = slice(part * width, (part + 1) * width)
                value = coupled[part, pair, :, turn * width : (turn + 1) * width]
                acc[whole + place, :, lane] = acc[whole + place, :, lane] + value.astype(
                    jnp.float32
                )

    merge(groups - 4, groups - TAIL)
    for group in range(groups - TAIL, groups):
        if group == groups - 1:
            for half in range(2):
                forward(group, half)
        mix_slot(near_slot, cut_of(group))
    take_back()

    @pl.when(has_behind)
    def _():
        tail_copy(every, groups - 2).wait_recv()

    @pl.when(jnp.logical_and(core == 1, has_behind))
    def _():
        tail_copy(half_of(0), groups - 1).wait_recv()

    by_core(has_behind, lambda some_rows: via_forward(some_rows).wait_recv())

    def sent(owners, some_rows, sem):
        view = xg.at[some_rows, 0 : owners * chans, :]
        remote(view, view, sem, fl, {"chan": partner}).wait_send()

    sent(peers, slice(0, rows - 1), xs)

    @pl.when(has_ahead)
    def _():
        sent(1, every, zs)

    by_core(has_behind, lambda some_rows: via_copy(some_rows).wait_send())


def device_step(peers, rads, psi, k_prev, gaunt, dipole, kinetic, chan_l, field_amp):
    _, chans, rows, width = psi.shape
    fits = (
        chans == 3 * 4 * GROUP
        and rows == GROUP
        and peers == 4
        and rads % 2 == 0
        and width == rads * rows
        and width == 128
    )
    if not fits:
        return on_device(psi, k_prev, gaunt, dipole, kinetic, chan_l, field_amp)
    orders = gaunt.shape[0] + 1
    chips = peers // 2
    groups = chans // GROUP
    lanes = 2 * width
    size = rows * GROUP
    f32, bf16, dma = (jnp.float32, jnp.bfloat16, pltpu.SemaphoreType.DMA)
    main_memory = pl.BlockSpec(memory_space=pltpu.HBM)
    vmem = pl.BlockSpec(memory_space=pltpu.VMEM)
    summed = jax.ShapeDtypeStruct((rows, chans, lanes), f32)
    early = jax.ShapeDtypeStruct((2, chans, rows // 2, width), f32)
    far_tail = jax.ShapeDtypeStruct((rows, TAIL * GROUP, lanes), bf16)
    mixing = jax.ShapeDtypeStruct((3, 2 * size, size), bf16)
    psi, k_prev, gaunt, dipole, kinetic, chan_l = (
        pltpu.with_memory_space_constraint(value, pltpu.HBM)
        for value in (psi, k_prev, gaunt, dipole, kinetic, chan_l.T)
    )
    parts = pl.pallas_call(
        functools.partial(fused_kernel, peers, rads),
        out_shape=(summed, early, far_tail, mixing),
        in_specs=[main_memory] * 6 + [pl.BlockSpec(memory_space=pltpu.SMEM)],
        out_specs=(vmem,) * 4,
        scratch_shapes=[
            pltpu.VMEM(kinetic.shape, f32),
            pltpu.VMEM((2, chans), jnp.int32),
            pltpu.VMEM((2, 2, chans, rows, width), f32),
            pltpu.VMEM((rows, chans, lanes), f32),
            pltpu.VMEM((rows, peers * chans, lanes), bf16),
            pltpu.VMEM((2, PAIRS, peers * chans, lanes), bf16),
            pltpu.VMEM((3, PAIRS, chans, lanes), bf16),
            pltpu.VMEM((2, rows, chans, lanes), bf16),
            pltpu.VMEM((2, orders, chans, peers * chans), bf16),
            pltpu.VMEM((lanes, lanes), bf16),
            pltpu.VMEM((chans, width), f32),
            pltpu.VMEM((chans, width), f32),
            dma((len(LOADS),)),
            dma((3,)),
            dma,
            dma,
            dma((rows - rows // 4 - 2 * PAIRS + 2,)),
            dma,
            dma,
            dma((rows - rows // 4 - 2 * PAIRS + 1,)),
            dma((2, groups)),
            dma,
            dma((groups,)),
            dma,
            dma((2,)),
            pltpu.VMEM((rows, GROUP, lanes), bf16),
        ],
        compiler_params=pltpu.CompilerParams(
            collective_id=0, has_side_effects=True, vmem_limit_bytes=36 * 1024 * 1024
        ),
    )(psi, k_prev, gaunt, dipole, kinetic, chan_l, field_amp)
    return pl.pallas_call(
        functools.partial(finish_kernel, rads),
        out_shape=jax.ShapeDtypeStruct(psi.shape, f32),
        in_specs=[vmem] * 4,
        out_specs=main_memory,
        scratch_shapes=[
            pltpu.VMEM((2, chans - TAIL * GROUP, rows // 2, width), f32),
            pltpu.VMEM((2, TAIL * GROUP, rows, width), f32),
            dma,
        ],
        compiler_params=pltpu.CompilerParams(vmem_limit_bytes=8 * 1024 * 1024),
    )(*parts)


def solution(mesh):
    placed = (
        P(None, "chan", "rad", None),
        P(None, "chan", "rad", None),
        P(),
        P(),
        P(),
        P("chan", None),
        P(),
    )
    return jax.shard_map(
        functools.partial(device_step, mesh.shape["chan"], mesh.shape["rad"]),
        mesh=mesh,
        in_specs=placed,
        out_specs=P(None, "chan", "rad", None),
        check_vma=False,
    )
```

```python
import functools

import jax
import jax.numpy as jnp
from jax import lax
from jax.experimental import pallas as pl
from jax.experimental.pallas import tpu as pltpu
from jax.sharding import PartitionSpec as P


def extended(array, sides, width):
    for axis, dim in sides:
        peers, length = (lax.axis_size(axis), array.shape[dim])
        up = [(i, (i + 1) % peers) for i in range(peers - 1)]
        down = [(j, i) for i, j in up]
        last = lax.slice_in_dim(array, length - width, length, axis=dim)
        initial = lax.slice_in_dim(array, 0, width, axis=dim)
        before = lax.ppermute(last, axis, up)
        after = lax.ppermute(initial, axis, down)
        array = jnp.concatenate([before, array, after], axis=dim)
    return array


def on_device(psi, k_prev, gaunt, dipole, kinetic, chan_l, field_amp):
    highest = lax.Precision.HIGHEST
    section = psi + 0.5 * k_prev
    local_chan = section.shape[1]
    rows = section.shape[2]
    width = section.shape[3]
    rad_at = lax.axis_index("rad")
    first_r = (
        1.0 + 8.0 * (rad_at * rows + jnp.arange(rows, dtype=jnp.int32)).astype(jnp.float32) / width
    )
    second_r = 1.0 + 8.0 * jnp.arange(width, dtype=jnp.float32) / width
    along_r2 = jnp.einsum("acij,kj->acik", section, kinetic, precision=highest)
    padded = extended(section.astype(jnp.bfloat16), (("rad", 2),), rows).astype(section.dtype)
    band = lax.dynamic_slice_in_dim(kinetic, rad_at * rows, rows, 0)
    widened = jnp.pad(band, ((0, 0), (rows, rows)))
    local_band = lax.dynamic_slice_in_dim(widened, rad_at * rows, 3 * rows, 1)
    along_r1 = jnp.einsum("ij,acjk->acik", local_band, padded, precision=highest)
    lvals = chan_l.astype(jnp.float32)
    first_l = lvals[:, 0] * (lvals[:, 0] + 1.0)
    second_l = lvals[:, 1] * (lvals[:, 1] + 1.0)
    potential = (
        first_l[:, None, None] / (2.0 * first_r * first_r)[None, :, None]
        + second_l[:, None, None] / (2.0 * second_r * second_r)[None, None, :]
        - 2.0 / first_r[None, :, None]
        - 2.0 / second_r[None, None, :]
    )
    sent = section.astype(jnp.bfloat16).reshape(2, local_chan, rows * width)
    chan_at = lax.axis_index("chan")
    block = lax.all_to_all(sent, "chan", split_axis=2, concat_axis=1, tiled=True)
    count = block.shape[2]
    place = chan_at * count + jnp.arange(count, dtype=jnp.int32)
    row_r = 1.0 + 8.0 * (rad_at * rows + place // width).astype(jnp.float32) / width
    col_r = 1.0 + 8.0 * (place % width).astype(jnp.float32) / width
    far = jnp.maximum(row_r, col_r)
    near = jnp.minimum(row_r, col_r)
    inverse = 1.0 / far
    ratio = near * inverse
    power = inverse
    total = jnp.zeros(block.shape, jnp.float32)
    for order in range(gaunt.shape[0]):
        mixed = jnp.einsum("cd,adq->acq", gaunt[order], block, preferred_element_type=jnp.float32)
        total = total + power[None, None, :] * mixed
        power = power * ratio
    mixed = jnp.einsum("cd,adq->acq", dipole, block, preferred_element_type=jnp.float32)
    total = total + (field_amp[0] * (row_r + col_r))[None, None, :] * mixed
    coupled = lax.all_to_all(
        total.astype(jnp.bfloat16), "chan", split_axis=1, concat_axis=2, tiled=True
    )
    coupled = coupled.reshape(coupled.shape[0], local_chan, rows, width)
    ham = along_r1 + along_r2 + potential[None] * section + coupled.astype(jnp.float32)
    return jnp.stack([ham[1], -ham[0]])


MESH = pl.DeviceIdType.MESH
GROUP = 16
PAIRS = 2
TAIL = 2
LOADS = ((0, 1), (1, 3), (3, 6), (6, 9), (9, 12))


def split_bf16(value):
    high = value.astype(jnp.bfloat16)
    return high, (value - high.astype(jnp.float32)).astype(jnp.bfloat16)


def lay_out(target, group, row, value):
    _, chans, height, width = target.shape
    start = group * GROUP * height + row % height
    place = (pl.ds(start, GROUP, stride=height), slice(None))
    target.at[0].reshape(chans * height, width)[place] = value[:, width:]
    target.at[1].reshape(chans * height, width)[place] = -value[:, :width]


def finish_kernel(rads, acc, early, far_tail, wr1, out, lower, late, sem):
    rows, chans, lanes = acc.shape
    size = rows * GROUP
    done = chans - TAIL * GROUP
    rad_at = lax.axis_index("rad")
    minor = rad_at % 2
    behind = rad_at - 2 + 4 * minor
    has_behind = jnp.logical_and(behind >= 0, behind < rads)
    half = rows // 2
    pltpu.make_async_copy(early.at[:, 0:done], out.at[:, 0:done, 0:half, :], sem).start()
    for first in range(0, done, 2 * GROUP):
        for group in range(first // GROUP, first // GROUP + 2):
            for row in range(half, rows):
                value = acc[row, group * GROUP : (group + 1) * GROUP, :]
                lay_out(lower, group, row, value)
        cut = slice(first, first + 2 * GROUP)
        pltpu.make_async_copy(lower.at[:, cut], out.at[:, cut, half:rows, :], sem).start()

    for group in range(TAIL):
        cut = slice(group * GROUP, (group + 1) * GROUP)
        there = slice(done + group * GROUP, done + (group + 1) * GROUP)

        @pl.when(has_behind)
        def _():
            value = far_tail[:, cut, :].reshape(size, lanes)
            both = jnp.dot(wr1[2 * minor], value, preferred_element_type=jnp.float32)
            total = (both[:size] + both[size:]).reshape(rows, GROUP, lanes)
            for row in range(rows):
                lay_out(late, group, row, acc[row, there, :] + total[row])

        @pl.when(jnp.logical_not(has_behind))
        def _():
            for row in range(rows):
                lay_out(late, group, row, acc[row, there, :])

        pltpu.make_async_copy(late.at[:, cut], out.at[:, there], sem).start()
    pltpu.make_async_copy(out, out, sem).wait()


def fused_kernel(
    peers,
    rads,
    psi,
    k_prev,
    gaunt,
    dipole,
    kin_main,
    chan_main,
    field,
    acc,
    early,
    far_tail,
    wr1,
    kin,
    chan_l,
    pk,
    sec,
    xg,
    xp,
    coupled,
    halo,
    weights,
    kk,
    lmul,
    langle,
    load_sem,
    small_sem,
    hr,
    xs,
    xr,
    cr,
    fl,
    fr,
    yr,
    zs,
    zr,
    vs,
    vr,
    via,
):
    rows, chans, lanes = sec.shape
    width = lanes // 2
    orders = weights.shape[1]
    chips = peers // 2
    groups = chans // GROUP
    lead = rows // 4
    chan_at = lax.axis_index("chan")
    rad_at = lax.axis_index("rad")
    core = chan_at % 2
    chip = chan_at // 2
    partner = chan_at + 1 - 2 * core
    minor = rad_at % 2
    other = rad_at + 1 - 2 * minor
    ahead = rad_at + 2 - 4 * minor
    behind = rad_at - 2 + 4 * minor
    has_ahead = jnp.logical_and(ahead >= 0, ahead < rads)
    has_behind = jnp.logical_and(behind >= 0, behind < rads)
    near_slot = 1 - minor
    far_slot = minor
    whole = rows - 2 * PAIRS
    back = 2
    peer = lax.rem(chip + 1, chips) * 2 + core

    def block(owner):
        return pl.ds(pl.multiple_of(owner * chans, GROUP), chans)

    def cut_of(group):
        return pl.ds(pl.multiple_of(group * GROUP, GROUP), GROUP)

    def block_cut(owner, group):
        return pl.ds(pl.multiple_of(owner * chans + group * GROUP, GROUP), GROUP)

    def chip_peer(step):
        return lax.rem(chip + step, chips) * 2 + core

    def chip_source(step):
        return lax.rem(chip - step + chips, chips) * 2 + core

    def load(which, part):
        first, last = LOADS[part]
        cut = slice(first * GROUP, last * GROUP)
        return pltpu.make_async_copy(
            (psi, k_prev)[which].at[:, cut, :, :], pk.at[which, :, cut, :, :], load_sem.at[part]
        )

    def arrive(part):
        first, last = LOADS[part]
        view = pk.at[:, :, first * GROUP : last * GROUP, :, :]
        pltpu.make_async_copy(view, view, load_sem.at[part]).wait()

    def load_weight(kind, order):
        source = gaunt.at[order] if order < orders - 1 else dipole
        owner = (peer, chan_at)[kind]
        return pltpu.make_async_copy(
            source.at[block(owner), :], weights.at[kind, order], small_sem.at[2]
        )

    def remote(source, target, send, recv, device):
        return pltpu.make_async_remote_copy(
            src_ref=source,
            dst_ref=target,
            send_sem=send,
            recv_sem=recv,
            device_id=device,
            device_id_type=MESH,
        )

    def lead_copy(some):
        view = xg.at[0:lead, some, :]
        return remote(view, view, xs, hr, {"chan": peer})

    def chip_copy(row, owner):
        view = xg.at[row, block(owner), :]
        return remote(view, view, xs, xr.at[row - lead], {"chan": peer})

    def part_copy(part, owner):
        view = xp.at[part, :, block(owner), :]
        return remote(view, view, xs, xr.at[whole - lead], {"chan": peer})

    def back_copy(part):
        source, target = (coupled.at[back], coupled.at[part])
        return remote(source, target, xs, xr.at[whole - lead + 1], {"chan": peer})

    def core_copy(some_rows, owner):
        view = xg.at[some_rows, block(owner), :]
        return remote(view, view, xs, cr, {"chan": partner})

    def core_part(owner):
        view = xp.at[chip, :, block(owner), :]
        return remote(view, view, xs, cr, {"chan": partner})

    def relay_lead(owner):
        view = xg.at[0:lead, block(owner), :]
        return remote(view, view, xs, fl, {"chan": partner})

    def relay_copy(row, owner):
        view = xg.at[row, block(owner), :]
        return remote(view, view, xs, fr.at[row - lead], {"chan": partner})

    def relay_part(owner):
        view = xp.at[chip, :, block(owner), :]
        return remote(view, view, xs, fr.at[whole - lead], {"chan": partner})

    def half_of(half):
        return slice(half * (rows // 2), (half + 1) * (rows // 2))

    def side_copy(group, half):
        source = xg.at[half_of(half), block_cut(chan_at, group), :]
        target = halo.at[minor, half_of(half), cut_of(group), :]
        return remote(source, target, xs, yr.at[half, group], {"rad": other})

    def far_copy(some_rows, some, place):
        source = halo.at[near_slot, some_rows, some, :]
        target = halo.at[minor, some_rows, some, :]
        return remote(source, target, zs, zr.at[place], {"rad": ahead})

    def tail_cut(group):
        return pl.ds(pl.multiple_of((group - groups + TAIL) * GROUP, GROUP), GROUP)

    def tail_copy(some_rows, group):
        source = halo.at[near_slot, some_rows, cut_of(group), :]
        target = far_tail.at[some_rows, tail_cut(group), :]
        return remote(source, target, zs, zr.at[group], {"rad": ahead})

    def via_copy(some_rows):
        source = xg.at[some_rows, block_cut(chan_at, groups - 1), :]
        return remote(source, via.at[some_rows], vs, vr.at[0], {"rad": behind})

    def via_forward(some_rows):
        target = far_tail.at[some_rows, tail_cut(groups - 1), :]
        return remote(via.at[some_rows], target, zs, vr.at[1], {"rad": other})

    def by_core(condition, work):
        for at, some_rows in enumerate((every, half_of(1))):

            @pl.when(jnp.logical_and(core == at, condition))
            def _():
                work(some_rows)

    every = slice(0, rows)
    small = [
        pltpu.make_async_copy(kin_main, kin, small_sem.at[0]),
        pltpu.make_async_copy(chan_main, chan_l, small_sem.at[1]),
    ]
    barrier = pltpu.get_barrier_semaphore()
    for step in range(1, chips):
        pl.semaphore_signal(
            barrier, inc=1, device_id={"chan": chip_peer(step)}, device_id_type=MESH
        )
    pl.semaphore_signal(barrier, inc=1, device_id={"chan": partner}, device_id_type=MESH)
    pl.semaphore_signal(barrier, inc=1, device_id={"rad": other}, device_id_type=MESH)

    @pl.when(has_ahead)
    def _():
        pl.semaphore_signal(barrier, inc=1, device_id={"rad": ahead}, device_id_type=MESH)

    @pl.when(has_behind)
    def _():
        pl.semaphore_signal(barrier, inc=1, device_id={"rad": behind}, device_id_type=MESH)

    for part in range(len(LOADS)):
        for which in range(2):
            load(which, part).start()

    def form(group):
        for part in range(2):
            first = pk.at[0, part].reshape(chans * rows, width)
            second = pk.at[1, part].reshape(chans * rows, width)
            cut = slice(part * width, (part + 1) * width)
            for row in range(rows):
                place = (pl.ds(group * GROUP * rows + row, GROUP, stride=rows), slice(None))
                value = first[place] + 0.5 * second[place]
                sec[row, cut_of(group), cut] = value
                rounded = value.astype(jnp.bfloat16)
                xg[row, block_cut(chan_at, group), cut] = rounded
                if row >= whole:
                    pair, turn = divmod(row - whole, 2)
                    lane = slice(turn * width, (turn + 1) * width)
                    xp[part, pair, block_cut(chan_at, group), lane] = rounded

    def send_group(group):
        for half in range(2):
            side_copy(group, half).start()
        alone = jnp.logical_or(group == 0, group == groups - 1)

        @pl.when(alone)
        def _():
            lead_copy(block_cut(chan_at, group)).start()

        @pl.when(jnp.logical_and(jnp.logical_not(alone), group % 2 == 0))
        def _():
            start = pl.multiple_of(chan_at * chans + (group - 1) * GROUP, GROUP)
            lead_copy(pl.ds(start, 2 * GROUP)).start()

    arrive(0)
    form(jnp.int32(0))
    pl.semaphore_wait(
        barrier, chips + 1 + has_ahead.astype(jnp.int32) + has_behind.astype(jnp.int32)
    )
    send_group(jnp.int32(0))
    arrive(1)
    form(jnp.int32(1))

    def form_next(group, carry):
        form(group)
        send_group(group - 1)
        return carry

    lax.fori_loop(2, LOADS[1][1], form_next, 0)
    for part in range(2, len(LOADS)):
        arrive(part)
        lax.fori_loop(LOADS[part][0], LOADS[part][1], form_next, 0)
    for copy in small:
        copy.start()
    for order in range(orders):
        for kind in range(2):
            load_weight(kind, order).start()

    send_group(jnp.int32(groups - 1))

    by_core(has_behind, lambda some_rows: via_copy(some_rows).start())

    part_copy(1 - chip, chan_at).start()
    for row in range(lead, whole):
        chip_copy(row, chan_at).start()
    for index in range(0, whole, lead):
        core_copy(slice(index, min(index + lead, whole)), chan_at).start()
    core_part(chan_at).start()

    def pass_on(group, half):
        side_copy(group, half).wait_recv()

        @pl.when(jnp.logical_and(has_ahead, group < groups - TAIL))
        def _():
            far_copy(half_of(half), cut_of(group), group).start()

        late = jnp.logical_and(group >= groups - TAIL, group < groups - 1 + core * (1 - half))

        @pl.when(jnp.logical_and(has_ahead, late))
        def _():
            tail_copy(half_of(half), group).start()

    def forward(group, half):
        @pl.when(group + core < groups)
        def _():
            pass_on(group + core, half)

    @pl.when(core == 1)
    def _():
        pass_on(0, 0)

    for copy in small:
        copy.wait()
    kin_high, kin_low = split_bf16(kin[...])
    both = jnp.concatenate([kin_high, kin_low], axis=1)
    kk[0:width, :] = both
    kk[width : 2 * width, :] = both

    band = kin[pl.ds(pl.multiple_of(rad_at * rows, rows), rows), :]
    size = rows * GROUP
    tall = jnp.broadcast_to(band[:, None, :], (rows, GROUP, width)).reshape(size, width)
    tall_high, tall_low = split_bf16(tall)
    at_row = lax.broadcasted_iota(jnp.int32, (size, size), 0)
    at_col = lax.broadcasted_iota(jnp.int32, (size, size), 1)
    same = (at_row % GROUP) == (at_col % GROUP)
    from_j = lax.broadcasted_iota(jnp.int32, (width, size), 0)
    to_col = lax.broadcasted_iota(jnp.int32, (width, size), 1)
    for side in range(3):
        pick = from_j == (rad_at + side - 1) * rows + to_col // GROUP
        pick = jnp.where(pick, 1.0, 0.0).astype(jnp.bfloat16)
        for level, source in enumerate((tall_high, tall_low)):
            wide = jnp.dot(source, pick, preferred_element_type=jnp.float32)
            wr1[side, level * size : (level + 1) * size, :] = jnp.where(same, wide, 0.0).astype(
                jnp.bfloat16
            )

    @pl.when(core == 0)
    def _():
        pass_on(0, 0)

    @pl.when(core == 1)
    def _():
        pass_on(0, 1)

    second_r = 1.0 + 8.0 * (
        lax.broadcasted_iota(jnp.int32, (1, lanes), 1) % width
    ).astype(jnp.float32) / width
    inner_r = second_r[:, :width]
    lvals = chan_l[...].astype(jnp.float32).astype(jnp.bfloat16)
    first = lax.broadcasted_iota(jnp.int32, (2, lanes), 0)
    spread = first == lax.broadcasted_iota(jnp.int32, (2, lanes), 1) // width
    spread = jnp.where(spread, 1.0, 0.0).astype(jnp.bfloat16)
    lwide = lax.dot_general(
        lvals, spread, (((0,), (0,)), ((), ())), preferred_element_type=jnp.float32
    )
    lwide = lwide * (lwide + 1.0)
    lmul[...] = lwide[:, :width]
    langle[...] = lwide[:, width:] / (2.0 * inner_r * inner_r) - 2.0 / inner_r

    def radius(row):
        place = jnp.full((1, lanes), rad_at * rows + row, jnp.int32)
        return 1.0 + 8.0 * place.astype(jnp.float32) / width

    def local_row(row):
        first_r = radius(row)[:, :width]
        scale = 1.0 / (2.0 * first_r * first_r)
        shift = 2.0 / first_r
        potential = lmul[...] * scale + langle[...] - shift
        for part in range(2):
            cut = slice(part * width, (part + 1) * width)
            value = sec[row, :, cut]
            high = xg[row, block(chan_at), cut]
            low = (value - high.astype(jnp.float32)).astype(jnp.bfloat16)
            both = jnp.dot(
                jnp.concatenate([high, low], axis=1), kk[...], preferred_element_type=jnp.float32
            )
            total = both[:, :width] + both[:, width:] + potential * value
            acc[row, :, cut] = acc[row, :, cut] + total

    def mix(side, value):
        both = jnp.dot(wr1[side], value, preferred_element_type=jnp.float32)
        return both[:size] + both[size:]

    def own_group(index):
        first = pl.multiple_of(index * GROUP, GROUP)
        start = pl.multiple_of(chan_at * chans + first, GROUP)
        high = xg[:, pl.ds(start, GROUP), :].reshape(size, lanes)
        value = sec[:, pl.ds(first, GROUP), :].reshape(size, lanes)
        low = (value - high.astype(jnp.float32)).astype(jnp.bfloat16)
        total = mix(1, high) + jnp.dot(
            wr1[1, 0:size, :], low, preferred_element_type=jnp.float32
        )
        acc[:, pl.ds(first, GROUP), :] = total.reshape(rows, GROUP, lanes)

    def side_group(index):
        first = pl.multiple_of(index * GROUP, GROUP)
        cut = pl.ds(first, GROUP)
        total = mix(0, halo[0, :, cut, :].reshape(size, lanes)) + mix(
            2, halo[1, :, cut, :].reshape(size, lanes)
        )
        acc[:, cut, :] = acc[:, cut, :] + total.reshape(rows, GROUP, lanes)

    def factors_of(first_r):
        inverse = 1.0 / jnp.maximum(first_r, second_r)
        ratio = jnp.minimum(first_r, second_r) * inverse
        factors = [inverse]
        for _ in range(orders - 2):
            factors.append(factors[-1] * ratio)
        factors.append(field[0] * (first_r + second_r))
        return factors

    def summed(factors, matrices, source, some):
        total = jnp.zeros((chans // 2, lanes), jnp.float32)
        for order in range(orders):
            total = total + factors[order] * jnp.dot(
                matrices[order, some, :], source[...], preferred_element_type=jnp.float32
            )
        return total.astype(jnp.bfloat16)

    cuts = (slice(0, chans // 2), slice(chans // 2, chans))

    def couple(row):
        factors = factors_of(radius(row))
        for some in cuts:
            total = summed(factors, weights.at[1], xg.at[row], some)
            acc[row, some, :] = acc[row, some, :] + total.astype(jnp.float32)

    def couple_parts(kind, pair):
        place = lax.broadcasted_iota(jnp.int32, (1, lanes), 1) // width
        place = place + (rad_at * rows + whole + 2 * pair)
        factors = factors_of(1.0 + 8.0 * place.astype(jnp.float32) / width)
        target = kind * chip + (1 - kind) * back
        for some in cuts:
            total = summed(factors, weights.at[kind], xp.at[chip, pair], some)
            coupled[target, pair, some, :] = total

    def take_parts(unit):
        @pl.when(unit == 0)
        def _():
            relay_part(peer + 1 - 2 * core).wait_recv()

        @pl.when(unit == 2 * PAIRS - 1)
        def _():
            back_copy(chip).start()

        couple_parts(unit // PAIRS, unit % PAIRS)

    def relay(base):
        row = base + core

        @pl.when(jnp.logical_and(row >= lead, row < whole))
        def _():
            chip_copy(row, peer).wait_recv()
            relay_copy(row, peer).start()

    def take_row(row):
        @pl.when(row >= lead)
        def _():
            relay_copy(row, peer + 1 - 2 * core).wait_recv()

        couple(row)

    def take_side(group):
        @pl.when(has_behind)
        def _():
            far_copy(every, cut_of(group), group).wait_recv()
            side_group(group)

        @pl.when(jnp.logical_not(has_behind))
        def _():
            mix_slot(near_slot, cut_of(group))

    def mix_slot(slot, cut):
        value = halo[slot, :, cut, :].reshape(size, lanes)
        total = mix(2 * slot, value).reshape(rows, GROUP, lanes)
        acc[:, cut, :] = acc[:, cut, :] + total

    def each_of(first, last, work):
        def step(index, carry):
            work(index)
            return carry

        lax.fori_loop(first, last, step, 0)

    def merge(first, last):
        def one(group):
            for row in range(rows // 2):
                lay_out(early, group, row, acc[row, cut_of(group), :])

        each_of(first, last, one)

    def take_lead(turn):
        @pl.when(core == turn)
        def _():
            lead_copy(block(peer)).wait_recv()
            relay_lead(peer).start()

    @pl.when(core == 1)
    def _():
        pass_on(1, 0)

    each_of(0, 3, own_group)
    forward(0, 1)
    each_of(3, 4, own_group)
    for half in range(2):
        forward(1, half)
        each_of(4 + 4 * half, 8 + 4 * half, own_group)
    for half in range(2):
        forward(2, half)
        take_lead(1 - half)
        each_of(6 * half, 6 + 6 * half, local_row)
    pltpu.make_async_copy(weights, weights, small_sem.at[2]).wait()
    core_copy(slice(0, whole + PAIRS), partner).wait_recv()
    each_of(12, rows - 1, local_row)

    def pass_via(some_rows):
        via_copy(some_rows).wait_recv()
        via_forward(some_rows).start()

    by_core(has_ahead, pass_via)

    def main(index, carry):
        start = index * lead - 1

        def each(first, second):
            return (1 - core) * first + core * second

        def when(condition, work, *args):
            @pl.when(condition)
            def _():
                work(*args)

        even, odd = (core == 0, core == 1)
        started, ended = (index == 1, index == 3)
        forward(3 * index, 0)

        @pl.when(started)
        def _():
            local_row(rows - 1)
            relay_lead(peer + 1 - 2 * core).wait_recv()

        when(jnp.logical_or(odd, started), take_row, each(0, start - 2))
        when(jnp.logical_and(even, index > 1), take_parts, 3 * index - 6)
        relay(start - 1)
        forward(3 * index, 1)
        take_side(3 * index - 2)
        when(jnp.logical_or(even, started), take_row, each(start - 1, 0))
        when(jnp.logical_and(odd, index > 1), take_parts, 2 * index - 3)
        forward(3 * index + 1, 0)
        relay(start)

        @pl.when(started)
        def _():
            part_copy(chip, peer).wait_recv()
            relay_part(peer).start()

        take_row(start - core)
        when(started, take_side, 0)
        when(jnp.logical_and(even, index == 2), take_parts, 1)
        when(ended, merge, 0, groups - 4)
        forward(3 * index + 1, 1)
        when(jnp.logical_or(odd, started), take_row, each(1, start))
        when(jnp.logical_and(even, index == 2), take_parts, 2)
        take_side(3 * index - 1)
        relay(start + 1)
        when(index < 3, forward, 3 * index + 2, 0)
        when(jnp.logical_and(even, index < 3), take_row, start + 1)
        when(jnp.logical_and(odd, index < 3), take_parts, 2 * index - 2)
        when(index < 3, forward, 3 * index + 2, 1)
        relay(start + 2)
        take_side(3 * index)
        when(index < 3, take_row, start + 2 - core)
        return carry

    lax.fori_loop(1, 4, main, 0)

    def take_back():
        back_copy(1 - chip).wait_recv()
        for place in range(rows - whole):
            pair, turn = divmod(place, 2)
            for part in range(2):
                lane = slice(part * width, (part + 1) * width)
                value = coupled[part, pair, :, turn * width : (turn + 1) * width]
                acc[whole + place, :, lane] = acc[whole + place, :, lane] + value.astype(
                    jnp.float32
                )

    merge(groups - 4, groups - TAIL)
    for group in range(groups - TAIL, groups):
        if group == groups - 1:
            for half in range(2):
                forward(group, half)
        mix_slot(near_slot, cut_of(group))
    take_back()

    @pl.when(has_behind)
    def _():
        tail_copy(every, groups - 2).wait_recv()

    @pl.when(jnp.logical_and(core == 1, has_behind))
    def _():
        tail_copy(half_of(0), groups - 1).wait_recv()

    by_core(has_behind, lambda some_rows: via_forward(some_rows).wait_recv())

    def sent(owners, some_rows, sem):
        view = xg.at[some_rows, 0 : owners * chans, :]
        remote(view, view, sem, fl, {"chan": partner}).wait_send()

    sent(peers, slice(0, rows - 1), xs)

    @pl.when(has_ahead)
    def _():
        sent(1, every, zs)

    by_core(has_behind, lambda some_rows: via_copy(some_rows).wait_send())


def device_step(peers, rads, psi, k_prev, gaunt, dipole, kinetic, chan_l, field_amp):
    _, chans, rows, width = psi.shape
    fits = (
        chans == 3 * 4 * GROUP
        and rows == GROUP
        and peers == 4
        and rads % 2 == 0
        and width == rads * rows
        and width == 128
    )
    if not fits:
        return on_device(psi, k_prev, gaunt, dipole, kinetic, chan_l, field_amp)
    orders = gaunt.shape[0] + 1
    chips = peers // 2
    groups = chans // GROUP
    lanes = 2 * width
    size = rows * GROUP
    f32, bf16, dma = (jnp.float32, jnp.bfloat16, pltpu.SemaphoreType.DMA)
    main_memory = pl.BlockSpec(memory_space=pltpu.HBM)
    vmem = pl.BlockSpec(memory_space=pltpu.VMEM)
    summed = jax.ShapeDtypeStruct((rows, chans, lanes), f32)
    early = jax.ShapeDtypeStruct((2, chans, rows // 2, width), f32)
    far_tail = jax.ShapeDtypeStruct((rows, TAIL * GROUP, lanes), bf16)
    mixing = jax.ShapeDtypeStruct((3, 2 * size, size), bf16)
    psi, k_prev, gaunt, dipole, kinetic, chan_l = (
        pltpu.with_memory_space_constraint(value, pltpu.HBM)
        for value in (psi, k_prev, gaunt, dipole, kinetic, chan_l.T)
    )
    parts = pl.pallas_call(
        functools.partial(fused_kernel, peers, rads),
        out_shape=(summed, early, far_tail, mixing),
        in_specs=[main_memory] * 6 + [pl.BlockSpec(memory_space=pltpu.SMEM)],
        out_specs=(vmem,) * 4,
        scratch_shapes=[
            pltpu.VMEM(kinetic.shape, f32),
            pltpu.VMEM((2, chans), jnp.int32),
            pltpu.VMEM((2, 2, chans, rows, width), f32),
            pltpu.VMEM((rows, chans, lanes), f32),
            pltpu.VMEM((rows, peers * chans, lanes), bf16),
            pltpu.VMEM((2, PAIRS, peers * chans, lanes), bf16),
            pltpu.VMEM((3, PAIRS, chans, lanes), bf16),
            pltpu.VMEM((2, rows, chans, lanes), bf16),
            pltpu.VMEM((2, orders, chans, peers * chans), bf16),
            pltpu.VMEM((lanes, lanes), bf16),
            pltpu.VMEM((chans, width), f32),
            pltpu.VMEM((chans, width), f32),
            dma((len(LOADS),)),
            dma((3,)),
            dma,
            dma,
            dma((rows - rows // 4 - 2 * PAIRS + 2,)),
            dma,
            dma,
            dma((rows - rows // 4 - 2 * PAIRS + 1,)),
            dma((2, groups)),
            dma,
            dma((groups,)),
            dma,
            dma((2,)),
            pltpu.VMEM((rows, GROUP, lanes), bf16),
        ],
        compiler_params=pltpu.CompilerParams(
            collective_id=0, has_side_effects=True, vmem_limit_bytes=36 * 1024 * 1024
        ),
    )(psi, k_prev, gaunt, dipole, kinetic, chan_l, field_amp)
    return pl.pallas_call(
        functools.partial(finish_kernel, rads),
        out_shape=jax.ShapeDtypeStruct(psi.shape, f32),
        in_specs=[vmem] * 4,
        out_specs=main_memory,
        scratch_shapes=[
            pltpu.VMEM((2, chans - TAIL * GROUP, rows // 2, width), f32),
            pltpu.VMEM((2, TAIL * GROUP, rows, width), f32),
            dma,
        ],
        compiler_params=pltpu.CompilerParams(vmem_limit_bytes=8 * 1024 * 1024),
    )(*parts)


def solution(mesh):
    placed = (
        P(None, "chan", "rad", None),
        P(None, "chan", "rad", None),
        P(),
        P(),
        P(),
        P("chan", None),
        P(),
    )
    return jax.shard_map(
        functools.partial(device_step, mesh.shape["chan"], mesh.shape["rad"]),
        mesh=mesh,
        in_specs=placed,
        out_specs=P(None, "chan", "rad", None),
        check_vma=False,
    )
```
